32 devices in a mesh: kv: 4 (over y, x), seq: 8 (over z, core).
Axes of the slice: x: 2, y: 2, z: 4, core: 2. Of those that a mesh axis runs over, the one named last changes fastest.
Arguments:
- queries: bfloat16 [1024, 12288], P('seq', 'kv'), may hold values from -400 to 400
- cache_keys: bfloat16 [8192, 768], P('seq', 'kv'), may hold values from -6 to 6
- cache_values: bfloat16 [8192, 512], P('seq', 'kv'), may hold values from -6 to 6
- incoming_keys: bfloat16 [1024, 768], P('seq', 'kv'), may hold values from -6 to 6
- new_values: bfloat16 [1024, 512], P('seq', 'kv'), may hold values from -6 to 6
- comp_key_weight: bfloat16 [6144, 192], P('kv'), may hold values from -0.078125 to 0.078125
- comp_value_weight: bfloat16 [4096, 128], P('kv'), may hold values from -0.09375 to 0.09375
- select_blocks: int32 [32, 4, 16], P('seq', 'kv'), may hold values from 0 to 127, as said below
- gate_weight: bfloat16 [64, 192, 3], P('kv'), may hold values from -0.4375 to 0.4375
Outputs:
- attended: bfloat16 [1024, 8192], P('seq', 'kv')
The draws below stay inside these ranges and needn't reach their ends.
Inputs may be any that keep to these rules, and one draw needn't show every extreme that they name: `select_blocks`: each row names 16 different blocks. For each KV group, the rows of one device of seq (4 tiles) name blocks of any one cache shard (the 16 blocks of one index of seq) at most 16 times in all, and in every draw the rows of every device name one shard's blocks exactly 16 times.
All inputs are finite; a program needn't handle non-finite values.
Results may differ from the reference program's by a relative error of at most 0.012.
Values may be sent and summed in bfloat16 or wider, within the bound.
A program may use at most 128 MiB of HBM per device.

```python
import jax
import jax.numpy as jnp
from jax import lax

HEADS = 64
KV_GROUPS = 4
HEAD_QK = 192
HEAD_V = 128
CMP_STRIDE = 16
SEL_BLOCK = 64
TOPN = 16
WINDOW = 512
TILE = 32
Q_DEV = 128
QUERIES = 1024
CACHE = 8192
TILES_DEV = 4
BLK_DEV = 16
CAP = 16
N_SEQ = 8


def draw_queries(key, part):
    drawn = jax.random.normal(jax.random.fold_in(key, 11), (QUERIES, HEADS * HEAD_QK), jnp.float32) * 2.5
    return jnp.clip(drawn, -400.0, 400.0).astype(jnp.bfloat16)


def one_device(subkey, busy):
    picks = TILES_DEV * TOPN
    slots = N_SEQ * CAP
    key_score, key_offset, key_order = jax.random.split(subkey, 3)
    places = jnp.arange(slots, dtype=jnp.int32)
    pool = places // CAP
    score = jax.random.randint(key_score, (slots,), 0, 1 << 16, dtype=jnp.int32) * slots + places
    score = jnp.where(pool == busy, places - slots, score)
    owner = pool[jnp.argsort(score, stable=True)][:picks]
    owner = owner[jax.random.permutation(key_order, picks)].reshape(TILES_DEV, TOPN)
    onehot = (owner[:, :, None] == jnp.arange(N_SEQ, dtype=jnp.int32)[None, None, :]).astype(jnp.int32)
    ranking = jnp.sum((jnp.cumsum(onehot, axis=1) - 1) * onehot, axis=2)
    offset = jax.random.randint(key_offset, (TILES_DEV, N_SEQ), 0, BLK_DEV, dtype=jnp.int32)
    local = (jnp.take_along_axis(offset, owner, axis=1) + ranking) % BLK_DEV
    return owner * BLK_DEV + local


def draw_select_blocks(key, part):
    columns = []
    for group in range(KV_GROUPS):
        group_key = jax.random.fold_in(key, 101 + group)
        busy = jax.random.randint(jax.random.fold_in(group_key, 7), (), 0, N_SEQ, dtype=jnp.int32)
        subkeys = jax.random.split(jax.random.fold_in(group_key, 9), N_SEQ)
        chosen = jax.vmap(lambda subkey: one_device(subkey, busy))(subkeys)
        columns.append(chosen.reshape(N_SEQ * TILES_DEV, TOPN))
    return jnp.stack(columns, axis=1).astype(jnp.int32)


def shard_levels(key, extent, cuts, least, top_value):
    def one(dim, shards_of):
        heights = jax.random.uniform(jax.random.fold_in(jax.random.fold_in(key, 6), dim), (shards_of,), jnp.float32, least / len(cuts), top_value / len(cuts))
        return jnp.repeat(jnp.exp(heights), extent[dim] // shards_of).reshape((-1,) + (1,) * (len(extent) - dim - 1))

    level = one(*cuts[0])
    for cut in cuts[1:]:
        level = level * one(*cut)
    return level


def normal_values(rng, dims, scale, limit, cuts=(), kind=jnp.bfloat16):
    gain = shard_levels(rng, dims, cuts, -0.22, 0.18) if cuts else 1.0
    result = jax.random.normal(rng, dims, jnp.float32) * scale * gain
    return jnp.minimum(jnp.maximum(result, -limit), limit).astype(kind)


def setup_inputs(seed: int = 0) -> dict:
    key_list = jax.random.split(jax.random.key(seed), 10)
    queries = draw_queries(jax.random.fold_in(key_list[9], 71), 0)
    cache_keys = normal_values(key_list[1], (CACHE, KV_GROUPS * HEAD_QK), 1.0, 6.0, ((0, 8), (1, 4)))
    cache_values = normal_values(key_list[2], (CACHE, KV_GROUPS * HEAD_V), 1.0, 6.0, ((0, 8), (1, 4)))
    incoming_keys = normal_values(key_list[3], (QUERIES, KV_GROUPS * HEAD_QK), 1.0, 6.0, ((0, 8), (1, 4)))
    new_values = normal_values(key_list[4], (QUERIES, KV_GROUPS * HEAD_V), 1.0, 6.0, ((0, 8), (1, 4)))
    comp_key_weight = normal_values(key_list[5], (2 * CMP_STRIDE * HEAD_QK, HEAD_QK), (2 * CMP_STRIDE * HEAD_QK) ** -0.5, 0.078125, ((0, 4),))
    comp_value_weight = normal_values(key_list[6], (2 * CMP_STRIDE * HEAD_V, HEAD_V), (2 * CMP_STRIDE * HEAD_V) ** -0.5, 0.09375, ((0, 4),))
    select_blocks = draw_select_blocks(jax.random.fold_in(key_list[9], 71), 0)
    gate_weight = normal_values(key_list[8], (HEADS, HEAD_QK, 3), HEAD_QK ** -0.5, 0.4375, ((0, 4),))
    return {"queries": queries, "cache_keys": cache_keys, "cache_values": cache_values, "incoming_keys": incoming_keys, "new_values": new_values, "comp_key_weight": comp_key_weight, "comp_value_weight": comp_value_weight, "select_blocks": select_blocks, "gate_weight": gate_weight}


MASKED = -1e30


def attend(rows, keys, values, allowed):
    scale = keys.shape[-1] ** -0.5
    scores = jnp.dot(rows, keys.T, preferred_element_type=jnp.float32) * scale
    scores = jnp.where(allowed, scores, MASKED)
    top = jnp.max(scores, axis=-1, keepdims=True)
    weights = jnp.exp(scores - top)
    total = jnp.sum(weights, axis=-1, keepdims=True)
    mixed = jnp.dot(weights.astype(jnp.bfloat16), values, preferred_element_type=jnp.float32)
    return mixed / total


def reference(queries, cache_keys, cache_values, incoming_keys, new_values, comp_key_weight, comp_value_weight, select_blocks, gate_weight):
    per_group = HEADS // KV_GROUPS
    count = CACHE // CMP_STRIDE - 1
    half_keys = CMP_STRIDE * HEAD_QK
    half_values = CMP_STRIDE * HEAD_V
    split_queries = queries.reshape(QUERIES, KV_GROUPS, per_group, HEAD_QK)
    span = Q_DEV + WINDOW
    offsets = jnp.arange(span, dtype=jnp.int32)[None, :] - jnp.arange(Q_DEV, dtype=jnp.int32)[:, None]
    near_rows = jnp.repeat((offsets > 0) & (offsets <= WINDOW), per_group, axis=0)
    results = []
    for group in range(KV_GROUPS):
        keys = cache_keys[:, group * HEAD_QK:(group + 1) * HEAD_QK]
        values = cache_values[:, group * HEAD_V:(group + 1) * HEAD_V]
        fresh_keys = incoming_keys[:, group * HEAD_QK:(group + 1) * HEAD_QK]
        fresh_values = new_values[:, group * HEAD_V:(group + 1) * HEAD_V]
        comp_keys = (jnp.dot(keys[:CACHE - CMP_STRIDE].reshape(count, half_keys), comp_key_weight[:half_keys], preferred_element_type=jnp.float32)
                     + jnp.dot(keys[CMP_STRIDE:].reshape(count, half_keys), comp_key_weight[half_keys:], preferred_element_type=jnp.float32)).astype(jnp.bfloat16)
        comp_values = (jnp.dot(values[:CACHE - CMP_STRIDE].reshape(count, half_values), comp_value_weight[:half_values], preferred_element_type=jnp.float32)
                       + jnp.dot(values[CMP_STRIDE:].reshape(count, half_values), comp_value_weight[half_values:], preferred_element_type=jnp.float32)).astype(jnp.bfloat16)
        group_queries = split_queries[:, group]
        blocks = group_queries.reshape(N_SEQ, Q_DEV * per_group, HEAD_QK)
        compressed_out = lax.map(lambda block: attend(block, comp_keys, comp_values, True), blocks)
        key_blocks = keys.reshape(CACHE // SEL_BLOCK, SEL_BLOCK, HEAD_QK)
        value_block_list = values.reshape(CACHE // SEL_BLOCK, SEL_BLOCK, HEAD_V)
        tiles = group_queries.reshape(QUERIES // TILE, TILE * per_group, HEAD_QK)

        def pick(inputs):
            tile, chosen = inputs
            chosen_keys = key_blocks[chosen].reshape(TOPN * SEL_BLOCK, HEAD_QK)
            chosen_values = value_block_list[chosen].reshape(TOPN * SEL_BLOCK, HEAD_V)
            return attend(tile, chosen_keys, chosen_values, True)

        selected_out = lax.map(pick, (tiles, select_blocks[:, group]))
        joined_keys = jnp.concatenate([keys[CACHE - WINDOW:], fresh_keys])
        joined_values = jnp.concatenate([values[CACHE - WINDOW:], fresh_values])

        def slide(inputs):
            index, block = inputs
            start = (index * Q_DEV).astype(jnp.int32)
            window_keys = lax.dynamic_slice_in_dim(joined_keys, start, span, 0)
            window_values = lax.dynamic_slice_in_dim(joined_values, start, span, 0)
            return attend(block, window_keys, window_values, near_rows)

        window_out = lax.map(slide, (jnp.arange(N_SEQ, dtype=jnp.int32), blocks))
        results.append((compressed_out.reshape(QUERIES, per_group, HEAD_V),
                        selected_out.reshape(QUERIES, per_group, HEAD_V),
                        window_out.reshape(QUERIES, per_group, HEAD_V)))
    compressed_all = jnp.concatenate([item[0] for item in results], axis=1)
    selected_all = jnp.concatenate([item[1] for item in results], axis=1)
    window_all = jnp.concatenate([item[2] for item in results], axis=1)
    logits = jnp.einsum("thd,hdb->thb", queries.reshape(QUERIES, HEADS, HEAD_QK).astype(jnp.float32), gate_weight.astype(jnp.float32))
    gates = jax.nn.sigmoid(logits)
    mixed = gates[:, :, 0:1] * compressed_all + gates[:, :, 1:2] * selected_all + gates[:, :, 2:3] * window_all
    return mixed.astype(jnp.bfloat16).reshape(QUERIES, HEADS * HEAD_V)
```

```python
import functools

import jax
import jax.numpy as jnp
from jax import lax
from jax.experimental import pallas as pl
from jax.experimental.pallas import tpu as pltpu
from jax.sharding import PartitionSpec as P

CMP_STRIDE = 16
SEL_BLOCK = 64
WINDOW = 512


MASKED = -1e30


def passed_along(block, axis, distance):
    devices = range(lax.axis_size(axis))
    route = [((i - distance) % len(devices), i) for i in devices]
    return lax.ppermute(block, axis, route)


def from_behind(x, axis, by):
    peers = lax.axis_size(axis)
    pairs = [(i, i + by) for i in range(peers) if 0 <= i + by < peers]
    return lax.ppermute(x, axis, pairs)


def pack_rows(keys, values):
    return jnp.concatenate([keys.reshape(-1), values.reshape(-1)])


def unpack_rows(flat, count, key_width, value_width):
    keys = flat[: count * key_width].reshape(count, key_width)
    values = flat[count * key_width : count * (key_width + value_width)].reshape(count, value_width)
    return (keys, values)


def finish_rows(scores, values):
    top = jnp.max(scores, axis=-1, keepdims=True)
    weights = jnp.exp(scores - top)
    total = jnp.sum(weights, axis=-1, keepdims=True)
    mixed = jnp.matmul(weights.astype(jnp.bfloat16), values, preferred_element_type=jnp.float32)
    return mixed / total


def shards_by_request(
    queries,
    cache_keys,
    cache_values,
    incoming_keys,
    new_values,
    comp_key_weight,
    comp_value_weight,
    select_blocks,
    gate_weight,
):
    heads, key_width, _ = gate_weight.shape
    value_width = cache_values.shape[1]
    query_count = queries.shape[0]
    cache_count = cache_keys.shape[0]
    ranks = lax.axis_size("seq")
    place = lax.axis_index("seq")
    scale = key_width ** (-0.5)
    rows = queries.reshape(query_count * heads, key_width)
    row_total = rows.shape[0]
    stretch_pos = place * query_count + jnp.arange(query_count, dtype=jnp.int32)
    lookback_length = -(-WINDOW // query_count)
    weight_keys, weight_values = (
        lax.all_gather(comp_key_weight, "kv", axis=0, tiled=True),
        lax.all_gather(comp_value_weight, "kv", axis=0, tiled=True),
    )
    tail_pack = pack_rows(cache_keys[cache_count - WINDOW :], cache_values[cache_count - WINDOW :])
    moved_tail = passed_along(tail_pack, "seq", 1)
    before_keys, before_values = unpack_rows(moved_tail, WINDOW, key_width, value_width)
    edge_keys = before_keys[WINDOW - CMP_STRIDE :]
    edge_values = before_values[WINDOW - CMP_STRIDE :]
    held_tail = jnp.where(place == 0, moved_tail, jnp.zeros_like(moved_tail))
    tail_size = held_tail.shape[0]
    tail_flat = held_tail
    near_keys = []
    near_values = []
    nearby_positions = []
    near_valid = []
    own = pack_rows(incoming_keys, new_values)
    own_size = own.shape[0]
    for back in range(lookback_length, 0, -1):
        moved = from_behind(jnp.concatenate([own, held_tail]), "seq", back)
        got_keys, got_values = unpack_rows(moved, query_count, key_width, value_width)
        tail_flat = jnp.where(place == back, moved[own_size : own_size + tail_size], tail_flat)
        near_keys.append(got_keys)
        near_values.append(got_values)
        nearby_positions.append(
            (place - back) * query_count + jnp.arange(query_count, dtype=jnp.int32)
        )
        near_valid.append(jnp.broadcast_to(place >= back, (query_count,)))
    tail_keys, tail_values = unpack_rows(tail_flat, WINDOW, key_width, value_width)
    near_keys.append(tail_keys)
    near_values.append(tail_values)
    nearby_positions.append(jnp.arange(WINDOW, dtype=jnp.int32) - WINDOW)
    near_valid.append(jnp.ones((WINDOW,), dtype=bool))
    near_keys.append(incoming_keys)
    near_values.append(new_values)
    nearby_positions.append(stretch_pos)
    near_valid.append(jnp.ones((query_count,), dtype=bool))
    half_keys = CMP_STRIDE * key_width
    half_values = CMP_STRIDE * value_width
    lead_keys = jnp.concatenate([edge_keys, cache_keys[: cache_count - CMP_STRIDE]]).reshape(
        -1, half_keys
    )
    lead_values = jnp.concatenate([edge_values, cache_values[: cache_count - CMP_STRIDE]]).reshape(
        -1, half_values
    )
    comp_keys = (
        jnp.dot(lead_keys, weight_keys[:half_keys], preferred_element_type=jnp.float32)
        + jnp.dot(
            cache_keys.reshape(-1, half_keys),
            weight_keys[half_keys:],
            preferred_element_type=jnp.float32,
        )
    ).astype(jnp.bfloat16)
    comp_values = (
        jnp.dot(lead_values, weight_values[:half_values], preferred_element_type=jnp.float32)
        + jnp.dot(
            cache_values.reshape(-1, half_values),
            weight_values[half_values:],
            preferred_element_type=jnp.float32,
        )
    ).astype(jnp.bfloat16)
    start = jnp.int32(0)
    top = jnp.full((row_total,), MASKED, jnp.float32)
    total = jnp.zeros((row_total,), jnp.float32)
    summed = jnp.zeros((row_total, value_width), jnp.float32)
    keys = lax.all_gather(comp_keys, "seq", axis=0, tiled=True)
    values = lax.all_gather(comp_values, "seq", axis=0, tiled=True)
    length = keys.shape[0]
    block = length
    for size in (1024, 512, 256, 128):
        if length % size == 0:
            block = size
            break
    for index in range(length // block):
        key_block = keys[index * block : (index + 1) * block]
        value_block = values[index * block : (index + 1) * block]
        scores = (
            jnp.einsum("rd,kd->rk", rows, key_block, preferred_element_type=jnp.float32) * scale
        )
        key_at = start + index * block + jnp.arange(block, dtype=jnp.int32)
        scores = jnp.where(key_at[None, :] > 0, scores, MASKED)
        newtop = jnp.maximum(top, jnp.max(scores, axis=1))
        factor = jnp.exp(top - newtop)
        weights = jnp.exp(scores - newtop[:, None])
        total = total * factor + jnp.sum(weights, axis=1)
        summed = summed * factor[:, None] + jnp.dot(
            weights.astype(jnp.bfloat16), value_block, preferred_element_type=jnp.float32
        )
        top = newtop
    top, total, summed = (top, total, summed)
    compressed_out = summed / total[:, None]
    chosen = select_blocks.reshape(-1)
    shard_blocks = cache_count // SEL_BLOCK
    capacity = max(2, 2 * chosen.shape[0] // ranks)
    owner = chosen // shard_blocks
    local = chosen - owner * shard_blocks
    count = chosen.shape[0]
    order = jnp.arange(count, dtype=jnp.int32)
    same = owner[:, None] == owner[None, :]
    position = jnp.sum((same & (order[None, :] < order[:, None])).astype(jnp.int32), axis=1)
    where_at = owner * capacity + position
    slots = jnp.arange(ranks * capacity, dtype=jnp.int32)
    wanted = where_at[:, None] == slots[None, :]
    request = jnp.sum(jnp.where(wanted, local[:, None], 0), axis=0).reshape(ranks, capacity)
    asked = lax.all_to_all(request, "seq", split_axis=0, concat_axis=0, tiled=True)
    tile_count = select_blocks.shape[0]

    def picked(hot, table):
        return jnp.dot(
            hot.astype(jnp.bfloat16), table, preferred_element_type=jnp.float32
        ).astype(jnp.bfloat16)

    asked_hot = asked.reshape(-1, 1) == jnp.arange(shard_blocks, dtype=jnp.int32)[None, :]

    def fetched(table):
        sent = picked(asked_hot, table.reshape(shard_blocks, -1)).reshape(ranks, capacity, -1)
        got = lax.all_to_all(sent, "seq", split_axis=0, concat_axis=0, tiled=True)
        return picked(wanted, got.reshape(ranks * capacity, -1))

    gathered_keys = fetched(cache_keys)
    picked_values = fetched(cache_values)
    gathered_keys, picked_values = (
        gathered_keys.reshape(tile_count, -1, key_width),
        picked_values.reshape(tile_count, -1, value_width),
    )
    tile_count = gathered_keys.shape[0]
    tile_row_count = rows.reshape(tile_count, -1, key_width)
    tile_scores = (
        jnp.einsum(
            "izu,ixu->izx", tile_row_count, gathered_keys, preferred_element_type=jnp.float32
        )
        * scale
    )
    selected_out = finish_rows(tile_scores, picked_values).reshape(row_total, value_width)
    context_keys = jnp.concatenate(near_keys)
    context_values = jnp.concatenate(near_values)
    context_positions = jnp.concatenate(nearby_positions)
    context_valid = jnp.concatenate(near_valid)
    sliding_scores = (
        jnp.einsum("rd,kd->rk", rows, context_keys, preferred_element_type=jnp.float32) * scale
    )
    allowed = (
        context_valid[None, :]
        & (context_positions[None, :] <= stretch_pos[:, None])
        & (context_positions[None, :] > stretch_pos[:, None] - WINDOW)
    )
    sliding_scores = jnp.where(
        allowed[:, None, :], sliding_scores.reshape(query_count, heads, -1), MASKED
    )
    window_out = finish_rows(sliding_scores.reshape(row_total, -1), context_values)
    logits = jnp.einsum(
        "thd,hdb->thb",
        queries.reshape(query_count, heads, key_width),
        gate_weight,
        preferred_element_type=jnp.float32,
    )
    gates = jax.nn.sigmoid(logits)
    mixed = (
        gates[:, :, 0:1] * compressed_out.reshape(query_count, heads, value_width)
        + gates[:, :, 1:2] * selected_out.reshape(query_count, heads, value_width)
        + gates[:, :, 2:3] * window_out.reshape(query_count, heads, value_width)
    )
    return mixed.astype(jnp.bfloat16).reshape(query_count, heads * value_width)


CORES = 2
PIECES = 4
LOG2E = 1.4426950408889634
MESH = pl.DeviceIdType.MESH


def fused_kernel(
    n_seq,
    n_kv,
    tiles,
    sel,
    q,
    ckt,
    cv,
    ikt,
    iv,
    wkt,
    wv,
    gw,
    out,
    q_vm,
    ckt_vm,
    ikt_vm,
    gw_vm,
    kh,
    v,
    kl,
    nkh,
    nv,
    nkl,
    k_ext,
    v_ext,
    perm,
    lhs_k,
    lhs_v,
    wk_all,
    wv_all,
    comp_vm,
    comp_all,
    compk,
    compv,
    rows_vm,
    gates_vm,
    acc,
    win_k,
    win_v,
    sel_k,
    sel_v,
    local_sem,
    own_sem,
    kv_send,
    kv_recv,
    new_send,
    new_recv,
    w_send,
    w_recv,
    comp_send,
    comp_recv,
):
    me = lax.axis_index("seq")
    group = lax.axis_index("kv")
    z = me // CORES
    core = lax.rem(me, CORES)
    chips = n_seq // CORES
    mate = z * CORES + 1 - core
    left = lax.rem(me - CORES + n_seq, n_seq)
    right = lax.rem(me + CORES, n_seq)
    route = (left, right, mate)
    width, cache = ckt.shape
    fresh = ikt.shape[1]
    vw = v.shape[2]
    low = width - vw
    per = cache // SEL_BLOCK
    new_per = fresh // SEL_BLOCK
    half_block = SEL_BLOCK // 2
    heads = q.shape[1] // width
    tile = fresh // tiles
    count = heads * tile
    lookback = WINDOW // fresh
    hops = -(-lookback // CORES)
    chunks = cache // CMP_STRIDE
    pad = chunks + CMP_STRIDE
    factor = width**-0.5 * LOG2E

    barrier = pltpu.get_barrier_semaphore()
    for d in range(1, n_seq):
        pl.semaphore_signal(
            barrier, inc=1, device_id={"seq": lax.rem(me + d, n_seq)}, device_id_type=MESH
        )
    for d in range(1, n_kv):
        pl.semaphore_signal(
            barrier, inc=1, device_id={"kv": lax.rem(group + d, n_kv)}, device_id_type=MESH
        )

    half_k = wkt.shape[1] // CORES
    half_v = wv.shape[0] // CORES
    loads = [
        (cv, v.at[pl.ds(me * per, per)]),
        (iv, nv.at[pl.ds(me * new_per, new_per)]),
        (ckt, ckt_vm),
        (ikt, ikt_vm),
        (q, q_vm),
        (gw, gw_vm),
    ]
    for half in range(CORES):
        loads.append((wkt.at[:, pl.ds(half * half_k, half_k)], wk_all.at[group, half]))
        loads.append((wv.at[pl.ds(half * half_v, half_v)], wv_all.at[group, half]))
    load_copies = [pltpu.make_async_copy(a, b, local_sem.at[n]) for n, (a, b) in enumerate(loads)]
    for copy in load_copies:
        copy.start()

    old = (v, kh, kl)
    new = (nv, nkh, nkl)

    def pieces_of(half):
        return range(PIECES // 2 * half, PIECES // 2 * (half + 1))[::-1]

    def old_msg(slot, way, part, piece):
        size = per // PIECES
        ref = old[part].at[pl.ds(slot * per + piece * size, size)]
        return pltpu.make_async_remote_copy(
            src_ref=ref,
            dst_ref=ref,
            send_sem=kv_send.at[way, slot, part, piece],
            recv_sem=kv_recv.at[slot, part, piece],
            device_id={"seq": route[way]},
            device_id_type=MESH,
        )

    def new_msg(slot, way, part, half):
        ref = new[part].at[pl.ds(slot * new_per, new_per)]
        return pltpu.make_async_remote_copy(
            src_ref=ref,
            dst_ref=ref,
            send_sem=new_send.at[way, slot, part],
            recv_sem=new_recv.at[slot, part],
            device_id={"seq": route[way]},
            device_id_type=MESH,
        )

    def start(make, slot, way, half, parts=range(3)):
        for part in parts:
            make(slot, way, part, half).start()

    def recv(make, slot, half):
        for part in range(3):
            make(slot, 2, part, half).wait_recv()

    def sent(make, slot, way, half):
        for part in range(3):
            make(slot, way, part, half).wait_send()

    def start_own(parts):
        for half in range(PIECES)[::-1]:

            @pl.when(z < chips - 1)
            def _():
                start(old_msg, me, 1, half, parts)

            @pl.when(z > 0)
            def _():
                start(old_msg, me, 0, half, parts)

            start(old_msg, me, 2, half, parts)

    w_all = (wk_all, wv_all)
    w_own = (
        wkt.at[:, pl.ds(pl.multiple_of(core * half_k, half_k), half_k)],
        wv.at[pl.ds(pl.multiple_of(core * half_v, half_v), half_v)],
    )

    def w_msg(d, part):
        return pltpu.make_async_remote_copy(
            src_ref=w_own[part],
            dst_ref=w_all[part].at[group, core],
            send_sem=w_send.at[d - 1, part],
            recv_sem=w_recv.at[group, core, part],
            device_id={"kv": lax.rem(group + d, n_kv)},
            device_id_type=MESH,
        )

    def w_arrived(who, half, part):
        return pltpu.make_async_remote_copy(
            src_ref=w_all[part].at[who, half],
            dst_ref=w_all[part].at[who, half],
            send_sem=w_send.at[n_kv - 1 + lax.rem(who - group + n_kv, n_kv) - 1, part],
            recv_sem=w_recv.at[who, half, part],
            device_id={"seq": mate},
            device_id_type=MESH,
        )

    load_copies[0].wait()
    load_copies[1].wait()
    pl.semaphore_wait(barrier, n_seq - 1 + n_kv - 1)
    start_own((0,))
    for d in range(1, n_kv):
        for part in range(2):
            w_msg(d, part).start()

    def pack(keys, blocks, hi, lo, at):
        hi[pl.ds(at, blocks)] = keys[:, 0:vw].reshape(blocks, SEL_BLOCK, vw)
        part = keys[:, vw:width].reshape(blocks, 2, half_block, low)
        lo[pl.ds(at, blocks)] = jnp.concatenate([part[:, 0], part[:, 1]], axis=-1)

    load_copies[2].wait()
    keys = ckt_vm[...].T
    pack(keys, per, kh, kl, me * per)
    k_ext[CMP_STRIDE:, :] = keys
    load_copies[3].wait()
    pack(ikt_vm[...].T, new_per, nkh, nkl, me * new_per)
    v_ext[CMP_STRIDE:, :] = v[pl.ds(me * per, per)].reshape(cache, vw)
    for copy in load_copies[4:]:
        copy.wait()

    @pl.when(z < chips - 1)
    def _():
        start(new_msg, me, 1, 0)

    start_own((1, 2))
    start(new_msg, me, 2, 0)

    @pl.loop(0, tiles)
    def _(t):
        part = q_vm[pl.ds(pl.multiple_of(t * tile, tile), tile), :]
        for h in range(heads):
            at = pl.multiple_of(t * count + h * tile, tile)
            rows_vm[pl.ds(at, tile), :] = part[:, h * width : (h + 1) * width]

    logits = lax.dot_general(
        rows_vm[...], gw_vm[...], (((1,), (1,)), ((), ())), preferred_element_type=jnp.float32
    )
    gates_vm[...] = jax.nn.sigmoid(logits)
    lag = lax.broadcasted_iota(jnp.int32, (pad, cache + CMP_STRIDE), 1)
    lag = lag - CMP_STRIDE * lax.broadcasted_iota(jnp.int32, lag.shape, 0)

    @pl.loop(0, CMP_STRIDE)
    def _(p):
        at = pl.multiple_of(p * pad, CMP_STRIDE)
        perm[pl.ds(at, pad), :] = jnp.where(lag == p, 1.0, 0.0).astype(jnp.bfloat16)

    for d in range(1, min(hops, chips - 1) + 1):

        @pl.when(z >= d)
        def _():
            slot = me - CORES * d
            recv(new_msg, slot, 0)
            if d < hops:

                @pl.when(z < chips - 1)
                def _():
                    start(new_msg, slot, 1, 0)

            start(new_msg, slot, 2, 0)

    def relay(d, side):
        for piece in pieces_of(side):
            relay_piece(d, piece)

    def recv_side(slot, side):
        for piece in pieces_of(side):
            recv(old_msg, slot, piece)

    def relay_piece(d, half):
        @pl.when(z >= d)
        def _():
            slot = me - CORES * d
            recv(old_msg, slot, half)

            @pl.when(z < chips - 1)
            def _():
                start(old_msg, slot, 1, half)

            start(old_msg, slot, 2, half)

        @pl.when(z + d < chips)
        def _():
            slot = me + CORES * d
            recv(old_msg, slot, half)

            @pl.when(z > 0)
            def _():
                start(old_msg, slot, 0, half)

            start(old_msg, slot, 2, half)

    def comp_send_own(d):
        to = lax.rem(me + CORES * d, n_seq) if d else mate
        return pltpu.make_async_remote_copy(
            src_ref=comp_vm,
            dst_ref=comp_all.at[me],
            send_sem=comp_send.at[d],
            recv_sem=comp_recv.at[me],
            device_id={"seq": to},
            device_id_type=MESH,
        )

    def comp_pass(d):
        who = lax.rem(me + CORES * d, n_seq)
        return pltpu.make_async_remote_copy(
            src_ref=comp_all.at[who],
            dst_ref=comp_all.at[who],
            send_sem=comp_send.at[chips + d - 1],
            recv_sem=comp_recv.at[who],
            device_id={"seq": mate},
            device_id_type=MESH,
        )

    def comp_take(who):
        return pltpu.make_async_remote_copy(
            src_ref=comp_all.at[who],
            dst_ref=comp_all.at[who],
            send_sem=comp_send.at[0],
            recv_sem=comp_recv.at[who],
            device_id={"seq": mate},
            device_id_type=MESH,
        )

    comp_keep = pltpu.make_async_copy(comp_vm, comp_all.at[me], own_sem)

    def spread_tokens():
        tail = SEL_BLOCK - CMP_STRIDE

        @pl.when(me > 0)
        def _():
            recv_side(me - 1, 1)
            block = me * per - 1
            k_ext[0:CMP_STRIDE, 0:vw] = kh[block, tail:SEL_BLOCK]
            k_ext[0:CMP_STRIDE, vw:width] = kl[block, tail - half_block : half_block, low:]
            v_ext[0:CMP_STRIDE, :] = v[block, tail:SEL_BLOCK]

        @pl.when(me == 0)
        def _():
            k_ext[0:CMP_STRIDE, :] = jnp.zeros((CMP_STRIDE, width), jnp.bfloat16)
            v_ext[0:CMP_STRIDE, :] = jnp.zeros((CMP_STRIDE, vw), jnp.bfloat16)

        for lhs, ext in ((lhs_k, k_ext), (lhs_v, v_ext)):
            spread = jnp.dot(perm[...], ext[...], preferred_element_type=jnp.float32)
            spread = spread.astype(jnp.bfloat16)
            each = ext.shape[1]
            for p in range(CMP_STRIDE):
                lhs[:, p * each : (p + 1) * each] = spread[p * pad : (p + 1) * pad]

    def pass_weights():
        for d in range(1, n_kv):
            who = lax.rem(group + n_kv - d, n_kv)
            for part in range(2):
                w_arrived(who, core, part).wait_recv()
                w_arrived(who, core, part).start()

    def compress():
        for d in range(1, n_kv):
            who = lax.rem(group + n_kv - d, n_kv)
            for part in range(2):
                w_arrived(who, 1 - core, part).wait_recv()
        results = []
        for lhs, w, dims in (
            (lhs_k, wk_all, (((1,), (1,)), ((), ()))),
            (lhs_v, wv_all, (((1,), (0,)), ((), ()))),
        ):
            pieces = n_kv * CORES // 2
            depth = lhs.shape[1] // pieces
            sums = []
            for side in range(2):
                total = None
                for n in range(pieces):
                    at = side * pieces + n
                    term = lax.dot_general(
                        lhs[:, n * depth : (n + 1) * depth],
                        w[at // CORES, at % CORES],
                        dims,
                        preferred_element_type=jnp.float32,
                    )
                    total = term if total is None else total + term
                sums.append(total)
            results.append((sums[0][0:chunks] + sums[1][1 : chunks + 1]).astype(jnp.bfloat16))
        made, made_v = results
        comp_vm[0:chunks, :] = made[:, 0:vw]
        comp_vm[chunks : 2 * chunks, :] = made_v
        comp_vm[2 * chunks :, :] = jnp.concatenate(
            [made[0 : chunks // 2, vw:width], made[chunks // 2 :, vw:width]], axis=-1
        )
        for d in range(1, chips):
            comp_send_own(d).start()
        comp_send_own(0).start()
        comp_keep.start()

    def attend(rows, keys, values, allowed):
        s = lax.dot_general(
            rows, keys, (((1,), (1,)), ((), ())), preferred_element_type=jnp.float32
        )
        if allowed is not None:
            s = jnp.where(allowed, s, MASKED)
        top = jnp.max(s, axis=-1, keepdims=True)
        w = jnp.exp2((s - top) * factor)
        total = jnp.sum(w, axis=-1, keepdims=True)
        o = jnp.dot(w.astype(jnp.bfloat16), values, preferred_element_type=jnp.float32)
        return o / total

    def gated(branch, t, o, emit):
        g = gates_vm[pl.ds(pl.multiple_of(t * count, count), count), :]
        for h in range(heads):
            a = slice(h * tile, (h + 1) * tile)
            at = branch * heads + h
            emit(h, pl.ds(pl.multiple_of(t * count + h * tile, tile), tile), g[a, at : at + 1] * o[a])

    def rows_of(t):
        return rows_vm[pl.ds(pl.multiple_of(t * count, count), count), :]

    def compressed():
        comp_keep.wait()
        for d in range(1, chips):
            comp_pass(d).wait_recv()
            comp_pass(d).start()
        for zz in range(chips):
            comp_take(zz * CORES + 1 - core).wait_recv()
        total = n_seq * chunks
        for slot in range(n_seq):
            at, mid = slot * chunks, slot * chunks + chunks // 2
            compk[at : at + chunks, 0:vw] = comp_all[slot, 0:chunks]
            compk[at:mid, vw:width] = comp_all[slot, 2 * chunks :, 0:low]
            compk[mid : at + chunks, vw:width] = comp_all[slot, 2 * chunks :, low : 2 * low]
            compv[at : at + chunks, :] = comp_all[slot, chunks : 2 * chunks]
        ok = lax.broadcasted_iota(jnp.int32, (count, total), 1) > 0

        @pl.loop(0, tiles)
        def _(t):
            o = attend(
                rows_of(t),
                compk[...],
                compv[...],
                ok,
            )

            def emit(h, at, x):
                acc[at, :] = x

            gated(0, t, o, emit)

    def put(dk, dv, at, khv, vv, klv):
        dk[pl.ds(at, SEL_BLOCK), 0:vw] = khv
        dk[pl.ds(at, half_block), vw:width] = klv[:, 0:low]
        dk[pl.ds(at + half_block, half_block), vw:width] = klv[:, low : 2 * low]
        dv[pl.ds(at, SEL_BLOCK), :] = vv

    def window():
        @pl.when(core == 0)
        def _():
            recv_side(n_seq - 1, 1)

        for d in range(0, min(hops, chips - 1) + 1):

            @pl.when(z >= d)
            def _():
                recv(new_msg, (z - d) * CORES + 1 - core, 0)

        for i in range(lookback + 1):
            chunk = me + i
            for b in range(new_per):
                at = (i * new_per + b) * SEL_BLOCK

                @pl.when(chunk < lookback)
                def _():
                    block = n_seq * per - lookback * new_per + chunk * new_per + b
                    put(win_k, win_v, at, kh[block], v[block], kl[block])

                @pl.when(chunk >= lookback)
                def _():
                    block = (chunk - lookback) * new_per + b
                    put(win_k, win_v, at, nkh[block], nv[block], nkl[block])

        span = WINDOW + tile
        diff = lax.broadcasted_iota(jnp.int32, (count, span), 1) - lax.rem(
            lax.broadcasted_iota(jnp.int32, (count, span), 0), tile
        )
        ok = (diff > 0) & (diff <= WINDOW)

        @pl.loop(0, tiles)
        def _(t):
            off = pl.multiple_of(t * tile, tile)
            o = attend(rows_of(t), win_k[pl.ds(off, span), :], win_v[pl.ds(off, span), :], ok)

            def emit(h, at, x):
                acc[at, :] += x

            gated(2, t, o, emit)

    def selected():
        picks = sel.shape[1]

        @pl.loop(0, tiles)
        def _(t):
            for n in range(picks):
                block = sel[t, n]
                put(sel_k, sel_v, n * SEL_BLOCK, kh[block], v[block], kl[block])
            o = attend(rows_of(t), sel_k[...], sel_v[...], None)

            def emit(h, at, x):
                to = pl.ds(pl.multiple_of(t * tile, tile), tile)
                out[to, h * vw : (h + 1) * vw] = (acc[at, :] + x).astype(out.dtype)

            gated(1, t, o, emit)

    relay(1, 1)
    relay(1, 0)
    spread_tokens()
    pass_weights()
    compress()
    for d in range(2, chips - 1):
        relay(d, 1)
        relay(d, 0)
    compressed()
    relay(chips - 1, 1)
    window()
    relay(chips - 1, 0)

    for zz in range(chips):
        slot = zz * CORES + 1 - core
        recv_side(slot, 0)
        early = slot == me - 1
        if zz == chips - 1:
            early = early | (core == 0)

        @pl.when(jnp.logical_not(early))
        def _():
            recv_side(slot, 1)

    selected()

    for d in range(1, n_kv):
        for part in range(2):
            w_msg(d, part).wait_send()
            w_arrived(lax.rem(group + n_kv - d, n_kv), core, part).wait_send()
    for d in range(0, chips):
        comp_send_own(d).wait_send()
    for d in range(1, chips):
        comp_pass(d).wait_send()

    def all_sent(slot, ways):
        for way in ways:
            for half in range(PIECES):
                sent(old_msg, slot, way, half)

    @pl.when(z < chips - 1)
    def _():
        sent(new_msg, me, 1, 0)
        all_sent(me, (1,))

    @pl.when(z > 0)
    def _():
        all_sent(me, (0,))

    sent(new_msg, me, 2, 0)
    all_sent(me, (2,))
    for d in range(1, chips):

        @pl.when(z >= d)
        def _():
            slot = me - CORES * d
            if d <= hops:
                sent(new_msg, slot, 2, 0)

                if d < hops:

                    @pl.when(z < chips - 1)
                    def _():
                        sent(new_msg, slot, 1, 0)

            all_sent(slot, (2,))

            @pl.when(z < chips - 1)
            def _():
                all_sent(slot, (1,))

        @pl.when(z + d < chips)
        def _():
            slot = me + CORES * d
            all_sent(slot, (2,))

            @pl.when(z > 0)
            def _():
                all_sent(slot, (0,))


def shards_gathered(q, ck, cv, ik, iv, wk, wv, sel, gw):
    n_seq, n_kv = lax.axis_size("seq"), lax.axis_size("kv")
    heads, width, branches = gw.shape
    vw = cv.shape[1]
    cache, fresh = ck.shape[0], ik.shape[0]
    tiles, picks = sel.shape[0], sel.shape[-1]
    chunks = cache // CMP_STRIDE
    pad = chunks + CMP_STRIDE
    per, new_per = cache // SEL_BLOCK, fresh // SEL_BLOCK
    tile_rows = heads * fresh
    bf = jnp.bfloat16
    any_spec = pl.BlockSpec(memory_space=pl.ANY)
    half_k, half_v = wk.shape[0] // CORES, wv.shape[0] // CORES

    def held(*shape):
        return pltpu.VMEM(shape, bf)

    dma = pltpu.SemaphoreType.DMA
    return pl.pallas_call(
        functools.partial(fused_kernel, n_seq, n_kv, tiles),
        out_shape=jax.ShapeDtypeStruct((fresh, heads * vw), bf),
        in_specs=[pl.BlockSpec(memory_space=pltpu.SMEM)] + [any_spec] * 8,
        out_specs=pl.BlockSpec(memory_space=pltpu.VMEM),
        scratch_shapes=[
            held(*q.shape),
            held(width, cache),
            held(width, fresh),
            held(heads * branches, width),
            held(n_seq * per, SEL_BLOCK, vw),
            held(n_seq * per, SEL_BLOCK, vw),
            held(n_seq * per, SEL_BLOCK // 2, vw),
            held(n_seq * new_per, SEL_BLOCK, vw),
            held(n_seq * new_per, SEL_BLOCK, vw),
            held(n_seq * new_per, SEL_BLOCK // 2, vw),
            held(cache + CMP_STRIDE, width),
            held(cache + CMP_STRIDE, vw),
            held(CMP_STRIDE * pad, cache + CMP_STRIDE),
            held(pad, CMP_STRIDE * width),
            held(pad, CMP_STRIDE * vw),
            held(n_kv, CORES, width, half_k),
            held(n_kv, CORES, half_v, vw),
            held(2 * chunks + chunks // 2, vw),
            held(n_seq, 2 * chunks + chunks // 2, vw),
            held(n_seq * chunks, width),
            held(n_seq * chunks, vw),
            held(tile_rows, width),
            pltpu.VMEM((tile_rows, heads * branches), jnp.float32),
            pltpu.VMEM((tile_rows, vw), jnp.float32),
            held(fresh + WINDOW, width),
            held(fresh + WINDOW, vw),
            held(picks * SEL_BLOCK, width),
            held(picks * SEL_BLOCK, vw),
            dma((6 + 2 * CORES,)),
            dma,
            dma((3, n_seq, 3, PIECES)),
            dma((n_seq, 3, PIECES)),
            dma((3, n_seq, 3)),
            dma((n_seq, 3)),
            dma((2 * (n_kv - 1), 2)),
            dma((n_kv, CORES, 2)),
            dma((n_seq - 1,)),
            dma((n_seq,)),
        ],
        compiler_params=pltpu.CompilerParams(
            collective_id=0, has_side_effects=True, vmem_limit_bytes=60 << 20
        ),
    )(
        sel.reshape(tiles, picks),
        q,
        ck.T,
        cv.reshape(per, SEL_BLOCK, vw),
        ik.T,
        iv.reshape(new_per, SEL_BLOCK, vw),
        wk.T,
        wv,
        jnp.transpose(gw, (2, 0, 1)).reshape(heads * branches, width),
    )


GATHER_BYTES = 1 << 24


def shards(queries, cache_keys, cache_values, *rest):
    ranks = lax.axis_size("seq")
    size = ranks * 2 * (cache_keys.size + cache_values.size)
    form = shards_gathered if size <= GATHER_BYTES else shards_by_request
    return form(queries, cache_keys, cache_values, *rest)


def solution(mesh):
    placed = (
        P("seq", "kv"),
        P("seq", "kv"),
        P("seq", "kv"),
        P("seq", "kv"),
        P("seq", "kv"),
        P("kv", None),
        P("kv", None),
        P("seq", "kv", None),
        P("kv", None, None),
    )
    return jax.shard_map(
        shards, mesh=mesh, in_specs=placed, out_specs=P("seq", "kv"), check_vma=False
    )
```

```python
import functools

import jax
import jax.numpy as jnp
from jax import lax
from jax.experimental import pallas as pl
from jax.experimental.pallas import tpu as pltpu
from jax.sharding import PartitionSpec as P

CMP_STRIDE = 16
SEL_BLOCK = 64
WINDOW = 512


MASKED = -1e30


def passed_along(block, axis, distance):
    devices = range(lax.axis_size(axis))
    route = [((i - distance) % len(devices), i) for i in devices]
    return lax.ppermute(block, axis, route)


def from_behind(x, axis, by):
    peers = lax.axis_size(axis)
    pairs = [(i, i + by) for i in range(peers) if 0 <= i + by < peers]
    return lax.ppermute(x, axis, pairs)


def pack_rows(keys, values):
    return jnp.concatenate([keys.reshape(-1), values.reshape(-1)])


def unpack_rows(flat, count, key_width, value_width):
    keys = flat[: count * key_width].reshape(count, key_width)
    values = flat[count * key_width : count * (key_width + value_width)].reshape(count, value_width)
    return (keys, values)


def finish_rows(scores, values):
    top = jnp.max(scores, axis=-1, keepdims=True)
    weights = jnp.exp(scores - top)
    total = jnp.sum(weights, axis=-1, keepdims=True)
    mixed = jnp.matmul(weights.astype(jnp.bfloat16), values, preferred_element_type=jnp.float32)
    return mixed / total


def shards_by_request(
    queries,
    cache_keys,
    cache_values,
    incoming_keys,
    new_values,
    comp_key_weight,
    comp_value_weight,
    select_blocks,
    gate_weight,
):
    heads, key_width, _ = gate_weight.shape
    value_width = cache_values.shape[1]
    query_count = queries.shape[0]
    cache_count = cache_keys.shape[0]
    ranks = lax.axis_size("seq")
    place = lax.axis_index("seq")
    scale = key_width ** (-0.5)
    rows = queries.reshape(query_count * heads, key_width)
    row_total = rows.shape[0]
    stretch_pos = place * query_count + jnp.arange(query_count, dtype=jnp.int32)
    lookback_length = -(-WINDOW // query_count)
    weight_keys, weight_values = (
        lax.all_gather(comp_key_weight, "kv", axis=0, tiled=True),
        lax.all_gather(comp_value_weight, "kv", axis=0, tiled=True),
    )
    tail_pack = pack_rows(cache_keys[cache_count - WINDOW :], cache_values[cache_count - WINDOW :])
    moved_tail = passed_along(tail_pack, "seq", 1)
    before_keys, before_values = unpack_rows(moved_tail, WINDOW, key_width, value_width)
    edge_keys = before_keys[WINDOW - CMP_STRIDE :]
    edge_values = before_values[WINDOW - CMP_STRIDE :]
    held_tail = jnp.where(place == 0, moved_tail, jnp.zeros_like(moved_tail))
    tail_size = held_tail.shape[0]
    tail_flat = held_tail
    near_keys = []
    near_values = []
    nearby_positions = []
    near_valid = []
    own = pack_rows(incoming_keys, new_values)
    own_size = own.shape[0]
    for back in range(lookback_length, 0, -1):
        moved = from_behind(jnp.concatenate([own, held_tail]), "seq", back)
        got_keys, got_values = unpack_rows(moved, query_count, key_width, value_width)
        tail_flat = jnp.where(place == back, moved[own_size : own_size + tail_size], tail_flat)
        near_keys.append(got_keys)
        near_values.append(got_values)
        nearby_positions.append(
            (place - back) * query_count + jnp.arange(query_count, dtype=jnp.int32)
        )
        near_valid.append(jnp.broadcast_to(place >= back, (query_count,)))
    tail_keys, tail_values = unpack_rows(tail_flat, WINDOW, key_width, value_width)
    near_keys.append(tail_keys)
    near_values.append(tail_values)
    nearby_positions.append(jnp.arange(WINDOW, dtype=jnp.int32) - WINDOW)
    near_valid.append(jnp.ones((WINDOW,), dtype=bool))
    near_keys.append(incoming_keys)
    near_values.append(new_values)
    nearby_positions.append(stretch_pos)
    near_valid.append(jnp.ones((query_count,), dtype=bool))
    half_keys = CMP_STRIDE * key_width
    half_values = CMP_STRIDE * value_width
    lead_keys = jnp.concatenate([edge_keys, cache_keys[: cache_count - CMP_STRIDE]]).reshape(
        -1, half_keys
    )
    lead_values = jnp.concatenate([edge_values, cache_values[: cache_count - CMP_STRIDE]]).reshape(
        -1, half_values
    )
    comp_keys = (
        jnp.dot(lead_keys, weight_keys[:half_keys], preferred_element_type=jnp.float32)
        + jnp.dot(
            cache_keys.reshape(-1, half_keys),
            weight_keys[half_keys:],
            preferred_element_type=jnp.float32,
        )
    ).astype(jnp.bfloat16)
    comp_values = (
        jnp.dot(lead_values, weight_values[:half_values], preferred_element_type=jnp.float32)
        + jnp.dot(
            cache_values.reshape(-1, half_values),
            weight_values[half_values:],
            preferred_element_type=jnp.float32,
        )
    ).astype(jnp.bfloat16)
    start = jnp.int32(0)
    top = jnp.full((row_total,), MASKED, jnp.float32)
    total = jnp.zeros((row_total,), jnp.float32)
    summed = jnp.zeros((row_total, value_width), jnp.float32)
    keys = lax.all_gather(comp_keys, "seq", axis=0, tiled=True)
    values = lax.all_gather(comp_values, "seq", axis=0, tiled=True)
    length = keys.shape[0]
    block = length
    for size in (1024, 512, 256, 128):
        if length % size == 0:
            block = size
            break
    for index in range(length // block):
        key_block = keys[index * block : (index + 1) * block]
        value_block = values[index * block : (index + 1) * block]
        scores = (
            jnp.einsum("rd,kd->rk", rows, key_block, preferred_element_type=jnp.float32) * scale
        )
        key_at = start + index * block + jnp.arange(block, dtype=jnp.int32)
        scores = jnp.where(key_at[None, :] > 0, scores, MASKED)
        newtop = jnp.maximum(top, jnp.max(scores, axis=1))
        factor = jnp.exp(top - newtop)
        weights = jnp.exp(scores - newtop[:, None])
        total = total * factor + jnp.sum(weights, axis=1)
        summed = summed * factor[:, None] + jnp.dot(
            weights.astype(jnp.bfloat16), value_block, preferred_element_type=jnp.float32
        )
        top = newtop
    top, total, summed = (top, total, summed)
    compressed_out = summed / total[:, None]
    chosen = select_blocks.reshape(-1)
    shard_blocks = cache_count // SEL_BLOCK
    capacity = max(2, 2 * chosen.shape[0] // ranks)
    owner = chosen // shard_blocks
    local = chosen - owner * shard_blocks
    count = chosen.shape[0]
    order = jnp.arange(count, dtype=jnp.int32)
    same = owner[:, None] == owner[None, :]
    position = jnp.sum((same & (order[None, :] < order[:, None])).astype(jnp.int32), axis=1)
    where_at = owner * capacity + position
    slots = jnp.arange(ranks * capacity, dtype=jnp.int32)
    wanted = where_at[:, None] == slots[None, :]
    request = jnp.sum(jnp.where(wanted, local[:, None], 0), axis=0).reshape(ranks, capacity)
    asked = lax.all_to_all(request, "seq", split_axis=0, concat_axis=0, tiled=True)
    tile_count = select_blocks.shape[0]

    def picked(hot, table):
        return jnp.dot(
            hot.astype(jnp.bfloat16), table, preferred_element_type=jnp.float32
        ).astype(jnp.bfloat16)

    asked_hot = asked.reshape(-1, 1) == jnp.arange(shard_blocks, dtype=jnp.int32)[None, :]

    def fetched(table):
        sent = picked(asked_hot, table.reshape(shard_blocks, -1)).reshape(ranks, capacity, -1)
        got = lax.all_to_all(sent, "seq", split_axis=0, concat_axis=0, tiled=True)
        return picked(wanted, got.reshape(ranks * capacity, -1))

    gathered_keys = fetched(cache_keys)
    picked_values = fetched(cache_values)
    gathered_keys, picked_values = (
        gathered_keys.reshape(tile_count, -1, key_width),
        picked_values.reshape(tile_count, -1, value_width),
    )
    tile_count = gathered_keys.shape[0]
    tile_row_count = rows.reshape(tile_count, -1, key_width)
    tile_scores = (
        jnp.einsum(
            "izu,ixu->izx", tile_row_count, gathered_keys, preferred_element_type=jnp.float32
        )
        * scale
    )
    selected_out = finish_rows(tile_scores, picked_values).reshape(row_total, value_width)
    context_keys = jnp.concatenate(near_keys)
    context_values = jnp.concatenate(near_values)
    context_positions = jnp.concatenate(nearby_positions)
    context_valid = jnp.concatenate(near_valid)
    sliding_scores = (
        jnp.einsum("rd,kd->rk", rows, context_keys, preferred_element_type=jnp.float32) * scale
    )
    allowed = (
        context_valid[None, :]
        & (context_positions[None, :] <= stretch_pos[:, None])
        & (context_positions[None, :] > stretch_pos[:, None] - WINDOW)
    )
    sliding_scores = jnp.where(
        allowed[:, None, :], sliding_scores.reshape(query_count, heads, -1), MASKED
    )
    window_out = finish_rows(sliding_scores.reshape(row_total, -1), context_values)
    logits = jnp.einsum(
        "thd,hdb->thb",
        queries.reshape(query_count, heads, key_width),
        gate_weight,
        preferred_element_type=jnp.float32,
    )
    gates = jax.nn.sigmoid(logits)
    mixed = (
        gates[:, :, 0:1] * compressed_out.reshape(query_count, heads, value_width)
        + gates[:, :, 1:2] * selected_out.reshape(query_count, heads, value_width)
        + gates[:, :, 2:3] * window_out.reshape(query_count, heads, value_width)
    )
    return mixed.astype(jnp.bfloat16).reshape(query_count, heads * value_width)


CORES = 2
CHIPS = 4
PIECES = 8
LOG2E = 1.4426950408889634
MESH = pl.DeviceIdType.MESH
FAR, NEAR, ACROSS = range(3)
OWN_INNER, NEAR_INNER, TAIL_OUTER, OWN_MATE, NEAR_MATE, ACROSS_MATE, FAR_MATE = range(7)


def fused_kernel(
    n_seq,
    n_kv,
    tiles,
    sel,
    sel_out,
    q,
    ckt,
    cv,
    ikt,
    iv,
    wkt,
    wv,
    gw,
    out,
    q_vm,
    q_far,
    sel_vm,
    sel_far,
    ckt_vm,
    ikt_vm,
    gw_vm,
    kv,
    new,
    edge_own,
    edge_in,
    lhs_k,
    lhs_v,
    wk_all,
    wv_all,
    comp_vm,
    comp_all,
    compk,
    compv,
    rows_vm,
    rows_far,
    gates_vm,
    acc,
    part_out,
    part_in,
    out_vm,
    win_k,
    win_v,
    sel_k,
    sel_v,
    local_sem,
    own_sem,
    sel_sem,
    out_sem,
    kv_send,
    kv_recv,
    kv_mate,
    new_send,
    new_recv,
    q_send,
    q_recv,
    far_send,
    far_recv,
    part_send,
    part_recv,
    w_send,
    w_recv,
    w_mate,
    comp_send,
    comp_recv,
):
    me = lax.axis_index("seq")
    group = lax.axis_index("kv")
    z = me // CORES
    core = lax.rem(me, CORES)
    chips = n_seq // CORES
    mate = z * CORES + 1 - core
    half_line = z // (chips // 2)
    step = CORES - 2 * CORES * half_line
    inner = me + step
    outer = lax.rem(me - step + n_seq, n_seq)
    middle = (z > 0) & (z < chips - 1)
    at_end = jnp.logical_not(middle)
    right = lax.rem(me + CORES, n_seq)
    width, cache = ckt.shape
    fresh = ikt.shape[1]
    vw = cv.shape[2]
    low = width - vw
    wide = rows_vm.shape[1]
    per = cache // SEL_BLOCK
    size = per // PIECES
    new_per = fresh // SEL_BLOCK
    half_block = SEL_BLOCK // 2
    heads = q.shape[1] // width
    tile = fresh // tiles
    picks = sel.shape[1]
    count = heads * tile
    lookback = WINDOW // fresh
    hops = -(-lookback // CORES)
    chunks = cache // CMP_STRIDE
    pad = chunks + CMP_STRIDE
    factor = width**-0.5 * LOG2E
    tail_pieces = range(PIECES - WINDOW // SEL_BLOCK // size, PIECES)[::-1]
    all_pieces = range(PIECES)[::-1]

    across = inner
    near = (n_seq - CORES) * half_line + core
    far = (n_seq - CORES) * (1 - half_line) + core
    last = n_seq - 1
    takes_tail = (z == 0) & (core == CORES - 1)
    gives_tail = (z == 1) & (core == CORES - 1)
    wants_tail = (z == 0) & (core == 0)

    barrier = pltpu.get_barrier_semaphore()
    for d in range(1, n_seq):
        pl.semaphore_signal(
            barrier, inc=1, device_id={"seq": lax.rem(me + d, n_seq)}, device_id_type=MESH
        )
    for d in range(1, n_kv):
        pl.semaphore_signal(
            barrier, inc=1, device_id={"kv": lax.rem(group + d, n_kv)}, device_id_type=MESH
        )

    half_k = wkt.shape[1] // CORES
    half_v = wv.shape[0] // CORES
    value_rows = pl.ds(SEL_BLOCK, SEL_BLOCK)
    loads = [
        (ckt, ckt_vm),
        (ikt, ikt_vm),
        (iv, new.at[pl.ds(me * new_per, new_per), value_rows]),
        (q, q_vm),
        (gw, gw_vm),
    ]
    for half in range(CORES):
        loads.append((wkt.at[:, pl.ds(half * half_k, half_k)], wk_all.at[group, half]))
        loads.append((wv.at[pl.ds(half * half_v, half_v)], wv_all.at[group, half]))
    load_copies = [pltpu.make_async_copy(a, b, local_sem.at[n]) for n, (a, b) in enumerate(loads)]
    for copy in load_copies:
        copy.start()

    own_at = pl.multiple_of(me * per, per)
    own_values = pltpu.make_async_copy(
        cv, kv.at[pl.ds(own_at, per), value_rows], local_sem.at[len(loads)]
    )
    own_values.start()

    def remote(src, dst, send, recv, to, axis="seq"):
        return pltpu.make_async_remote_copy(
            src_ref=src,
            dst_ref=dst,
            send_sem=send,
            recv_sem=recv,
            device_id={axis: to},
            device_id_type=MESH,
        )

    def blocks(slot, piece, pieces=1):
        return kv.at[pl.ds(pl.multiple_of(slot * per + piece * size, size), pieces * size)]

    def kv_msg(slot, piece, send, recv, to, pieces=1):
        ref = blocks(slot, piece, pieces)
        return remote(ref, ref, kv_send.at[send], recv, to)

    def kv_taken(slot, recv, piece=0, pieces=PIECES):
        kv_msg(slot, piece, 0, recv, mate, pieces).wait_recv()

    def new_msg(slot, send, recv, to):
        ref = new.at[pl.ds(slot * new_per, new_per)]
        return remote(ref, ref, new_send.at[send], new_recv.at[recv], to)

    def new_taken(slot, recv):
        new_msg(slot, 0, recv, mate).wait_recv()

    def new_sent(send):
        new_msg(me, send, 0, mate).wait_send()

    def q_msg(t):
        ref = pl.ds(t * tile, tile)
        return remote(q.at[ref], q_far.at[ref], q_send, q_recv.at[t], inner)

    def sel_msg():
        return remote(sel_out, sel_vm, far_send.at[0], far_recv.at[0], inner)

    def edge_msg():
        return remote(
            edge_own, edge_in, far_send.at[1], far_recv.at[1], lax.rem(me + 1, n_seq)
        )

    def part_msg(t):
        return remote(part_out.at[t], part_in.at[t], part_send, part_recv.at[t], outer)

    w_all = (wk_all, wv_all)
    w_own = (
        wkt.at[:, pl.ds(pl.multiple_of(core * half_k, half_k), half_k)],
        wv.at[pl.ds(pl.multiple_of(core * half_v, half_v), half_v)],
    )

    def w_msg(d, part):
        return remote(
            w_own[part],
            w_all[part].at[group, core],
            w_send.at[part],
            w_recv.at[d - 1, part],
            lax.rem(group + d, n_kv),
            "kv",
        )

    def w_pass(d, part):
        ref = w_all[part].at[lax.rem(group + n_kv - d, n_kv), core]
        return remote(ref, ref, w_send.at[2 + part], w_mate.at[part], mate)

    def w_taken(d, part):
        ref = w_all[part].at[lax.rem(group + n_kv - d, n_kv), core]
        remote(ref, ref, w_send.at[part], w_recv.at[d - 1, part], mate).wait_recv()

    def w_all_but_own(part, send):
        ref = w_all[part].at[pl.ds(0, n_kv - 1), 0]
        return remote(ref, ref, w_send.at[send], w_mate.at[part], mate)

    pl.semaphore_wait(barrier, n_seq - 1 + n_kv - 1)

    @pl.when(at_end)
    def _():
        sel_msg().start()

    for d in range(1, n_kv):
        for part in range(2):
            w_msg(d, part).start()

    def pack(keys, blocks, held, at):
        held[pl.ds(at, blocks), 0:SEL_BLOCK] = keys[:, 0:vw].reshape(blocks, SEL_BLOCK, vw)
        part = keys[:, vw:width].reshape(blocks, 2, half_block, low)
        held[pl.ds(at, blocks), 2 * SEL_BLOCK :] = jnp.concatenate(
            [part[:, 0], part[:, 1]], axis=-1
        )

    for copy in load_copies[0:3]:
        copy.wait()
    pack(ikt_vm[...].T, new_per, new, me * new_per)

    up = z < chips - 1

    @pl.when(up)
    def _():
        new_msg(me, 0, 0, right).start()

    keys = ckt_vm[...].T
    pack(keys, per, kv, own_at)
    own_values.wait()

    @pl.when(at_end)
    def _():
        for piece in all_pieces:
            kv_msg(me, piece, OWN_INNER, kv_recv.at[NEAR, piece], inner).start()
        for t in range(tiles // 2):
            q_msg(t).start()

    @pl.when(middle)
    def _():
        for piece in all_pieces:
            kv_msg(me, piece, OWN_INNER, kv_recv.at[ACROSS, piece], inner).start()
        for piece in all_pieces:
            kv_msg(me, piece, OWN_MATE, kv_mate.at[0], mate).start()

    none = jnp.zeros((CMP_STRIDE, wide - width), jnp.bfloat16)
    edge_own[:, 0:wide] = jnp.concatenate([keys[cache - CMP_STRIDE :], none], axis=-1)
    edge_own[:, wide:] = kv[own_at + per - 1, 2 * SEL_BLOCK - CMP_STRIDE : 2 * SEL_BLOCK]
    has_next = me < n_seq - 1

    @pl.when(has_next)
    def _():
        edge_msg().start()

    new_msg(me, 2, 2, mate).start()
    for copy in load_copies[3:]:
        copy.wait()

    lane = lax.broadcasted_iota(jnp.int32, (tile, wide - width), 1)
    one = jnp.where(lane == 0, 1.0, 0.0).astype(jnp.bfloat16)

    def split_heads(src, t, dst, at):
        part = src[pl.ds(pl.multiple_of(t * tile, tile), tile), :]
        for h in range(heads):
            dst[pl.ds(at + h * tile, tile), :] = jnp.concatenate(
                [part[:, h * width : (h + 1) * width], one], axis=-1
            )

    @pl.loop(0, tiles)
    def _(t):
        split_heads(q_vm, t, rows_vm, pl.multiple_of(t * count, count))

    logits = lax.dot_general(
        rows_vm[:, 0:width],
        gw_vm[...],
        (((1,), (1,)), ((), ())),
        preferred_element_type=jnp.float32,
    )
    gates_vm[...] = jax.nn.sigmoid(logits)

    def relay_new(d):
        slot = me - CORES * d

        @pl.when(z >= d)
        def _():
            new_taken(slot, d - 1)
            new_msg(slot, 2 + d, 2 + d, mate).start()

    def raise_new(at):
        @pl.when(at)
        def _():
            new_msg(me - CORES, 1, 1, right).start()

    def relay_across(pieces):
        @pl.when(middle)
        def _():
            for piece in pieces:
                kv_taken(across, kv_recv.at[ACROSS, piece], piece, 1)
                kv_msg(across, piece, ACROSS_MATE, kv_mate.at[1], mate).start()

    def relay_near(pieces):
        @pl.when(middle)
        def _():
            for piece in pieces:
                kv_taken(near, kv_recv.at[NEAR, piece], piece, 1)
                kv_msg(near, piece, NEAR_INNER, kv_recv.at[FAR, piece], inner).start()
                kv_msg(near, piece, NEAR_MATE, kv_mate.at[2], mate).start()

    def relay_far(pieces):
        @pl.when(middle)
        def _():
            for piece in pieces:
                kv_taken(far, kv_recv.at[FAR, piece], piece, 1)
                kv_msg(far, piece, FAR_MATE, kv_mate.at[3], mate).start()
                if piece in tail_pieces:

                    @pl.when(gives_tail)
                    def _():
                        kv_msg(
                            last, piece, TAIL_OUTER, kv_recv.at[FAR, piece], outer
                        ).start()

    def take_tail():
        @pl.when(takes_tail)
        def _():
            for piece in tail_pieces:
                kv_taken(last, kv_recv.at[FAR, piece], piece, 1)
                kv_msg(last, piece, FAR_MATE, kv_mate.at[3], mate).start()

        @pl.when(wants_tail)
        def _():
            kv_taken(last, kv_mate.at[3], tail_pieces[-1], len(tail_pieces))

    def comp_send_own(d):
        to = lax.rem(me + CORES * d, n_seq)
        return remote(comp_vm, comp_all.at[me], comp_send, comp_recv.at[chips - d - 1], to)

    def comp_pass(d):
        ref = comp_all.at[lax.rem(me + CORES * d, n_seq)]
        return remote(ref, ref, comp_send, comp_recv.at[chips - 1], mate)

    def comp_taken(d):
        ref = comp_all.at[lax.rem(me + CORES * d, n_seq)]
        remote(ref, ref, comp_send, comp_recv.at[d - 1], mate).wait_recv()

    def comp_some(slots):
        ref = comp_all.at[pl.ds(0, slots)]
        return remote(ref, ref, comp_send, comp_recv.at[chips - 1], mate)

    comp_keep = pltpu.make_async_copy(comp_vm, comp_all.at[me], own_sem)

    group_rows = CMP_STRIDE * CMP_STRIDE

    def spread_tokens():
        row = lax.broadcasted_iota(jnp.int32, (group_rows, group_rows), 0)
        token = lax.broadcasted_iota(jnp.int32, (group_rows, group_rows), 1)
        want = lax.rem(row, CMP_STRIDE) * CMP_STRIDE + row // CMP_STRIDE
        perm = jnp.where(token == want, 1.0, 0.0).astype(jnp.bfloat16)

        def lay(lhs, at, spread, each):
            spread = spread.astype(jnp.bfloat16)
            for p in range(CMP_STRIDE):
                lhs[at : at + CMP_STRIDE, p * each : (p + 1) * each] = spread[
                    p * CMP_STRIDE : (p + 1) * CMP_STRIDE
                ]

        for n in range(cache // group_rows):
            some = group_rows // SEL_BLOCK
            v = kv[pl.ds(own_at + n * some, some), SEL_BLOCK : 2 * SEL_BLOCK]
            v = v.reshape(group_rows, vw)
            lay(lhs_v, n * CMP_STRIDE, jnp.dot(perm, v, preferred_element_type=jnp.float32), vw)

        for n in range(cache // group_rows):
            spread = lax.dot_general(
                perm,
                ckt_vm[:, n * group_rows : (n + 1) * group_rows],
                (((1,), (1,)), ((), ())),
                preferred_element_type=jnp.float32,
            )
            lay(lhs_k, n * CMP_STRIDE, spread, width)

        @pl.when(me == 0)
        def _():
            edge_in[...] = jnp.zeros(edge_in.shape, jnp.bfloat16)

        @pl.when(me > 0)
        def _():
            edge_msg().wait_recv()

        row = lax.broadcasted_iota(jnp.int32, (group_rows, CMP_STRIDE), 0)
        token = lax.broadcasted_iota(jnp.int32, (group_rows, CMP_STRIDE), 1)
        want = (token == row // CMP_STRIDE) & (lax.rem(row, CMP_STRIDE) == CMP_STRIDE - 1)
        lead = jnp.where(want, 1.0, 0.0).astype(jnp.bfloat16)
        spread = jnp.dot(lead, edge_in[...], preferred_element_type=jnp.float32)
        lay(lhs_k, chunks, spread[:, 0:width], width)
        lay(lhs_v, chunks, spread[:, wide:], vw)

    def pass_weights():
        for part in range(2):
            for d in range(1, n_kv):
                w_taken(d, part)
                w_pass(d, part).start()

    def compress():
        for part in range(2):
            w_all_but_own(part, part).wait_recv()
        results = []
        for lhs, w, dims in (
            (lhs_k, wk_all, (((1,), (1,)), ((), ()))),
            (lhs_v, wv_all, (((1,), (0,)), ((), ()))),
        ):
            pieces = n_kv * CORES // 2
            depth = lhs.shape[1] // pieces
            sums = []
            for side in range(2):
                total = None
                for n in range(pieces):
                    at = side * pieces + n
                    term = lax.dot_general(
                        lhs[:, n * depth : (n + 1) * depth],
                        w[at // CORES, at % CORES],
                        dims,
                        preferred_element_type=jnp.float32,
                    )
                    total = term if total is None else total + term
                sums.append(total)
            lead = jnp.concatenate([sums[0][pad - 1 : pad], sums[0][0 : chunks - 1]], axis=0)
            results.append((lead + sums[1][0:chunks]).astype(jnp.bfloat16))
        made, made_v = results
        comp_vm[0:chunks, :] = made[:, 0:vw]
        comp_vm[chunks : 2 * chunks, :] = made_v
        comp_vm[2 * chunks :, :] = jnp.concatenate(
            [made[0 : chunks // 2, vw:width], made[chunks // 2 :, vw:width]], axis=-1
        )
        for d in range(1, chips):
            comp_send_own(d).start()
        remote(comp_vm, comp_all.at[me], comp_send, comp_recv.at[chips - 1], mate).start()
        comp_keep.start()

    def attend(rows, keys, values, allowed):
        s = lax.dot_general(
            rows, keys, (((1,), (1,)), ((), ())), preferred_element_type=jnp.float32
        )
        if allowed is not None:
            s = jnp.where(allowed, s, MASKED)
        top = jnp.max(s, axis=-1, keepdims=True)
        w = jnp.exp2((s - top) * factor)
        total = jnp.sum(w, axis=-1, keepdims=True)
        o = jnp.dot(w.astype(jnp.bfloat16), values, preferred_element_type=jnp.float32)
        return o, top, total

    def gated(branch, t, o, emit):
        g = gates_vm[pl.ds(pl.multiple_of(t * count, count), count), :]
        for h in range(heads):
            a = slice(h * tile, (h + 1) * tile)
            at = branch * heads + h
            emit(h, pl.ds(pl.multiple_of(t * count + h * tile, tile), tile), g[a, at : at + 1] * o[a])

    def rows_of(t):
        return rows_vm[pl.ds(pl.multiple_of(t * count, count), count), :]

    def bias_lanes(rows, value):
        lane = lax.broadcasted_iota(jnp.int32, (rows, wide - width), 1)
        return jnp.where(lane == 0, value, 0.0).astype(jnp.bfloat16)

    def compressed():
        comp_keep.wait()
        for d in range(1, chips):
            comp_taken(d)
            comp_pass(d).start()
        comp_some(chips).wait_recv()
        total = n_seq * chunks
        first = lax.broadcasted_iota(jnp.int32, (total, wide - width), 0) == 0
        compk[:, width:wide] = bias_lanes(total, jnp.where(first, MASKED, 0.0))
        for slot in range(n_seq):
            at, mid = slot * chunks, slot * chunks + chunks // 2
            compk[at : at + chunks, 0:vw] = comp_all[slot, 0:chunks]
            compk[at:mid, vw:width] = comp_all[slot, 2 * chunks :, 0:low]
            compk[mid : at + chunks, vw:width] = comp_all[slot, 2 * chunks :, low : 2 * low]
            compv[at : at + chunks, :] = comp_all[slot, chunks : 2 * chunks]

        @pl.loop(0, tiles)
        def _(t):
            o, _, total = attend(rows_of(t), compk[...], compv[...], None)

            def emit(h, at, x):
                acc[at, :] = x

            gated(0, t, o / total, emit)

    def put(dk, dv, at, block, bias):
        rest = block[2 * SEL_BLOCK :]
        rest = jnp.concatenate([rest[:, 0:low], rest[:, low : 2 * low]], axis=0)
        dk[pl.ds(at, SEL_BLOCK), 0:vw] = block[0:SEL_BLOCK]
        dk[pl.ds(at, SEL_BLOCK), vw:wide] = jnp.concatenate([rest, bias], axis=-1)
        dv[pl.ds(at, SEL_BLOCK), :] = block[SEL_BLOCK : 2 * SEL_BLOCK]

    def window():
        relay_new(hops)
        for d in range(hops + 1):

            @pl.when(z >= d)
            def _():
                new_taken((z - d) * CORES + 1 - core, 2 + d)

        none = bias_lanes(SEL_BLOCK, 0.0)
        for i in range(lookback + 1):
            chunk = me + i
            for b in range(new_per):
                at = (i * new_per + b) * SEL_BLOCK

                @pl.when(chunk < lookback)
                def _():
                    block = n_seq * per - lookback * new_per + chunk * new_per + b
                    put(win_k, win_v, at, kv[block], none)

                @pl.when(chunk >= lookback)
                def _():
                    put(win_k, win_v, at, new[(chunk - lookback) * new_per + b], none)

        span = WINDOW + tile
        diff = lax.broadcasted_iota(jnp.int32, (count, span), 1) - lax.rem(
            lax.broadcasted_iota(jnp.int32, (count, span), 0), tile
        )
        ok = (diff > 0) & (diff <= WINDOW)

        @pl.loop(0, tiles)
        def _(t):
            off = pl.multiple_of(t * tile, tile)
            o, _, total = attend(
                rows_of(t), win_k[pl.ds(off, span), :], win_v[pl.ds(off, span), :], ok
            )

            def emit(h, at, x):
                acc[at, :] += x

            gated(2, t, o / total, emit)

    def pick(chosen, t):
        none = bias_lanes(SEL_BLOCK, 0.0)
        for n in range(picks):
            put(sel_k, sel_v, n * SEL_BLOCK, kv[chosen[t, n]], none)

    def exported():
        @pl.loop(0, tiles)
        def _(t):
            q_msg(t).wait_recv()
            split_heads(q_far, t, rows_far, 0)
            pick(sel_far, t)
            o, _, total = attend(rows_far[...], sel_k[...], sel_v[...], None)
            part_out[t] = (o / total).astype(jnp.bfloat16)
            part_msg(t).start()

    def finish(t, o):
        to = pl.ds(pl.multiple_of(t * tile, tile), tile)

        def emit(h, at, x):
            out_vm[to, h * vw : (h + 1) * vw] = (acc[at, :] + x).astype(out.dtype)

        gated(1, t, o, emit)
        pltpu.make_async_copy(out_vm.at[to], out.at[to], out_sem).start()

    relay_new(1)
    raise_new(z == chips // 2)
    spread_tokens()
    for piece in all_pieces[:-2]:
        relay_across((piece,))
        relay_near((piece,))
    relay_across(all_pieces[-2:])
    pass_weights()
    compress()
    relay_near(all_pieces[-2:])
    raise_new((z > 0) & (z < chips // 2))

    @pl.when(at_end)
    def _():
        for t in range(tiles // 2, tiles):
            q_msg(t).start()

    relay_far(all_pieces[: PIECES // 2])
    compressed()
    relay_far(all_pieces[PIECES // 2 :])
    take_tail()

    @pl.when(middle)
    def _():
        sel_msg().wait_recv()
        copy = pltpu.make_async_copy(sel_vm, sel_far, sel_sem)
        copy.start()
        copy.wait()
        for n, slot in enumerate((mate, across, near, far)):
            kv_taken(slot + 1 - 2 * core if n else mate, kv_mate.at[n])
        exported()

    window()

    @pl.when(middle)
    def _():
        @pl.loop(0, tiles)
        def _(t):
            pick(sel, t)
            o, _, total = attend(rows_of(t), sel_k[...], sel_v[...], None)
            finish(t, o / total)

        remote(part_out, part_in, part_send, part_recv.at[0], outer).wait_send()
        for send in (OWN_INNER, NEAR_INNER, OWN_MATE, NEAR_MATE, ACROSS_MATE, FAR_MATE):
            kv_msg(me, 0, send, kv_mate.at[0], mate, PIECES).wait_send()

    @pl.when(gives_tail)
    def _():
        kv_msg(me, 0, TAIL_OUTER, kv_mate.at[0], mate, len(tail_pieces)).wait_send()

    @pl.when(at_end)
    def _():
        @pl.loop(0, tiles)
        def _(t):
            part_msg(t).wait_recv()
            finish(t, part_in[t].astype(jnp.float32))

        kv_msg(me, 0, OWN_INNER, kv_mate.at[0], mate, PIECES).wait_send()
        sel_msg().wait_send()
        remote(q_vm, q_far, q_send, q_recv.at[0], inner).wait_send()

    @pl.when(takes_tail)
    def _():
        kv_msg(me, 0, FAR_MATE, kv_mate.at[0], mate, len(tail_pieces)).wait_send()

    @pl.when(has_next)
    def _():
        edge_msg().wait_send()

    @pl.when(up)
    def _():
        new_sent(0)

    @pl.when(up & (z > 0))
    def _():
        new_sent(1)

    new_sent(2)
    for d in range(1, hops + 1):

        @pl.when(z >= d)
        def _():
            new_sent(2 + d)

    for part in range(2):
        w_all_but_own(part, part).wait_send()
        w_all_but_own(part, 2 + part).wait_send()
    comp_some(n_seq - 1).wait_send()
    pltpu.make_async_copy(out_vm, out, out_sem).wait()


def shards_gathered(q, ck, cv, ik, iv, wk, wv, sel, gw):
    n_seq, n_kv = lax.axis_size("seq"), lax.axis_size("kv")
    heads, width, branches = gw.shape
    vw = cv.shape[1]
    cache, fresh = ck.shape[0], ik.shape[0]
    tiles, picks = sel.shape[0], sel.shape[-1]
    chunks = cache // CMP_STRIDE
    pad = chunks + CMP_STRIDE
    per, new_per = cache // SEL_BLOCK, fresh // SEL_BLOCK
    tile_rows = heads * fresh
    count = tile_rows // tiles
    wide = -(-width // 128) * 128
    block_rows = 2 * SEL_BLOCK + SEL_BLOCK // 2
    bf = jnp.bfloat16
    any_spec = pl.BlockSpec(memory_space=pl.ANY)
    half_k, half_v = wk.shape[0] // CORES, wv.shape[0] // CORES

    def held(*shape):
        return pltpu.VMEM(shape, bf)

    dma = pltpu.SemaphoreType.DMA
    picked = sel.reshape(tiles, picks)
    return pl.pallas_call(
        functools.partial(fused_kernel, n_seq, n_kv, tiles),
        out_shape=jax.ShapeDtypeStruct((fresh, heads * vw), bf),
        in_specs=[
            pl.BlockSpec(memory_space=pltpu.SMEM),
            pl.BlockSpec(memory_space=pltpu.VMEM),
        ]
        + [any_spec] * 8,
        out_specs=any_spec,
        scratch_shapes=[
            held(*q.shape),
            held(*q.shape),
            pltpu.VMEM((tiles, picks), jnp.int32),
            pltpu.SMEM((tiles, picks), jnp.int32),
            held(width, cache),
            held(width, fresh),
            held(heads * branches, width),
            held(n_seq * per, block_rows, vw),
            held(n_seq * new_per, block_rows, vw),
            held(CMP_STRIDE, wide + vw),
            held(CMP_STRIDE, wide + vw),
            held(pad, CMP_STRIDE * width),
            held(pad, CMP_STRIDE * vw),
            held(n_kv, CORES, width, half_k),
            held(n_kv, CORES, half_v, vw),
            held(2 * chunks + chunks // 2, vw),
            held(n_seq, 2 * chunks + chunks // 2, vw),
            held(n_seq * chunks, wide),
            held(n_seq * chunks, vw),
            held(tile_rows, wide),
            held(count, wide),
            pltpu.VMEM((tile_rows, heads * branches), jnp.float32),
            pltpu.VMEM((tile_rows, vw), jnp.float32),
            held(tiles, count, vw),
            held(tiles, count, vw),
            held(fresh, heads * vw),
            held(fresh + WINDOW, wide),
            held(fresh + WINDOW, vw),
            held(picks * SEL_BLOCK, wide),
            held(picks * SEL_BLOCK, vw),
            dma((6 + 2 * CORES,)),
            dma,
            dma,
            dma,
            dma((7,)),
            dma((3, PIECES)),
            dma((4,)),
            dma((3 + -(-WINDOW // (fresh * CORES)),)),
            dma((3 + -(-WINDOW // (fresh * CORES)),)),
            dma,
            dma((tiles,)),
            dma((2,)),
            dma((2,)),
            dma,
            dma((tiles,)),
            dma((4,)),
            dma((n_kv - 1, 2)),
            dma((2,)),
            dma,
            dma((n_seq // CORES,)),
        ],
        compiler_params=pltpu.CompilerParams(
            collective_id=0, has_side_effects=True, vmem_limit_bytes=60 << 20
        ),
    )(
        picked,
        picked,
        q,
        ck.T,
        cv.reshape(per, SEL_BLOCK, vw),
        ik.T,
        iv.reshape(new_per, SEL_BLOCK, vw),
        wk.T,
        wv,
        jnp.transpose(gw, (2, 0, 1)).reshape(heads * branches, width),
    )


GATHER_BYTES = 1 << 24


def shards(queries, cache_keys, cache_values, *rest):
    ranks = lax.axis_size("seq")
    size = ranks * 2 * (cache_keys.size + cache_values.size)
    fits = size <= GATHER_BYTES and ranks == CORES * CHIPS
    form = shards_gathered if fits else shards_by_request
    return form(queries, cache_keys, cache_values, *rest)


def solution(mesh):
    placed = (
        P("seq", "kv"),
        P("seq", "kv"),
        P("seq", "kv"),
        P("seq", "kv"),
        P("seq", "kv"),
        P("kv", None),
        P("kv", None),
        P("seq", "kv", None),
        P("kv", None, None),
    )
    return jax.shard_map(
        shards, mesh=mesh, in_specs=placed, out_specs=P("seq", "kv"), check_vma=False
    )
```

```python
import functools

import jax
import jax.numpy as jnp
from jax import lax
from jax.experimental import pallas as pl
from jax.experimental.pallas import tpu as pltpu
from jax.sharding import PartitionSpec as P

CMP_STRIDE = 16
SEL_BLOCK = 64
WINDOW = 512


MASKED = -1e30


def passed_along(block, axis, distance):
    devices = range(lax.axis_size(axis))
    route = [((i - distance) % len(devices), i) for i in devices]
    return lax.ppermute(block, axis, route)


def from_behind(x, axis, by):
    peers = lax.axis_size(axis)
    pairs = [(i, i + by) for i in range(peers) if 0 <= i + by < peers]
    return lax.ppermute(x, axis, pairs)


def pack_rows(keys, values):
    return jnp.concatenate([keys.reshape(-1), values.reshape(-1)])


def unpack_rows(flat, count, key_width, value_width):
    keys = flat[: count * key_width].reshape(count, key_width)
    values = flat[count * key_width : count * (key_width + value_width)].reshape(count, value_width)
    return (keys, values)


def finish_rows(scores, values):
    top = jnp.max(scores, axis=-1, keepdims=True)
    weights = jnp.exp(scores - top)
    total = jnp.sum(weights, axis=-1, keepdims=True)
    mixed = jnp.matmul(weights.astype(jnp.bfloat16), values, preferred_element_type=jnp.float32)
    return mixed / total


def shards_by_request(
    queries,
    cache_keys,
    cache_values,
    incoming_keys,
    new_values,
    comp_key_weight,
    comp_value_weight,
    select_blocks,
    gate_weight,
):
    heads, key_width, _ = gate_weight.shape
    value_width = cache_values.shape[1]
    query_count = queries.shape[0]
    cache_count = cache_keys.shape[0]
    ranks = lax.axis_size("seq")
    place = lax.axis_index("seq")
    scale = key_width ** (-0.5)
    rows = queries.reshape(query_count * heads, key_width)
    row_total = rows.shape[0]
    stretch_pos = place * query_count + jnp.arange(query_count, dtype=jnp.int32)
    lookback_length = -(-WINDOW // query_count)
    weight_keys, weight_values = (
        lax.all_gather(comp_key_weight, "kv", axis=0, tiled=True),
        lax.all_gather(comp_value_weight, "kv", axis=0, tiled=True),
    )
    tail_pack = pack_rows(cache_keys[cache_count - WINDOW :], cache_values[cache_count - WINDOW :])
    moved_tail = passed_along(tail_pack, "seq", 1)
    before_keys, before_values = unpack_rows(moved_tail, WINDOW, key_width, value_width)
    edge_keys = before_keys[WINDOW - CMP_STRIDE :]
    edge_values = before_values[WINDOW - CMP_STRIDE :]
    held_tail = jnp.where(place == 0, moved_tail, jnp.zeros_like(moved_tail))
    tail_size = held_tail.shape[0]
    tail_flat = held_tail
    near_keys = []
    near_values = []
    nearby_positions = []
    near_valid = []
    own = pack_rows(incoming_keys, new_values)
    own_size = own.shape[0]
    for back in range(lookback_length, 0, -1):
        moved = from_behind(jnp.concatenate([own, held_tail]), "seq", back)
        got_keys, got_values = unpack_rows(moved, query_count, key_width, value_width)
        tail_flat = jnp.where(place == back, moved[own_size : own_size + tail_size], tail_flat)
        near_keys.append(got_keys)
        near_values.append(got_values)
        nearby_positions.append(
            (place - back) * query_count + jnp.arange(query_count, dtype=jnp.int32)
        )
        near_valid.append(jnp.broadcast_to(place >= back, (query_count,)))
    tail_keys, tail_values = unpack_rows(tail_flat, WINDOW, key_width, value_width)
    near_keys.append(tail_keys)
    near_values.append(tail_values)
    nearby_positions.append(jnp.arange(WINDOW, dtype=jnp.int32) - WINDOW)
    near_valid.append(jnp.ones((WINDOW,), dtype=bool))
    near_keys.append(incoming_keys)
    near_values.append(new_values)
    nearby_positions.append(stretch_pos)
    near_valid.append(jnp.ones((query_count,), dtype=bool))
    half_keys = CMP_STRIDE * key_width
    half_values = CMP_STRIDE * value_width
    lead_keys = jnp.concatenate([edge_keys, cache_keys[: cache_count - CMP_STRIDE]]).reshape(
        -1, half_keys
    )
    lead_values = jnp.concatenate([edge_values, cache_values[: cache_count - CMP_STRIDE]]).reshape(
        -1, half_values
    )
    comp_keys = (
        jnp.dot(lead_keys, weight_keys[:half_keys], preferred_element_type=jnp.float32)
        + jnp.dot(
            cache_keys.reshape(-1, half_keys),
            weight_keys[half_keys:],
            preferred_element_type=jnp.float32,
        )
    ).astype(jnp.bfloat16)
    comp_values = (
        jnp.dot(lead_values, weight_values[:half_values], preferred_element_type=jnp.float32)
        + jnp.dot(
            cache_values.reshape(-1, half_values),
            weight_values[half_values:],
            preferred_element_type=jnp.float32,
        )
    ).astype(jnp.bfloat16)
    start = jnp.int32(0)
    top = jnp.full((row_total,), MASKED, jnp.float32)
    total = jnp.zeros((row_total,), jnp.float32)
    summed = jnp.zeros((row_total, value_width), jnp.float32)
    keys = lax.all_gather(comp_keys, "seq", axis=0, tiled=True)
    values = lax.all_gather(comp_values, "seq", axis=0, tiled=True)
    length = keys.shape[0]
    block = length
    for size in (1024, 512, 256, 128):
        if length % size == 0:
            block = size
            break
    for index in range(length // block):
        key_block = keys[index * block : (index + 1) * block]
        value_block = values[index * block : (index + 1) * block]
        scores = (
            jnp.einsum("rd,kd->rk", rows, key_block, preferred_element_type=jnp.float32) * scale
        )
        key_at = start + index * block + jnp.arange(block, dtype=jnp.int32)
        scores = jnp.where(key_at[None, :] > 0, scores, MASKED)
        newtop = jnp.maximum(top, jnp.max(scores, axis=1))
        factor = jnp.exp(top - newtop)
        weights = jnp.exp(scores - newtop[:, None])
        total = total * factor + jnp.sum(weights, axis=1)
        summed = summed * factor[:, None] + jnp.dot(
            weights.astype(jnp.bfloat16), value_block, preferred_element_type=jnp.float32
        )
        top = newtop
    top, total, summed = (top, total, summed)
    compressed_out = summed / total[:, None]
    chosen = select_blocks.reshape(-1)
    shard_blocks = cache_count // SEL_BLOCK
    capacity = max(2, 2 * chosen.shape[0] // ranks)
    owner = chosen // shard_blocks
    local = chosen - owner * shard_blocks
    count = chosen.shape[0]
    order = jnp.arange(count, dtype=jnp.int32)
    same = owner[:, None] == owner[None, :]
    position = jnp.sum((same & (order[None, :] < order[:, None])).astype(jnp.int32), axis=1)
    where_at = owner * capacity + position
    slots = jnp.arange(ranks * capacity, dtype=jnp.int32)
    wanted = where_at[:, None] == slots[None, :]
    request = jnp.sum(jnp.where(wanted, local[:, None], 0), axis=0).reshape(ranks, capacity)
    asked = lax.all_to_all(request, "seq", split_axis=0, concat_axis=0, tiled=True)
    tile_count = select_blocks.shape[0]

    def picked(hot, table):
        return jnp.dot(
            hot.astype(jnp.bfloat16), table, preferred_element_type=jnp.float32
        ).astype(jnp.bfloat16)

    asked_hot = asked.reshape(-1, 1) == jnp.arange(shard_blocks, dtype=jnp.int32)[None, :]

    def fetched(table):
        sent = picked(asked_hot, table.reshape(shard_blocks, -1)).reshape(ranks, capacity, -1)
        got = lax.all_to_all(sent, "seq", split_axis=0, concat_axis=0, tiled=True)
        return picked(wanted, got.reshape(ranks * capacity, -1))

    gathered_keys = fetched(cache_keys)
    picked_values = fetched(cache_values)
    gathered_keys, picked_values = (
        gathered_keys.reshape(tile_count, -1, key_width),
        picked_values.reshape(tile_count, -1, value_width),
    )
    tile_count = gathered_keys.shape[0]
    tile_row_count = rows.reshape(tile_count, -1, key_width)
    tile_scores = (
        jnp.einsum(
            "izu,ixu->izx", tile_row_count, gathered_keys, preferred_element_type=jnp.float32
        )
        * scale
    )
    selected_out = finish_rows(tile_scores, picked_values).reshape(row_total, value_width)
    context_keys = jnp.concatenate(near_keys)
    context_values = jnp.concatenate(near_values)
    context_positions = jnp.concatenate(nearby_positions)
    context_valid = jnp.concatenate(near_valid)
    sliding_scores = (
        jnp.einsum("rd,kd->rk", rows, context_keys, preferred_element_type=jnp.float32) * scale
    )
    allowed = (
        context_valid[None, :]
        & (context_positions[None, :] <= stretch_pos[:, None])
        & (context_positions[None, :] > stretch_pos[:, None] - WINDOW)
    )
    sliding_scores = jnp.where(
        allowed[:, None, :], sliding_scores.reshape(query_count, heads, -1), MASKED
    )
    window_out = finish_rows(sliding_scores.reshape(row_total, -1), context_values)
    logits = jnp.einsum(
        "thd,hdb->thb",
        queries.reshape(query_count, heads, key_width),
        gate_weight,
        preferred_element_type=jnp.float32,
    )
    gates = jax.nn.sigmoid(logits)
    mixed = (
        gates[:, :, 0:1] * compressed_out.reshape(query_count, heads, value_width)
        + gates[:, :, 1:2] * selected_out.reshape(query_count, heads, value_width)
        + gates[:, :, 2:3] * window_out.reshape(query_count, heads, value_width)
    )
    return mixed.astype(jnp.bfloat16).reshape(query_count, heads * value_width)


CORES = 2
CHIPS, GROUPS = 4, 4
PIECES = 8
LOG2E = 1.4426950408889634
MESH = pl.DeviceIdType.MESH
FAR, NEAR, ACROSS = range(3)
OWN_INNER, NEAR_INNER, TAIL_OUTER, OWN_MATE, NEAR_MATE, ACROSS_MATE, FAR_MATE = range(7)


def fused_kernel(
    n_seq,
    n_kv,
    tiles,
    sel,
    sel_out,
    q,
    ckt,
    cv,
    ikt,
    iv,
    wkt,
    wv,
    gw,
    out,
    q_vm,
    q_far,
    sel_vm,
    sel_far,
    ckt_vm,
    ikt_vm,
    gw_vm,
    kv,
    new,
    edge_own,
    edge_in,
    lhs_k,
    lhs_v,
    wk_all,
    wv_all,
    comp_vm,
    comp_all,
    compk,
    compv,
    rows_vm,
    rows_far,
    gates_vm,
    acc,
    part_out,
    part_in,
    out_vm,
    win_k,
    win_v,
    sel_k,
    sel_v,
    local_sem,
    own_sem,
    sel_sem,
    out_sem,
    kv_send,
    kv_recv,
    kv_mate,
    new_send,
    new_recv,
    q_send,
    q_recv,
    far_send,
    far_recv,
    part_send,
    part_recv,
    w_send,
    w_recv,
    w_mate,
    comp_send,
    comp_recv,
):
    me = lax.axis_index("seq")
    group = lax.axis_index("kv")
    z = me // CORES
    core = lax.rem(me, CORES)
    chips = n_seq // CORES
    mate = z * CORES + 1 - core
    half_line = z // (chips // 2)
    step = CORES - 2 * CORES * half_line
    inner = me + step
    outer = lax.rem(me - step + n_seq, n_seq)
    middle = (z > 0) & (z < chips - 1)
    at_end = jnp.logical_not(middle)
    right = lax.rem(me + CORES, n_seq)
    width, cache = ckt.shape
    fresh = ikt.shape[1]
    vw = cv.shape[2]
    low = width - vw
    wide = rows_vm.shape[1]
    per = cache // SEL_BLOCK
    size = per // PIECES
    new_per = fresh // SEL_BLOCK
    half_block = SEL_BLOCK // 2
    heads = q.shape[1] // width
    tile = fresh // tiles
    picks = sel.shape[1]
    count = heads * tile
    lookback = WINDOW // fresh
    hops = -(-lookback // CORES)
    chunks = cache // CMP_STRIDE
    pad = chunks + CMP_STRIDE
    factor = width**-0.5 * LOG2E
    tail_pieces = range(PIECES - WINDOW // SEL_BLOCK // size, PIECES)[::-1]
    all_pieces = range(PIECES)[::-1]

    across = inner
    near = (n_seq - CORES) * half_line + core
    far = (n_seq - CORES) * (1 - half_line) + core
    last = n_seq - 1
    takes_tail = (z == 0) & (core == CORES - 1)
    gives_tail = (z == 1) & (core == CORES - 1)
    wants_tail = (z == 0) & (core == 0)

    flip = group + 1 - 2 * lax.rem(group, 2)
    turn = lax.rem(group + n_kv // 2, n_kv)
    beside = (flip + core * (turn - flip), turn + core * (flip - turn))
    opposite = n_kv - 1 - group

    barrier = pltpu.get_barrier_semaphore()
    for to, when in (
        (me + CORES, z < chips - 1),
        (me - CORES, z > 0),
        (me + 1, (core == CORES - 1) & (z < chips - 1)),
        (me - 1, (core == 0) & (z > 0)),
    ):

        @pl.when(when)
        def _():
            pl.semaphore_signal(barrier, inc=1, device_id={"seq": to}, device_id_type=MESH)

    pl.semaphore_signal(barrier, inc=1, device_id={"seq": mate}, device_id_type=MESH)
    for to in beside:
        pl.semaphore_signal(barrier, inc=1, device_id={"kv": to}, device_id_type=MESH)

    half_k = wkt.shape[1] // CORES
    half_v = wv.shape[0] // CORES
    value_rows = pl.ds(SEL_BLOCK, SEL_BLOCK)
    loads = []
    for half in range(CORES):
        loads.append((wkt.at[:, pl.ds(half * half_k, half_k)], wk_all.at[group, half]))
        loads.append((wv.at[pl.ds(half * half_v, half_v)], wv_all.at[group, half]))
    held_weights = len(loads)
    loads += [
        (ikt, ikt_vm),
        (iv, new.at[pl.ds(me * new_per, new_per), value_rows]),
        (ckt, ckt_vm),
        (q, q_vm),
        (gw, gw_vm),
    ]
    load_copies = [pltpu.make_async_copy(a, b, local_sem.at[n]) for n, (a, b) in enumerate(loads)]
    for copy in load_copies:
        copy.start()

    own_at = pl.multiple_of(me * per, per)
    own_values = pltpu.make_async_copy(
        cv, kv.at[pl.ds(own_at, per), value_rows], local_sem.at[len(loads)]
    )
    own_values.start()

    def remote(src, dst, send, recv, to, axis="seq"):
        return pltpu.make_async_remote_copy(
            src_ref=src,
            dst_ref=dst,
            send_sem=send,
            recv_sem=recv,
            device_id={axis: to},
            device_id_type=MESH,
        )

    def blocks(slot, piece, pieces=1):
        return kv.at[pl.ds(pl.multiple_of(slot * per + piece * size, size), pieces * size)]

    def kv_msg(slot, piece, send, recv, to, pieces=1):
        ref = blocks(slot, piece, pieces)
        return remote(ref, ref, kv_send.at[send], recv, to)

    def kv_taken(slot, recv, piece=0, pieces=PIECES):
        kv_msg(slot, piece, 0, recv, mate, pieces).wait_recv()

    def new_msg(slot, send, recv, to):
        ref = new.at[pl.ds(slot * new_per, new_per)]
        return remote(ref, ref, new_send.at[send], new_recv.at[recv], to)

    def new_taken(slot, recv):
        new_msg(slot, 0, recv, mate).wait_recv()

    def new_sent(send):
        new_msg(me, send, 0, mate).wait_send()

    def q_msg(t):
        ref = pl.ds(t * tile, tile)
        return remote(q.at[ref], q_far.at[ref], q_send, q_recv.at[t], inner)

    def sel_msg():
        return remote(sel_out, sel_vm, far_send.at[0], far_recv.at[0], inner)

    def edge_msg():
        return remote(
            edge_own, edge_in, far_send.at[1], far_recv.at[1], lax.rem(me + 1, n_seq)
        )

    def part_msg(t):
        return remote(part_out.at[t], part_in.at[t], part_send, part_recv.at[t], outer)

    w_all = (wk_all, wv_all)
    origins = (*beside, opposite)

    def w_msg(n, part):
        return remote(
            w_all[part].at[group, core],
            w_all[part].at[group, core],
            w_send.at[part],
            w_recv.at[n, part],
            beside[n],
            "kv",
        )

    def w_onward(part):
        ref = w_all[part].at[beside[0], core]
        return remote(ref, ref, w_send.at[part], w_recv.at[2, part], beside[1], "kv")

    def w_pass(n, part):
        ref = w_all[part].at[origins[n], core]
        return remote(ref, ref, w_send.at[2 + part], w_mate.at[part], mate)

    def w_taken(n, part):
        ref = w_all[part].at[origins[n], core]
        remote(ref, ref, w_send.at[part], w_recv.at[n, part], mate).wait_recv()

    def w_all_but_own(part, send):
        ref = w_all[part].at[pl.ds(0, n_kv - 1), 0]
        return remote(ref, ref, w_send.at[send], w_mate.at[part], mate)


    @pl.when(middle)
    def _():
        pl.semaphore_wait(barrier, 6)

    @pl.when(at_end)
    def _():
        pl.semaphore_wait(barrier, 4 + (1 - half_line) * core + half_line * (1 - core))

    @pl.when(at_end)
    def _():
        sel_msg().start()

    for copy in load_copies[:held_weights]:
        copy.wait()
    for part in range(2):
        for n in range(2):
            w_msg(n, part).start()

    def pack(keys, blocks, held, at):
        held[pl.ds(at, blocks), 0:SEL_BLOCK] = keys[:, 0:vw].reshape(blocks, SEL_BLOCK, vw)
        part = keys[:, vw:width].reshape(blocks, 2, half_block, low)
        held[pl.ds(at, blocks), 2 * SEL_BLOCK :] = jnp.concatenate(
            [part[:, 0], part[:, 1]], axis=-1
        )

    for copy in load_copies[held_weights : held_weights + 3]:
        copy.wait()
    pack(ikt_vm[...].T, new_per, new, me * new_per)

    up = z < chips - 1

    @pl.when(up)
    def _():
        new_msg(me, 0, 0, right).start()

    keys = ckt_vm[...].T
    pack(keys, per, kv, own_at)
    own_values.wait()

    none = jnp.zeros((CMP_STRIDE, wide - width), jnp.bfloat16)
    edge_own[:, 0:wide] = jnp.concatenate([keys[cache - CMP_STRIDE :], none], axis=-1)
    edge_own[:, wide:] = kv[own_at + per - 1, 2 * SEL_BLOCK - CMP_STRIDE : 2 * SEL_BLOCK]
    has_next = me < n_seq - 1

    @pl.when(has_next)
    def _():
        edge_msg().start()

    @pl.when(at_end)
    def _():
        for piece in all_pieces:
            kv_msg(me, piece, OWN_INNER, kv_recv.at[NEAR, piece], inner).start()
        q_msg(0).start()

    @pl.when(middle)
    def _():
        for piece in all_pieces:
            kv_msg(me, piece, OWN_INNER, kv_recv.at[ACROSS, piece], inner).start()
        for piece in all_pieces:
            kv_msg(me, piece, OWN_MATE, kv_mate.at[0], mate).start()

    new_msg(me, 2, 2, mate).start()
    for copy in load_copies[held_weights + 3 :]:
        copy.wait()

    lane = lax.broadcasted_iota(jnp.int32, (tile, wide - width), 1)
    one = jnp.where(lane == 0, 1.0, 0.0).astype(jnp.bfloat16)

    for held in (compv, win_v, sel_v):
        held[:, vw:] = jnp.ones((held.shape[0], vw), jnp.bfloat16)

    def split_heads(src, t, dst, at):
        part = src[pl.ds(pl.multiple_of(t * tile, tile), tile), :]
        for h in range(heads):
            dst[pl.ds(at + h * tile, tile), :] = jnp.concatenate(
                [part[:, h * width : (h + 1) * width], one], axis=-1
            )

    @pl.loop(0, tiles)
    def _(t):
        split_heads(q_vm, t, rows_vm, pl.multiple_of(t * count, count))

    logits = lax.dot_general(
        rows_vm[:, 0:width],
        gw_vm[...],
        (((1,), (1,)), ((), ())),
        preferred_element_type=jnp.float32,
    )
    gates_vm[...] = jax.nn.sigmoid(logits)

    def relay_new(d):
        slot = me - CORES * d

        @pl.when(z >= d)
        def _():
            new_taken(slot, d - 1)
            new_msg(slot, 2 + d, 2 + d, mate).start()

    def raise_new(at):
        @pl.when(at)
        def _():
            new_msg(me - CORES, 1, 1, right).start()

    def relay_across(pieces):
        @pl.when(middle)
        def _():
            for piece in pieces:
                kv_taken(across, kv_recv.at[ACROSS, piece], piece, 1)
                kv_msg(across, piece, ACROSS_MATE, kv_mate.at[1], mate).start()

    def relay_near(pieces):
        @pl.when(middle)
        def _():
            for piece in pieces:
                kv_taken(near, kv_recv.at[NEAR, piece], piece, 1)
                kv_msg(near, piece, NEAR_INNER, kv_recv.at[FAR, piece], inner).start()
                kv_msg(near, piece, NEAR_MATE, kv_mate.at[2], mate).start()

    def relay_far(pieces):
        @pl.when(middle)
        def _():
            for piece in pieces:
                kv_taken(far, kv_recv.at[FAR, piece], piece, 1)
                sem = kv_mate.at[3 if piece in tail_pieces else 4]
                kv_msg(far, piece, FAR_MATE, sem, mate).start()
                if piece in tail_pieces:

                    @pl.when(gives_tail)
                    def _():
                        kv_msg(
                            last, piece, TAIL_OUTER, kv_recv.at[FAR, piece], outer
                        ).start()

    def take_tail():
        @pl.when(takes_tail)
        def _():
            for piece in tail_pieces:
                kv_taken(last, kv_recv.at[FAR, piece], piece, 1)
                kv_msg(last, piece, FAR_MATE, kv_mate.at[3], mate).start()

        @pl.when(wants_tail)
        def _():
            kv_taken(last, kv_mate.at[3], tail_pieces[-1], len(tail_pieces))

    def comp_msg(slot, send, recv, to):
        ref = comp_all.at[slot]
        src = comp_vm if slot is me else ref
        return remote(src, ref, comp_send.at[send], comp_recv.at[recv], to)

    def comp_some(slots, send):
        ref = comp_all.at[pl.ds(0, slots)]
        return remote(ref, ref, comp_send.at[send], comp_recv.at[3], mate)

    def comp_relay(n, to=None, recv=0):
        @pl.when(middle)
        def _():
            slot = (outer, inner, far)[n]
            comp_msg(slot, 0, n, mate).wait_recv()
            if to is not None:
                comp_msg(slot, 1, recv, to).start()
            comp_msg(slot, 0, 3, mate).start()

    comp_keep = pltpu.make_async_copy(comp_vm, comp_all.at[me], own_sem)

    group_rows = CMP_STRIDE * CMP_STRIDE

    def spread_tokens():
        row = lax.broadcasted_iota(jnp.int32, (group_rows, group_rows), 0)
        token = lax.broadcasted_iota(jnp.int32, (group_rows, group_rows), 1)
        want = lax.rem(row, CMP_STRIDE) * CMP_STRIDE + row // CMP_STRIDE
        perm = jnp.where(token == want, 1.0, 0.0).astype(jnp.bfloat16)

        def lay(lhs, at, spread, each):
            spread = spread.astype(jnp.bfloat16)
            for p in range(CMP_STRIDE):
                lhs[at : at + CMP_STRIDE, p * each : (p + 1) * each] = spread[
                    p * CMP_STRIDE : (p + 1) * CMP_STRIDE
                ]

        for n in range(cache // group_rows):
            some = group_rows // SEL_BLOCK
            v = kv[pl.ds(own_at + n * some, some), SEL_BLOCK : 2 * SEL_BLOCK]
            v = v.reshape(group_rows, vw)
            lay(lhs_v, n * CMP_STRIDE, jnp.dot(perm, v, preferred_element_type=jnp.float32), vw)

        for n in range(cache // group_rows):
            spread = lax.dot_general(
                perm,
                ckt_vm[:, n * group_rows : (n + 1) * group_rows],
                (((1,), (1,)), ((), ())),
                preferred_element_type=jnp.float32,
            )
            lay(lhs_k, n * CMP_STRIDE, spread, width)

        @pl.when(me == 0)
        def _():
            edge_in[...] = jnp.zeros(edge_in.shape, jnp.bfloat16)

        @pl.when(me > 0)
        def _():
            edge_msg().wait_recv()

        row = lax.broadcasted_iota(jnp.int32, (group_rows, CMP_STRIDE), 0)
        token = lax.broadcasted_iota(jnp.int32, (group_rows, CMP_STRIDE), 1)
        want = (token == row // CMP_STRIDE) & (lax.rem(row, CMP_STRIDE) == CMP_STRIDE - 1)
        lead = jnp.where(want, 1.0, 0.0).astype(jnp.bfloat16)
        spread = jnp.dot(lead, edge_in[...], preferred_element_type=jnp.float32)
        lay(lhs_k, chunks, spread[:, 0:width], width)
        lay(lhs_v, chunks, spread[:, wide:], vw)

    def relay_weights():
        for part in range(2):
            w_taken(0, part)
            w_onward(part).start()
            w_pass(0, part).start()
        for part in range(2):
            w_taken(1, part)
            w_pass(1, part).start()

    def pass_weights():
        for part in range(2):
            w_taken(2, part)
            w_pass(2, part).start()

    def compress():
        for part in range(2):
            w_all_but_own(part, part).wait_recv()
        results = []
        for lhs, w, dims in (
            (lhs_k, wk_all, (((1,), (1,)), ((), ()))),
            (lhs_v, wv_all, (((1,), (0,)), ((), ()))),
        ):
            pieces = n_kv * CORES // 2
            depth = lhs.shape[1] // pieces
            sums = []
            for side in range(2):
                total = None
                for n in range(pieces):
                    at = side * pieces + n
                    term = lax.dot_general(
                        lhs[:, n * depth : (n + 1) * depth],
                        w[at // CORES, at % CORES],
                        dims,
                        preferred_element_type=jnp.float32,
                    )
                    total = term if total is None else total + term
                sums.append(total)
            lead = jnp.concatenate([sums[0][pad - 1 : pad], sums[0][0 : chunks - 1]], axis=0)
            results.append((lead + sums[1][0:chunks]).astype(jnp.bfloat16))
        made, made_v = results
        comp_vm[0:chunks, :] = made[:, 0:vw]
        comp_vm[chunks : 2 * chunks, :] = made_v
        comp_vm[2 * chunks :, :] = jnp.concatenate(
            [made[0 : chunks // 2, vw:width], made[chunks // 2 :, vw:width]], axis=-1
        )
        @pl.when(middle)
        def _():
            comp_msg(me, 1, 1, inner).start()
            comp_msg(me, 1, 0, outer).start()

        @pl.when(at_end)
        def _():
            comp_msg(me, 1, 0, inner).start()

        comp_msg(me, 0, 3, mate).start()
        comp_keep.start()

    def attend(rows, keys, values, mask):
        half = rows.shape[0] // 2
        done = []
        for n in range(2):
            s = lax.dot_general(
                rows[n * half : (n + 1) * half],
                keys,
                (((1,), (1,)), ((), ())),
                preferred_element_type=jnp.float32,
            )
            if mask is not None:
                s = mask(s)
            top = jnp.max(s, axis=-1, keepdims=True)
            w = jnp.exp2((s - top) * factor).astype(jnp.bfloat16)
            o = jnp.dot(w, values, preferred_element_type=jnp.float32)
            done.append(o[:, 0:vw] / o[:, vw:])
        return jnp.concatenate(done, axis=0)

    def gated(branch, t, o, emit):
        g = gates_vm[pl.ds(pl.multiple_of(t * count, count), count), :]
        for h in range(heads):
            a = slice(h * tile, (h + 1) * tile)
            at = branch * heads + h
            emit(h, pl.ds(pl.multiple_of(t * count + h * tile, tile), tile), g[a, at : at + 1] * o[a])

    def rows_of(t):
        return rows_vm[pl.ds(pl.multiple_of(t * count, count), count), :]

    def bias_lanes(rows, value):
        lane = lax.broadcasted_iota(jnp.int32, (rows, wide - width), 1)
        return jnp.where(lane == 0, value, 0.0).astype(jnp.bfloat16)

    def compressed():
        comp_keep.wait()

        @pl.when(at_end)
        def _():
            for n in range(chips - 1):
                slot = me + step * (n + 1)
                comp_msg(slot, 0, n, mate).wait_recv()
                comp_msg(slot, 0, 3, mate).start()

        comp_some(chips, 0).wait_recv()
        total = n_seq * chunks
        first = lax.broadcasted_iota(jnp.int32, (total, wide - width), 0) == 0
        compk[:, width:wide] = bias_lanes(total, jnp.where(first, MASKED, 0.0))
        for slot in range(n_seq):
            at, mid = slot * chunks, slot * chunks + chunks // 2
            compk[at : at + chunks, 0:vw] = comp_all[slot, 0:chunks]
            compk[at:mid, vw:width] = comp_all[slot, 2 * chunks :, 0:low]
            compk[mid : at + chunks, vw:width] = comp_all[slot, 2 * chunks :, low : 2 * low]
            compv[at : at + chunks, 0:vw] = comp_all[slot, chunks : 2 * chunks]

        @pl.loop(0, tiles)
        def _(t):
            o = attend(rows_of(t), compk[...], compv[...], None)

            def emit(h, at, x):
                acc[at, :] += x

            gated(0, t, o, emit)

    def put(dk, dv, at, block, bias):
        rest = block[2 * SEL_BLOCK :]
        rest = jnp.concatenate([rest[:, 0:low], rest[:, low : 2 * low]], axis=0)
        dk[pl.ds(at, SEL_BLOCK), 0:vw] = block[0:SEL_BLOCK]
        dk[pl.ds(at, SEL_BLOCK), vw:wide] = jnp.concatenate([rest, bias], axis=-1)
        dv[pl.ds(at, SEL_BLOCK), 0:vw] = block[SEL_BLOCK : 2 * SEL_BLOCK]

    def window():
        relay_new(hops)
        for d in range(hops + 1):

            @pl.when(z >= d)
            def _():
                new_taken((z - d) * CORES + 1 - core, 2 + d)

        none = bias_lanes(SEL_BLOCK, 0.0)
        for i in range(lookback + 1):
            chunk = me + i
            for b in range(new_per):
                at = (i * new_per + b) * SEL_BLOCK

                @pl.when(chunk < lookback)
                def _():
                    block = n_seq * per - lookback * new_per + chunk * new_per + b
                    put(win_k, win_v, at, kv[block], none)

                @pl.when(chunk >= lookback)
                def _():
                    put(win_k, win_v, at, new[(chunk - lookback) * new_per + b], none)

        span = WINDOW + tile

        def edges(first, last):
            diff = lax.broadcasted_iota(jnp.int32, (count // 2, last - first), 1) + first
            diff = diff - lax.rem(lax.broadcasted_iota(jnp.int32, diff.shape, 0), tile)
            return (diff > 0) & (diff <= WINDOW)

        head_ok, tail_ok = edges(0, vw), edges(WINDOW, span)

        def mask(s):
            return jnp.concatenate(
                [
                    jnp.where(head_ok, s[:, 0:vw], MASKED),
                    s[:, vw:WINDOW],
                    jnp.where(tail_ok, s[:, WINDOW:span], MASKED),
                ],
                axis=-1,
            )

        @pl.loop(0, tiles)
        def _(t):
            off = pl.multiple_of(t * tile, tile)
            o = attend(rows_of(t), win_k[pl.ds(off, span), :], win_v[pl.ds(off, span), :], mask)

            def emit(h, at, x):
                acc[at, :] = x

            gated(2, t, o, emit)

    def pick(chosen, t):
        none = bias_lanes(SEL_BLOCK, 0.0)
        for n in range(picks):
            put(sel_k, sel_v, n * SEL_BLOCK, kv[chosen[t, n]], none)

    def exported():
        @pl.loop(0, tiles)
        def _(t):
            q_msg(t).wait_recv()
            split_heads(q_far, t, rows_far, 0)
            pick(sel_far, t)
            o = attend(rows_far[...], sel_k[...], sel_v[...], None)
            part_out[t] = o.astype(jnp.bfloat16)
            part_msg(t).start()

    def finish(t, o):
        to = pl.ds(pl.multiple_of(t * tile, tile), tile)

        def emit(h, at, x):
            out_vm[to, h * vw : (h + 1) * vw] = (acc[at, :] + x).astype(out.dtype)

        gated(1, t, o, emit)
        pltpu.make_async_copy(out_vm.at[to], out.at[to], out_sem).start()

    relay_new(1)
    raise_new(middle)
    spread_tokens()
    for piece in all_pieces[:4]:
        relay_across((piece,))
        relay_near((piece,))
    relay_weights()
    relay_across(all_pieces[4:])
    pass_weights()
    compress()

    @pl.when(at_end)
    def _():
        for t in range(1, tiles):
            q_msg(t).start()

    relay_near(all_pieces[4:6])
    comp_relay(0, inner, 2)
    relay_near(all_pieces[6:])
    relay_far(tail_pieces)
    take_tail()
    rest = tail_pieces[-1]

    @pl.when(middle)
    def _():
        kv_taken(far + 1 - 2 * core, kv_mate.at[3], rest, PIECES - rest)

    window()
    comp_relay(1, outer, 1)
    comp_relay(2, outer, 2)
    relay_far(range(rest)[::-1])
    compressed()

    @pl.when(middle)
    def _():
        sel_msg().wait_recv()
        copy = pltpu.make_async_copy(sel_vm, sel_far, sel_sem)
        copy.start()
        copy.wait()
        kv_taken(mate, kv_mate.at[0])
        kv_taken(across + 1 - 2 * core, kv_mate.at[1])
        kv_taken(near + 1 - 2 * core, kv_mate.at[2])
        kv_taken(far + 1 - 2 * core, kv_mate.at[4], 0, rest)
        exported()

    @pl.when(middle)
    def _():
        @pl.loop(0, tiles)
        def _(t):
            pick(sel, t)
            finish(t, attend(rows_of(t), sel_k[...], sel_v[...], None))

        remote(part_out, part_in, part_send, part_recv.at[0], outer).wait_send()
        for send in (OWN_INNER, NEAR_INNER, OWN_MATE, NEAR_MATE, ACROSS_MATE, FAR_MATE):
            kv_msg(me, 0, send, kv_mate.at[0], mate, PIECES).wait_send()

    @pl.when(gives_tail)
    def _():
        kv_msg(me, 0, TAIL_OUTER, kv_mate.at[0], mate, len(tail_pieces)).wait_send()

    @pl.when(at_end)
    def _():
        @pl.loop(0, tiles)
        def _(t):
            part_msg(t).wait_recv()
            finish(t, part_in[t].astype(jnp.float32))

        kv_msg(me, 0, OWN_INNER, kv_mate.at[0], mate, PIECES).wait_send()
        sel_msg().wait_send()
        remote(q_vm, q_far, q_send, q_recv.at[0], inner).wait_send()

    @pl.when(takes_tail)
    def _():
        kv_msg(me, 0, FAR_MATE, kv_mate.at[0], mate, len(tail_pieces)).wait_send()

    @pl.when(has_next)
    def _():
        edge_msg().wait_send()

    @pl.when(up)
    def _():
        new_sent(0)

    @pl.when(up & (z > 0))
    def _():
        new_sent(1)

    new_sent(2)
    for d in range(1, hops + 1):

        @pl.when(z >= d)
        def _():
            new_sent(2 + d)

    for part in range(2):
        w_all_but_own(part, part).wait_send()
        w_all_but_own(part, 2 + part).wait_send()
    comp_some(chips, 0).wait_send()

    @pl.when(middle)
    def _():
        comp_some(chips + 1, 1).wait_send()

    @pl.when(at_end)
    def _():
        comp_some(1, 1).wait_send()

    pltpu.make_async_copy(out_vm, out, out_sem).wait()


def shards_gathered(q, ck, cv, ik, iv, wk, wv, sel, gw):
    n_seq, n_kv = lax.axis_size("seq"), lax.axis_size("kv")
    heads, width, branches = gw.shape
    vw = cv.shape[1]
    cache, fresh = ck.shape[0], ik.shape[0]
    tiles, picks = sel.shape[0], sel.shape[-1]
    chunks = cache // CMP_STRIDE
    pad = chunks + CMP_STRIDE
    per, new_per = cache // SEL_BLOCK, fresh // SEL_BLOCK
    tile_rows = heads * fresh
    count = tile_rows // tiles
    wide = -(-width // 128) * 128
    block_rows = 2 * SEL_BLOCK + SEL_BLOCK // 2
    bf = jnp.bfloat16
    any_spec = pl.BlockSpec(memory_space=pl.ANY)
    half_k, half_v = wk.shape[0] // CORES, wv.shape[0] // CORES

    def held(*shape):
        return pltpu.VMEM(shape, bf)

    dma = pltpu.SemaphoreType.DMA
    picked = sel.reshape(tiles, picks)
    return pl.pallas_call(
        functools.partial(fused_kernel, n_seq, n_kv, tiles),
        out_shape=jax.ShapeDtypeStruct((fresh, heads * vw), bf),
        in_specs=[
            pl.BlockSpec(memory_space=pltpu.SMEM),
            pl.BlockSpec(memory_space=pltpu.VMEM),
        ]
        + [any_spec] * 8,
        out_specs=any_spec,
        scratch_shapes=[
            held(*q.shape),
            held(*q.shape),
            pltpu.VMEM((tiles, picks), jnp.int32),
            pltpu.SMEM((tiles, picks), jnp.int32),
            held(width, cache),
            held(width, fresh),
            held(heads * branches, width),
            held(n_seq * per, block_rows, vw),
            held(n_seq * new_per, block_rows, vw),
            held(CMP_STRIDE, wide + vw),
            held(CMP_STRIDE, wide + vw),
            held(pad, CMP_STRIDE * width),
            held(pad, CMP_STRIDE * vw),
            held(n_kv, CORES, width, half_k),
            held(n_kv, CORES, half_v, vw),
            held(2 * chunks + chunks // 2, vw),
            held(n_seq, 2 * chunks + chunks // 2, vw),
            held(n_seq * chunks, wide),
            held(n_seq * chunks, 2 * vw),
            held(tile_rows, wide),
            held(count, wide),
            pltpu.VMEM((tile_rows, heads * branches), jnp.float32),
            pltpu.VMEM((tile_rows, vw), jnp.float32),
            held(tiles, count, vw),
            held(tiles, count, vw),
            held(fresh, heads * vw),
            held(fresh + WINDOW, wide),
            held(fresh + WINDOW, 2 * vw),
            held(picks * SEL_BLOCK, wide),
            held(picks * SEL_BLOCK, 2 * vw),
            dma((6 + 2 * CORES,)),
            dma,
            dma,
            dma,
            dma((7,)),
            dma((3, PIECES)),
            dma((5,)),
            dma((3 + -(-WINDOW // (fresh * CORES)),)),
            dma((3 + -(-WINDOW // (fresh * CORES)),)),
            dma,
            dma((tiles,)),
            dma((2,)),
            dma((2,)),
            dma,
            dma((tiles,)),
            dma((4,)),
            dma((3, 2)),
            dma((2,)),
            dma((2,)),
            dma((4,)),
        ],
        compiler_params=pltpu.CompilerParams(
            collective_id=0, has_side_effects=True, vmem_limit_bytes=60 << 20
        ),
    )(
        picked,
        picked,
        q,
        ck.T,
        cv.reshape(per, SEL_BLOCK, vw),
        ik.T,
        iv.reshape(new_per, SEL_BLOCK, vw),
        wk.T,
        wv,
        jnp.transpose(gw, (2, 0, 1)).reshape(heads * branches, width),
    )


GATHER_BYTES = 1 << 24


def shards(queries, cache_keys, cache_values, *rest):
    ranks = lax.axis_size("seq")
    size = ranks * 2 * (cache_keys.size + cache_values.size)
    fits = size <= GATHER_BYTES and ranks == CORES * CHIPS and lax.axis_size("kv") == GROUPS
    form = shards_gathered if fits else shards_by_request
    return form(queries, cache_keys, cache_values, *rest)


def solution(mesh):
    placed = (
        P("seq", "kv"),
        P("seq", "kv"),
        P("seq", "kv"),
        P("seq", "kv"),
        P("seq", "kv"),
        P("kv", None),
        P("kv", None),
        P("seq", "kv", None),
        P("kv", None, None),
    )
    return jax.shard_map(
        shards, mesh=mesh, in_specs=placed, out_specs=P("seq", "kv"), check_vma=False
    )
```

```python
import functools

import jax
import jax.numpy as jnp
from jax import lax
from jax.experimental import pallas as pl
from jax.experimental.pallas import tpu as pltpu
from jax.sharding import PartitionSpec as P

CMP_STRIDE = 16
SEL_BLOCK = 64
WINDOW = 512


MASKED = -1e30


def passed_along(block, axis, distance):
    devices = range(lax.axis_size(axis))
    route = [((i - distance) % len(devices), i) for i in devices]
    return lax.ppermute(block, axis, route)


def from_behind(x, axis, by):
    peers = lax.axis_size(axis)
    pairs = [(i, i + by) for i in range(peers) if 0 <= i + by < peers]
    return lax.ppermute(x, axis, pairs)


def pack_rows(keys, values):
    return jnp.concatenate([keys.reshape(-1), values.reshape(-1)])


def unpack_rows(flat, count, key_width, value_width):
    keys = flat[: count * key_width].reshape(count, key_width)
    values = flat[count * key_width : count * (key_width + value_width)].reshape(count, value_width)
    return (keys, values)


def finish_rows(scores, values):
    top = jnp.max(scores, axis=-1, keepdims=True)
    weights = jnp.exp(scores - top)
    total = jnp.sum(weights, axis=-1, keepdims=True)
    mixed = jnp.matmul(weights.astype(jnp.bfloat16), values, preferred_element_type=jnp.float32)
    return mixed / total


def shards_by_request(
    queries,
    cache_keys,
    cache_values,
    incoming_keys,
    new_values,
    comp_key_weight,
    comp_value_weight,
    select_blocks,
    gate_weight,
):
    heads, key_width, _ = gate_weight.shape
    value_width = cache_values.shape[1]
    query_count = queries.shape[0]
    cache_count = cache_keys.shape[0]
    ranks = lax.axis_size("seq")
    place = lax.axis_index("seq")
    scale = key_width ** (-0.5)
    rows = queries.reshape(query_count * heads, key_width)
    row_total = rows.shape[0]
    stretch_pos = place * query_count + jnp.arange(query_count, dtype=jnp.int32)
    lookback_length = -(-WINDOW // query_count)
    weight_keys, weight_values = (
        lax.all_gather(comp_key_weight, "kv", axis=0, tiled=True),
        lax.all_gather(comp_value_weight, "kv", axis=0, tiled=True),
    )
    tail_pack = pack_rows(cache_keys[cache_count - WINDOW :], cache_values[cache_count - WINDOW :])
    moved_tail = passed_along(tail_pack, "seq", 1)
    before_keys, before_values = unpack_rows(moved_tail, WINDOW, key_width, value_width)
    edge_keys = before_keys[WINDOW - CMP_STRIDE :]
    edge_values = before_values[WINDOW - CMP_STRIDE :]
    held_tail = jnp.where(place == 0, moved_tail, jnp.zeros_like(moved_tail))
    tail_size = held_tail.shape[0]
    tail_flat = held_tail
    near_keys = []
    near_values = []
    nearby_positions = []
    near_valid = []
    own = pack_rows(incoming_keys, new_values)
    own_size = own.shape[0]
    for back in range(lookback_length, 0, -1):
        moved = from_behind(jnp.concatenate([own, held_tail]), "seq", back)
        got_keys, got_values = unpack_rows(moved, query_count, key_width, value_width)
        tail_flat = jnp.where(place == back, moved[own_size : own_size + tail_size], tail_flat)
        near_keys.append(got_keys)
        near_values.append(got_values)
        nearby_positions.append(
            (place - back) * query_count + jnp.arange(query_count, dtype=jnp.int32)
        )
        near_valid.append(jnp.broadcast_to(place >= back, (query_count,)))
    tail_keys, tail_values = unpack_rows(tail_flat, WINDOW, key_width, value_width)
    near_keys.append(tail_keys)
    near_values.append(tail_values)
    nearby_positions.append(jnp.arange(WINDOW, dtype=jnp.int32) - WINDOW)
    near_valid.append(jnp.ones((WINDOW,), dtype=bool))
    near_keys.append(incoming_keys)
    near_values.append(new_values)
    nearby_positions.append(stretch_pos)
    near_valid.append(jnp.ones((query_count,), dtype=bool))
    half_keys = CMP_STRIDE * key_width
    half_values = CMP_STRIDE * value_width
    lead_keys = jnp.concatenate([edge_keys, cache_keys[: cache_count - CMP_STRIDE]]).reshape(
        -1, half_keys
    )
    lead_values = jnp.concatenate([edge_values, cache_values[: cache_count - CMP_STRIDE]]).reshape(
        -1, half_values
    )
    comp_keys = (
        jnp.dot(lead_keys, weight_keys[:half_keys], preferred_element_type=jnp.float32)
        + jnp.dot(
            cache_keys.reshape(-1, half_keys),
            weight_keys[half_keys:],
            preferred_element_type=jnp.float32,
        )
    ).astype(jnp.bfloat16)
    comp_values = (
        jnp.dot(lead_values, weight_values[:half_values], preferred_element_type=jnp.float32)
        + jnp.dot(
            cache_values.reshape(-1, half_values),
            weight_values[half_values:],
            preferred_element_type=jnp.float32,
        )
    ).astype(jnp.bfloat16)
    start = jnp.int32(0)
    top = jnp.full((row_total,), MASKED, jnp.float32)
    total = jnp.zeros((row_total,), jnp.float32)
    summed = jnp.zeros((row_total, value_width), jnp.float32)
    keys = lax.all_gather(comp_keys, "seq", axis=0, tiled=True)
    values = lax.all_gather(comp_values, "seq", axis=0, tiled=True)
    length = keys.shape[0]
    block = length
    for size in (1024, 512, 256, 128):
        if length % size == 0:
            block = size
            break
    for index in range(length // block):
        key_block = keys[index * block : (index + 1) * block]
        value_block = values[index * block : (index + 1) * block]
        scores = (
            jnp.einsum("rd,kd->rk", rows, key_block, preferred_element_type=jnp.float32) * scale
        )
        key_at = start + index * block + jnp.arange(block, dtype=jnp.int32)
        scores = jnp.where(key_at[None, :] > 0, scores, MASKED)
        newtop = jnp.maximum(top, jnp.max(scores, axis=1))
        factor = jnp.exp(top - newtop)
        weights = jnp.exp(scores - newtop[:, None])
        total = total * factor + jnp.sum(weights, axis=1)
        summed = summed * factor[:, None] + jnp.dot(
            weights.astype(jnp.bfloat16), value_block, preferred_element_type=jnp.float32
        )
        top = newtop
    top, total, summed = (top, total, summed)
    compressed_out = summed / total[:, None]
    chosen = select_blocks.reshape(-1)
    shard_blocks = cache_count // SEL_BLOCK
    capacity = max(2, 2 * chosen.shape[0] // ranks)
    owner = chosen // shard_blocks
    local = chosen - owner * shard_blocks
    count = chosen.shape[0]
    order = jnp.arange(count, dtype=jnp.int32)
    same = owner[:, None] == owner[None, :]
    position = jnp.sum((same & (order[None, :] < order[:, None])).astype(jnp.int32), axis=1)
    where_at = owner * capacity + position
    slots = jnp.arange(ranks * capacity, dtype=jnp.int32)
    wanted = where_at[:, None] == slots[None, :]
    request = jnp.sum(jnp.where(wanted, local[:, None], 0), axis=0).reshape(ranks, capacity)
    asked = lax.all_to_all(request, "seq", split_axis=0, concat_axis=0, tiled=True)
    tile_count = select_blocks.shape[0]

    def picked(hot, table):
        return jnp.dot(
            hot.astype(jnp.bfloat16), table, preferred_element_type=jnp.float32
        ).astype(jnp.bfloat16)

    asked_hot = asked.reshape(-1, 1) == jnp.arange(shard_blocks, dtype=jnp.int32)[None, :]

    def fetched(table):
        sent = picked(asked_hot, table.reshape(shard_blocks, -1)).reshape(ranks, capacity, -1)
        got = lax.all_to_all(sent, "seq", split_axis=0, concat_axis=0, tiled=True)
        return picked(wanted, got.reshape(ranks * capacity, -1))

    gathered_keys = fetched(cache_keys)
    picked_values = fetched(cache_values)
    gathered_keys, picked_values = (
        gathered_keys.reshape(tile_count, -1, key_width),
        picked_values.reshape(tile_count, -1, value_width),
    )
    tile_count = gathered_keys.shape[0]
    tile_row_count = rows.reshape(tile_count, -1, key_width)
    tile_scores = (
        jnp.einsum(
            "izu,ixu->izx", tile_row_count, gathered_keys, preferred_element_type=jnp.float32
        )
        * scale
    )
    selected_out = finish_rows(tile_scores, picked_values).reshape(row_total, value_width)
    context_keys = jnp.concatenate(near_keys)
    context_values = jnp.concatenate(near_values)
    context_positions = jnp.concatenate(nearby_positions)
    context_valid = jnp.concatenate(near_valid)
    sliding_scores = (
        jnp.einsum("rd,kd->rk", rows, context_keys, preferred_element_type=jnp.float32) * scale
    )
    allowed = (
        context_valid[None, :]
        & (context_positions[None, :] <= stretch_pos[:, None])
        & (context_positions[None, :] > stretch_pos[:, None] - WINDOW)
    )
    sliding_scores = jnp.where(
        allowed[:, None, :], sliding_scores.reshape(query_count, heads, -1), MASKED
    )
    window_out = finish_rows(sliding_scores.reshape(row_total, -1), context_values)
    logits = jnp.einsum(
        "thd,hdb->thb",
        queries.reshape(query_count, heads, key_width),
        gate_weight,
        preferred_element_type=jnp.float32,
    )
    gates = jax.nn.sigmoid(logits)
    mixed = (
        gates[:, :, 0:1] * compressed_out.reshape(query_count, heads, value_width)
        + gates[:, :, 1:2] * selected_out.reshape(query_count, heads, value_width)
        + gates[:, :, 2:3] * window_out.reshape(query_count, heads, value_width)
    )
    return mixed.astype(jnp.bfloat16).reshape(query_count, heads * value_width)


CORES = 2
CHIPS, GROUPS = 4, 4
PIECES = 8
LOG2E = 1.4426950408889634
MESH = pl.DeviceIdType.MESH
FAR, NEAR, ACROSS = range(3)
OWN_INNER, NEAR_INNER, TAIL_OUTER, OWN_MATE, NEAR_MATE, ACROSS_MATE, FAR_MATE = range(7)


def fused_kernel(
    n_seq,
    n_kv,
    tiles,
    sel,
    sel_out,
    q,
    ckt,
    cv,
    ikt,
    iv,
    wkt,
    wv,
    gw,
    out,
    q_vm,
    q_far,
    sel_vm,
    sel_far,
    ckt_vm,
    ikt_vm,
    gw_vm,
    kv,
    new,
    edge_own,
    edge_in,
    lhs_k,
    lhs_v,
    wk_all,
    wv_all,
    comp_vm,
    comp_all,
    compk,
    compv,
    rows_vm,
    rows_far,
    gates_vm,
    acc,
    part_out,
    part_in,
    out_vm,
    win_k,
    win_v,
    sel_k,
    sel_v,
    local_sem,
    own_sem,
    sel_sem,
    out_sem,
    kv_send,
    kv_recv,
    kv_mate,
    new_send,
    new_recv,
    q_send,
    q_recv,
    far_send,
    far_recv,
    part_send,
    part_recv,
    w_send,
    w_recv,
    w_mate,
    comp_send,
    comp_recv,
):
    me = lax.axis_index("seq")
    group = lax.axis_index("kv")
    z = me // CORES
    core = lax.rem(me, CORES)
    chips = n_seq // CORES
    mate = z * CORES + 1 - core
    half_line = z // (chips // 2)
    step = CORES - 2 * CORES * half_line
    inner = me + step
    outer = lax.rem(me - step + n_seq, n_seq)
    middle = (z > 0) & (z < chips - 1)
    at_end = jnp.logical_not(middle)
    right = lax.rem(me + CORES, n_seq)
    width, cache = ckt.shape
    fresh = ikt.shape[1]
    vw = cv.shape[2]
    low = width - vw
    wide = rows_vm.shape[1]
    per = cache // SEL_BLOCK
    size = per // PIECES
    new_per = fresh // SEL_BLOCK
    half_block = SEL_BLOCK // 2
    heads = q.shape[1] // width
    tile = fresh // tiles
    picks = sel.shape[1]
    count = heads * tile
    lookback = WINDOW // fresh
    hops = -(-lookback // CORES)
    chunks = cache // CMP_STRIDE
    pad = chunks + CMP_STRIDE
    factor = width**-0.5 * LOG2E
    tail_pieces = range(PIECES - WINDOW // SEL_BLOCK // size, PIECES)[::-1]
    all_pieces = range(PIECES)[::-1]

    across = inner
    near = (n_seq - CORES) * half_line + core
    far = (n_seq - CORES) * (1 - half_line) + core
    last = n_seq - 1
    takes_tail = (z == 0) & (core == CORES - 1)
    gives_tail = (z == 1) & (core == CORES - 1)
    wants_tail = (z == 0) & (core == 0)

    flip = group + 1 - 2 * lax.rem(group, 2)
    turn = lax.rem(group + n_kv // 2, n_kv)
    beside = (flip + core * (turn - flip), turn + core * (flip - turn))
    opposite = n_kv - 1 - group

    barrier = pltpu.get_barrier_semaphore()
    for to, when in (
        (me + CORES, z < chips - 1),
        (me - CORES, z > 0),
        (me + 1, (core == CORES - 1) & (z < chips - 1)),
        (me - 1, (core == 0) & (z > 0)),
    ):

        @pl.when(when)
        def _():
            pl.semaphore_signal(barrier, inc=1, device_id={"seq": to}, device_id_type=MESH)

    pl.semaphore_signal(barrier, inc=1, device_id={"seq": mate}, device_id_type=MESH)
    for to in beside:
        pl.semaphore_signal(barrier, inc=1, device_id={"kv": to}, device_id_type=MESH)

    half_k = wkt.shape[1] // CORES
    half_v = wv.shape[0] // CORES
    value_rows = pl.ds(SEL_BLOCK, SEL_BLOCK)
    loads = []
    for half in range(CORES):
        loads.append((wkt.at[:, pl.ds(half * half_k, half_k)], wk_all.at[group, half]))
        loads.append((wv.at[pl.ds(half * half_v, half_v)], wv_all.at[group, half]))
    held_weights = len(loads)
    loads += [
        (ikt, ikt_vm),
        (iv, new.at[pl.ds(me * new_per, new_per), value_rows]),
        (ckt, ckt_vm),
        (q, q_vm),
        (gw, gw_vm),
    ]
    load_copies = [pltpu.make_async_copy(a, b, local_sem.at[n]) for n, (a, b) in enumerate(loads)]
    for copy in load_copies:
        copy.start()

    own_at = pl.multiple_of(me * per, per)
    own_values = pltpu.make_async_copy(
        cv, kv.at[pl.ds(own_at, per), value_rows], local_sem.at[len(loads)]
    )
    own_values.start()

    def remote(src, dst, send, recv, to, axis="seq"):
        return pltpu.make_async_remote_copy(
            src_ref=src,
            dst_ref=dst,
            send_sem=send,
            recv_sem=recv,
            device_id={axis: to},
            device_id_type=MESH,
        )

    def blocks(slot, piece, pieces=1):
        return kv.at[pl.ds(pl.multiple_of(slot * per + piece * size, size), pieces * size)]

    def kv_msg(slot, piece, send, recv, to, pieces=1):
        ref = blocks(slot, piece, pieces)
        return remote(ref, ref, kv_send.at[send], recv, to)

    def kv_taken(slot, recv, piece=0, pieces=PIECES):
        kv_msg(slot, piece, 0, recv, mate, pieces).wait_recv()

    def new_msg(slot, send, recv, to):
        ref = new.at[pl.ds(slot * new_per, new_per)]
        return remote(ref, ref, new_send.at[send], new_recv.at[recv], to)

    def new_taken(slot, recv):
        new_msg(slot, 0, recv, mate).wait_recv()

    def new_sent(send):
        new_msg(me, send, 0, mate).wait_send()

    def q_msg(t):
        ref = pl.ds(t * tile, tile)
        return remote(q.at[ref], q_far.at[ref], q_send, q_recv.at[t], inner)

    def sel_msg():
        return remote(sel_out, sel_vm, far_send.at[0], far_recv.at[0], inner)

    def edge_msg():
        return remote(
            edge_own, edge_in, far_send.at[1], far_recv.at[1], lax.rem(me + 1, n_seq)
        )

    def part_msg(t):
        return remote(part_out.at[t], part_in.at[t], part_send, part_recv.at[t], outer)

    w_all = (wk_all, wv_all)
    origins = (*beside, opposite)

    def w_msg(n, part):
        return remote(
            w_all[part].at[group, core],
            w_all[part].at[group, core],
            w_send.at[part],
            w_recv.at[n, part],
            beside[n],
            "kv",
        )

    def w_onward(part):
        ref = w_all[part].at[beside[0], core]
        return remote(ref, ref, w_send.at[part], w_recv.at[2, part], beside[1], "kv")

    def w_pass(n, part):
        ref = w_all[part].at[origins[n], core]
        return remote(ref, ref, w_send.at[2 + part], w_mate.at[part], mate)

    def w_taken(n, part):
        ref = w_all[part].at[origins[n], core]
        remote(ref, ref, w_send.at[part], w_recv.at[n, part], mate).wait_recv()

    def w_all_but_own(part, send):
        ref = w_all[part].at[pl.ds(0, n_kv - 1), 0]
        return remote(ref, ref, w_send.at[send], w_mate.at[part], mate)


    def pack(keys, blocks, held, at):
        held[pl.ds(at, blocks), 0:SEL_BLOCK] = keys[:, 0:vw].reshape(blocks, SEL_BLOCK, vw)
        part = keys[:, vw:width].reshape(blocks, 2, half_block, low)
        held[pl.ds(at, blocks), 2 * SEL_BLOCK :] = jnp.concatenate(
            [part[:, 0], part[:, 1]], axis=-1
        )

    for copy in load_copies[held_weights : held_weights + 3]:
        copy.wait()
    pack(ikt_vm[...].T, new_per, new, me * new_per)

    keys = ckt_vm[...].T
    pack(keys, per, kv, own_at)
    own_values.wait()

    none = jnp.zeros((CMP_STRIDE, wide - width), jnp.bfloat16)
    edge_own[:, 0:wide] = jnp.concatenate([keys[cache - CMP_STRIDE :], none], axis=-1)
    edge_own[:, wide:] = kv[own_at + per - 1, 2 * SEL_BLOCK - CMP_STRIDE : 2 * SEL_BLOCK]
    @pl.when(middle)
    def _():
        pl.semaphore_wait(barrier, 6)

    @pl.when(at_end)
    def _():
        pl.semaphore_wait(barrier, 4 + (1 - half_line) * core + half_line * (1 - core))

    @pl.when(at_end)
    def _():
        sel_msg().start()

    up = z < chips - 1

    @pl.when(up)
    def _():
        new_msg(me, 0, 0, right).start()

    has_next = me < n_seq - 1

    @pl.when(has_next)
    def _():
        edge_msg().start()

    @pl.when(at_end)
    def _():
        for piece in all_pieces:
            kv_msg(me, piece, OWN_INNER, kv_recv.at[NEAR, piece], inner).start()
        q_msg(0).start()

    @pl.when(middle)
    def _():
        for piece in all_pieces:
            kv_msg(me, piece, OWN_INNER, kv_recv.at[ACROSS, piece], inner).start()
        for piece in all_pieces:
            kv_msg(me, piece, OWN_MATE, kv_mate.at[0], mate).start()

    for copy in load_copies[:held_weights]:
        copy.wait()
    for part in range(2):
        for n in range(2):
            w_msg(n, part).start()

    new_msg(me, 2, 2, mate).start()
    for copy in load_copies[held_weights + 3 :]:
        copy.wait()

    lane = lax.broadcasted_iota(jnp.int32, (tile, wide - width), 1)
    one = jnp.where(lane == 0, 1.0, 0.0).astype(jnp.bfloat16)

    for held in (compv, win_v, sel_v):
        held[:, vw:] = jnp.ones((held.shape[0], vw), jnp.bfloat16)

    def split_heads(src, t, dst, at):
        part = src[pl.ds(pl.multiple_of(t * tile, tile), tile), :]
        for h in range(heads):
            dst[pl.ds(at + h * tile, tile), :] = jnp.concatenate(
                [part[:, h * width : (h + 1) * width], one], axis=-1
            )

    @pl.loop(0, tiles)
    def _(t):
        split_heads(q_vm, t, rows_vm, pl.multiple_of(t * count, count))

    logits = lax.dot_general(
        rows_vm[:, 0:width],
        gw_vm[...],
        (((1,), (1,)), ((), ())),
        preferred_element_type=jnp.float32,
    )
    gates_vm[...] = jax.nn.sigmoid(logits)

    def relay_new(d):
        slot = me - CORES * d

        @pl.when(z >= d)
        def _():
            new_taken(slot, d - 1)
            new_msg(slot, 2 + d, 2 + d, mate).start()

    def raise_new(at):
        @pl.when(at)
        def _():
            new_msg(me - CORES, 1, 1, right).start()

    def relay_across(pieces):
        @pl.when(middle)
        def _():
            for piece in pieces:
                kv_taken(across, kv_recv.at[ACROSS, piece], piece, 1)
                kv_msg(across, piece, ACROSS_MATE, kv_mate.at[1], mate).start()

    def relay_near(pieces):
        @pl.when(middle)
        def _():
            for piece in pieces:
                kv_taken(near, kv_recv.at[NEAR, piece], piece, 1)
                kv_msg(near, piece, NEAR_INNER, kv_recv.at[FAR, piece], inner).start()
                kv_msg(near, piece, NEAR_MATE, kv_mate.at[2], mate).start()

    def relay_far(pieces):
        @pl.when(middle)
        def _():
            for piece in pieces:
                kv_taken(far, kv_recv.at[FAR, piece], piece, 1)
                sem = kv_mate.at[3 if piece in tail_pieces else 4]
                kv_msg(far, piece, FAR_MATE, sem, mate).start()
                if piece in tail_pieces:

                    @pl.when(gives_tail)
                    def _():
                        kv_msg(
                            last, piece, TAIL_OUTER, kv_recv.at[FAR, piece], outer
                        ).start()

    def take_tail():
        @pl.when(takes_tail)
        def _():
            for piece in tail_pieces:
                kv_taken(last, kv_recv.at[FAR, piece], piece, 1)
                kv_msg(last, piece, FAR_MATE, kv_mate.at[3], mate).start()

        @pl.when(wants_tail)
        def _():
            kv_taken(last, kv_mate.at[3], tail_pieces[-1], len(tail_pieces))

    def comp_msg(slot, send, recv, to):
        ref = comp_all.at[slot]
        src = comp_vm if slot is me else ref
        return remote(src, ref, comp_send.at[send], comp_recv.at[recv], to)

    def comp_some(slots, send):
        ref = comp_all.at[pl.ds(0, slots)]
        return remote(ref, ref, comp_send.at[send], comp_recv.at[3], mate)

    def comp_relay(n, to=None, recv=0):
        @pl.when(middle)
        def _():
            slot = (outer, inner, far)[n]
            comp_msg(slot, 0, n, mate).wait_recv()
            if to is not None:
                comp_msg(slot, 1, recv, to).start()
            comp_msg(slot, 0, 3, mate).start()

    comp_keep = pltpu.make_async_copy(comp_vm, comp_all.at[me], own_sem)

    group_rows = CMP_STRIDE * CMP_STRIDE

    def spread_tokens():
        row = lax.broadcasted_iota(jnp.int32, (group_rows, group_rows), 0)
        token = lax.broadcasted_iota(jnp.int32, (group_rows, group_rows), 1)
        want = lax.rem(row, CMP_STRIDE) * CMP_STRIDE + row // CMP_STRIDE
        perm = jnp.where(token == want, 1.0, 0.0).astype(jnp.bfloat16)

        def lay(lhs, at, spread, each):
            spread = spread.astype(jnp.bfloat16)
            for p in range(CMP_STRIDE):
                lhs[at : at + CMP_STRIDE, p * each : (p + 1) * each] = spread[
                    p * CMP_STRIDE : (p + 1) * CMP_STRIDE
                ]

        for n in range(cache // group_rows):
            some = group_rows // SEL_BLOCK
            v = kv[pl.ds(own_at + n * some, some), SEL_BLOCK : 2 * SEL_BLOCK]
            v = v.reshape(group_rows, vw)
            lay(lhs_v, n * CMP_STRIDE, jnp.dot(perm, v, preferred_element_type=jnp.float32), vw)

        for n in range(cache // group_rows):
            spread = lax.dot_general(
                perm,
                ckt_vm[:, n * group_rows : (n + 1) * group_rows],
                (((1,), (1,)), ((), ())),
                preferred_element_type=jnp.float32,
            )
            lay(lhs_k, n * CMP_STRIDE, spread, width)

        @pl.when(me == 0)
        def _():
            edge_in[...] = jnp.zeros(edge_in.shape, jnp.bfloat16)

        @pl.when(me > 0)
        def _():
            edge_msg().wait_recv()

        row = lax.broadcasted_iota(jnp.int32, (group_rows, CMP_STRIDE), 0)
        token = lax.broadcasted_iota(jnp.int32, (group_rows, CMP_STRIDE), 1)
        want = (token == row // CMP_STRIDE) & (lax.rem(row, CMP_STRIDE) == CMP_STRIDE - 1)
        lead = jnp.where(want, 1.0, 0.0).astype(jnp.bfloat16)
        spread = jnp.dot(lead, edge_in[...], preferred_element_type=jnp.float32)
        lay(lhs_k, chunks, spread[:, 0:width], width)
        lay(lhs_v, chunks, spread[:, wide:], vw)

    def relay_weights():
        for part in range(2):
            w_taken(0, part)
            w_onward(part).start()
            w_pass(0, part).start()
        for part in range(2):
            w_taken(1, part)
            w_pass(1, part).start()

    def pass_weights():
        for part in range(2):
            w_taken(2, part)
            w_pass(2, part).start()

    def compress():
        for part in range(2):
            w_all_but_own(part, part).wait_recv()
        results = []
        for lhs, w, dims in (
            (lhs_k, wk_all, (((1,), (1,)), ((), ()))),
            (lhs_v, wv_all, (((1,), (0,)), ((), ()))),
        ):
            pieces = n_kv * CORES // 2
            depth = lhs.shape[1] // pieces
            sums = []
            for side in range(2):
                total = None
                for n in range(pieces):
                    at = side * pieces + n
                    term = lax.dot_general(
                        lhs[:, n * depth : (n + 1) * depth],
                        w[at // CORES, at % CORES],
                        dims,
                        preferred_element_type=jnp.float32,
                    )
                    total = term if total is None else total + term
                sums.append(total)
            lead = jnp.concatenate([sums[0][pad - 1 : pad], sums[0][0 : chunks - 1]], axis=0)
            results.append((lead + sums[1][0:chunks]).astype(jnp.bfloat16))
        made, made_v = results
        comp_vm[0:chunks, :] = made[:, 0:vw]
        comp_vm[chunks : 2 * chunks, :] = made_v
        comp_vm[2 * chunks :, :] = jnp.concatenate(
            [made[0 : chunks // 2, vw:width], made[chunks // 2 :, vw:width]], axis=-1
        )
        @pl.when(middle)
        def _():
            comp_msg(me, 1, 1, inner).start()
            comp_msg(me, 1, 0, outer).start()

        @pl.when(at_end)
        def _():
            comp_msg(me, 1, 0, inner).start()

        comp_msg(me, 0, 3, mate).start()
        comp_keep.start()

    def attend(rows, keys, values, mask):
        half = rows.shape[0] // 2
        done = []
        for n in range(2):
            s = lax.dot_general(
                rows[n * half : (n + 1) * half],
                keys,
                (((1,), (1,)), ((), ())),
                preferred_element_type=jnp.float32,
            )
            if mask is not None:
                s = mask(s)
            top = jnp.max(s, axis=-1, keepdims=True)
            w = jnp.exp2((s - top) * factor).astype(jnp.bfloat16)
            o = jnp.dot(w, values, preferred_element_type=jnp.float32)
            done.append(o[:, 0:vw] / o[:, vw:])
        return jnp.concatenate(done, axis=0)

    def gated(branch, t, o, emit):
        g = gates_vm[pl.ds(pl.multiple_of(t * count, count), count), :]
        for h in range(heads):
            a = slice(h * tile, (h + 1) * tile)
            at = branch * heads + h
            emit(h, pl.ds(pl.multiple_of(t * count + h * tile, tile), tile), g[a, at : at + 1] * o[a])

    def rows_of(t):
        return rows_vm[pl.ds(pl.multiple_of(t * count, count), count), :]

    def bias_lanes(rows, value):
        lane = lax.broadcasted_iota(jnp.int32, (rows, wide - width), 1)
        return jnp.where(lane == 0, value, 0.0).astype(jnp.bfloat16)

    def compressed():
        comp_keep.wait()

        @pl.when(at_end)
        def _():
            for n in range(chips - 1):
                slot = me + step * (n + 1)
                comp_msg(slot, 0, n, mate).wait_recv()
                comp_msg(slot, 0, 3, mate).start()

        comp_some(chips, 0).wait_recv()
        total = n_seq * chunks
        first = lax.broadcasted_iota(jnp.int32, (total, wide - width), 0) == 0
        compk[:, width:wide] = bias_lanes(total, jnp.where(first, MASKED, 0.0))
        for slot in range(n_seq):
            at, mid = slot * chunks, slot * chunks + chunks // 2
            compk[at : at + chunks, 0:vw] = comp_all[slot, 0:chunks]
            compk[at:mid, vw:width] = comp_all[slot, 2 * chunks :, 0:low]
            compk[mid : at + chunks, vw:width] = comp_all[slot, 2 * chunks :, low : 2 * low]
            compv[at : at + chunks, 0:vw] = comp_all[slot, chunks : 2 * chunks]

        @pl.loop(0, tiles)
        def _(t):
            o = attend(rows_of(t), compk[...], compv[...], None)

            def emit(h, at, x):
                acc[at, :] += x

            gated(0, t, o, emit)

    def put(dk, dv, at, block, bias):
        rest = block[2 * SEL_BLOCK :]
        rest = jnp.concatenate([rest[:, 0:low], rest[:, low : 2 * low]], axis=0)
        dk[pl.ds(at, SEL_BLOCK), 0:vw] = block[0:SEL_BLOCK]
        dk[pl.ds(at, SEL_BLOCK), vw:wide] = jnp.concatenate([rest, bias], axis=-1)
        dv[pl.ds(at, SEL_BLOCK), 0:vw] = block[SEL_BLOCK : 2 * SEL_BLOCK]

    def window():
        relay_new(hops)
        for d in range(hops + 1):

            @pl.when(z >= d)
            def _():
                new_taken((z - d) * CORES + 1 - core, 2 + d)

        none = bias_lanes(SEL_BLOCK, 0.0)
        for i in range(lookback + 1):
            chunk = me + i
            for b in range(new_per):
                at = (i * new_per + b) * SEL_BLOCK

                @pl.when(chunk < lookback)
                def _():
                    block = n_seq * per - lookback * new_per + chunk * new_per + b
                    put(win_k, win_v, at, kv[block], none)

                @pl.when(chunk >= lookback)
                def _():
                    put(win_k, win_v, at, new[(chunk - lookback) * new_per + b], none)

        span = WINDOW + tile

        def edges(first, last):
            diff = lax.broadcasted_iota(jnp.int32, (count // 2, last - first), 1) + first
            diff = diff - lax.rem(lax.broadcasted_iota(jnp.int32, diff.shape, 0), tile)
            return (diff > 0) & (diff <= WINDOW)

        head_ok, tail_ok = edges(0, vw), edges(WINDOW, span)

        def mask(s):
            return jnp.concatenate(
                [
                    jnp.where(head_ok, s[:, 0:vw], MASKED),
                    s[:, vw:WINDOW],
                    jnp.where(tail_ok, s[:, WINDOW:span], MASKED),
                ],
                axis=-1,
            )

        @pl.loop(0, tiles)
        def _(t):
            off = pl.multiple_of(t * tile, tile)
            o = attend(rows_of(t), win_k[pl.ds(off, span), :], win_v[pl.ds(off, span), :], mask)

            def emit(h, at, x):
                acc[at, :] = x

            gated(2, t, o, emit)

    def pick(chosen, t):
        none = bias_lanes(SEL_BLOCK, 0.0)
        for n in range(picks):
            put(sel_k, sel_v, n * SEL_BLOCK, kv[chosen[t, n]], none)

    early = tiles // 2

    def far_row(t):
        q_msg(t).wait_recv()
        split_heads(q_far, t, rows_far, pl.multiple_of(t * count, count))

    def far_rows(first, last):
        @pl.when(middle)
        def _():
            pl.loop(first, last)(far_row)

    def exported():
        @pl.loop(0, tiles)
        def _(t):
            pl.when(t >= early)(lambda: far_row(t))
            pick(sel_far, t)
            o = attend(rows_far[pl.ds(pl.multiple_of(t * count, count), count), :], sel_k[...], sel_v[...], None)
            part_out[t] = o.astype(jnp.bfloat16)
            part_msg(t).start()

            @pl.when(t == 0)
            def _():
                comp_relay(1, outer, 1)
                comp_relay(2, outer, 2)

    def finish(t, o):
        to = pl.ds(pl.multiple_of(t * tile, tile), tile)

        def emit(h, at, x):
            out_vm[to, h * vw : (h + 1) * vw] = (acc[at, :] + x).astype(out.dtype)

        gated(1, t, o, emit)
        pltpu.make_async_copy(out_vm.at[to], out.at[to], out_sem).start()

    relay_new(1)
    raise_new(middle)
    spread_tokens()
    for piece in all_pieces[:4]:
        relay_across((piece,))
        relay_near((piece,))
    relay_weights()
    for piece in all_pieces[4:]:
        relay_across((piece,))
        relay_near((piece,))
    pass_weights()
    compress()

    @pl.when(at_end)
    def _():
        for t in range(1, tiles):
            q_msg(t).start()

    comp_relay(0, inner, 2)
    relay_far(tail_pieces)
    take_tail()
    rest = tail_pieces[-1]

    @pl.when(middle)
    def _():
        kv_taken(far + 1 - 2 * core, kv_mate.at[3], rest, PIECES - rest)

    window()
    relay_far(range(rest)[::-1])
    far_rows(0, early)

    @pl.when(middle)
    def _():
        sel_msg().wait_recv()
        copy = pltpu.make_async_copy(sel_vm, sel_far, sel_sem)
        copy.start()
        copy.wait()
        kv_taken(mate, kv_mate.at[0])
        kv_taken(across + 1 - 2 * core, kv_mate.at[1])
        kv_taken(near + 1 - 2 * core, kv_mate.at[2])
        kv_taken(far + 1 - 2 * core, kv_mate.at[4], 0, rest)
        exported()

    compressed()

    @pl.when(middle)
    def _():
        @pl.loop(0, tiles)
        def _(t):
            pick(sel, t)
            finish(t, attend(rows_of(t), sel_k[...], sel_v[...], None))

        remote(part_out, part_in, part_send, part_recv.at[0], outer).wait_send()
        for send in (OWN_INNER, NEAR_INNER, OWN_MATE, NEAR_MATE, ACROSS_MATE, FAR_MATE):
            kv_msg(me, 0, send, kv_mate.at[0], mate, PIECES).wait_send()

    @pl.when(gives_tail)
    def _():
        kv_msg(me, 0, TAIL_OUTER, kv_mate.at[0], mate, len(tail_pieces)).wait_send()

    @pl.when(at_end)
    def _():
        @pl.loop(0, tiles)
        def _(t):
            part_msg(t).wait_recv()
            finish(t, part_in[t].astype(jnp.float32))

        kv_msg(me, 0, OWN_INNER, kv_mate.at[0], mate, PIECES).wait_send()
        sel_msg().wait_send()
        remote(q_vm, q_far, q_send, q_recv.at[0], inner).wait_send()

    @pl.when(takes_tail)
    def _():
        kv_msg(me, 0, FAR_MATE, kv_mate.at[0], mate, len(tail_pieces)).wait_send()

    @pl.when(has_next)
    def _():
        edge_msg().wait_send()

    @pl.when(up)
    def _():
        new_sent(0)

    @pl.when(up & (z > 0))
    def _():
        new_sent(1)

    new_sent(2)
    for d in range(1, hops + 1):

        @pl.when(z >= d)
        def _():
            new_sent(2 + d)

    for part in range(2):
        w_all_but_own(part, part).wait_send()
        w_all_but_own(part, 2 + part).wait_send()
    comp_some(chips, 0).wait_send()

    @pl.when(middle)
    def _():
        comp_some(chips + 1, 1).wait_send()

    @pl.when(at_end)
    def _():
        comp_some(1, 1).wait_send()

    pltpu.make_async_copy(out_vm, out, out_sem).wait()


def shards_gathered(q, ck, cv, ik, iv, wk, wv, sel, gw):
    n_seq, n_kv = lax.axis_size("seq"), lax.axis_size("kv")
    heads, width, branches = gw.shape
    vw = cv.shape[1]
    cache, fresh = ck.shape[0], ik.shape[0]
    tiles, picks = sel.shape[0], sel.shape[-1]
    chunks = cache // CMP_STRIDE
    pad = chunks + CMP_STRIDE
    per, new_per = cache // SEL_BLOCK, fresh // SEL_BLOCK
    tile_rows = heads * fresh
    count = tile_rows // tiles
    wide = -(-width // 128) * 128
    block_rows = 2 * SEL_BLOCK + SEL_BLOCK // 2
    bf = jnp.bfloat16
    any_spec = pl.BlockSpec(memory_space=pl.ANY)
    half_k, half_v = wk.shape[0] // CORES, wv.shape[0] // CORES

    def held(*shape):
        return pltpu.VMEM(shape, bf)

    dma = pltpu.SemaphoreType.DMA
    picked = sel.reshape(tiles, picks)
    return pl.pallas_call(
        functools.partial(fused_kernel, n_seq, n_kv, tiles),
        out_shape=jax.ShapeDtypeStruct((fresh, heads * vw), bf),
        in_specs=[
            pl.BlockSpec(memory_space=pltpu.SMEM),
            pl.BlockSpec(memory_space=pltpu.VMEM),
        ]
        + [any_spec] * 8,
        out_specs=any_spec,
        scratch_shapes=[
            held(*q.shape),
            held(*q.shape),
            pltpu.VMEM((tiles, picks), jnp.int32),
            pltpu.SMEM((tiles, picks), jnp.int32),
            held(width, cache),
            held(width, fresh),
            held(heads * branches, width),
            held(n_seq * per, block_rows, vw),
            held(n_seq * new_per, block_rows, vw),
            held(CMP_STRIDE, wide + vw),
            held(CMP_STRIDE, wide + vw),
            held(pad, CMP_STRIDE * width),
            held(pad, CMP_STRIDE * vw),
            held(n_kv, CORES, width, half_k),
            held(n_kv, CORES, half_v, vw),
            held(2 * chunks + chunks // 2, vw),
            held(n_seq, 2 * chunks + chunks // 2, vw),
            held(n_seq * chunks, wide),
            held(n_seq * chunks, 2 * vw),
            held(tile_rows, wide),
            held(tile_rows, wide),
            pltpu.VMEM((tile_rows, heads * branches), jnp.float32),
            pltpu.VMEM((tile_rows, vw), jnp.float32),
            held(tiles, count, vw),
            held(tiles, count, vw),
            held(fresh, heads * vw),
            held(fresh + WINDOW, wide),
            held(fresh + WINDOW, 2 * vw),
            held(picks * SEL_BLOCK, wide),
            held(picks * SEL_BLOCK, 2 * vw),
            dma((6 + 2 * CORES,)),
            dma,
            dma,
            dma,
            dma((7,)),
            dma((3, PIECES)),
            dma((5,)),
            dma((3 + -(-WINDOW // (fresh * CORES)),)),
            dma((3 + -(-WINDOW // (fresh * CORES)),)),
            dma,
            dma((tiles,)),
            dma((2,)),
            dma((2,)),
            dma,
            dma((tiles,)),
            dma((4,)),
            dma((3, 2)),
            dma((2,)),
            dma((2,)),
            dma((4,)),
        ],
        compiler_params=pltpu.CompilerParams(
            collective_id=0, has_side_effects=True, vmem_limit_bytes=60 << 20
        ),
    )(
        picked,
        picked,
        q,
        ck.T,
        cv.reshape(per, SEL_BLOCK, vw),
        ik.T,
        iv.reshape(new_per, SEL_BLOCK, vw),
        wk.T,
        wv,
        jnp.transpose(gw, (2, 0, 1)).reshape(heads * branches, width),
    )


GATHER_BYTES = 1 << 24


def shards(queries, cache_keys, cache_values, *rest):
    ranks = lax.axis_size("seq")
    size = ranks * 2 * (cache_keys.size + cache_values.size)
    fits = size <= GATHER_BYTES and ranks == CORES * CHIPS and lax.axis_size("kv") == GROUPS
    form = shards_gathered if fits else shards_by_request
    return form(queries, cache_keys, cache_values, *rest)


def solution(mesh):
    placed = (
        P("seq", "kv"),
        P("seq", "kv"),
        P("seq", "kv"),
        P("seq", "kv"),
        P("seq", "kv"),
        P("kv", None),
        P("kv", None),
        P("seq", "kv", None),
        P("kv", None, None),
    )
    return jax.shard_map(
        shards, mesh=mesh, in_specs=placed, out_specs=P("seq", "kv"), check_vma=False
    )
```

```python
import functools

import jax
import jax.numpy as jnp
from jax import lax
from jax.experimental import pallas as pl
from jax.experimental.pallas import tpu as pltpu
from jax.sharding import PartitionSpec as P

CMP_STRIDE = 16
SEL_BLOCK = 64
WINDOW = 512


MASKED = -1e30


def passed_along(block, axis, distance):
    devices = range(lax.axis_size(axis))
    route = [((i - distance) % len(devices), i) for i in devices]
    return lax.ppermute(block, axis, route)


def from_behind(x, axis, by):
    peers = lax.axis_size(axis)
    pairs = [(i, i + by) for i in range(peers) if 0 <= i + by < peers]
    return lax.ppermute(x, axis, pairs)


def pack_rows(keys, values):
    return jnp.concatenate([keys.reshape(-1), values.reshape(-1)])


def unpack_rows(flat, count, key_width, value_width):
    keys = flat[: count * key_width].reshape(count, key_width)
    values = flat[count * key_width : count * (key_width + value_width)].reshape(count, value_width)
    return (keys, values)


def finish_rows(scores, values):
    top = jnp.max(scores, axis=-1, keepdims=True)
    weights = jnp.exp(scores - top)
    total = jnp.sum(weights, axis=-1, keepdims=True)
    mixed = jnp.matmul(weights.astype(jnp.bfloat16), values, preferred_element_type=jnp.float32)
    return mixed / total


def shards_by_request(
    queries,
    cache_keys,
    cache_values,
    incoming_keys,
    new_values,
    comp_key_weight,
    comp_value_weight,
    select_blocks,
    gate_weight,
):
    heads, key_width, _ = gate_weight.shape
    value_width = cache_values.shape[1]
    query_count = queries.shape[0]
    cache_count = cache_keys.shape[0]
    ranks = lax.axis_size("seq")
    place = lax.axis_index("seq")
    scale = key_width ** (-0.5)
    rows = queries.reshape(query_count * heads, key_width)
    row_total = rows.shape[0]
    stretch_pos = place * query_count + jnp.arange(query_count, dtype=jnp.int32)
    lookback_length = -(-WINDOW // query_count)
    weight_keys, weight_values = (
        lax.all_gather(comp_key_weight, "kv", axis=0, tiled=True),
        lax.all_gather(comp_value_weight, "kv", axis=0, tiled=True),
    )
    tail_pack = pack_rows(cache_keys[cache_count - WINDOW :], cache_values[cache_count - WINDOW :])
    moved_tail = passed_along(tail_pack, "seq", 1)
    before_keys, before_values = unpack_rows(moved_tail, WINDOW, key_width, value_width)
    edge_keys = before_keys[WINDOW - CMP_STRIDE :]
    edge_values = before_values[WINDOW - CMP_STRIDE :]
    held_tail = jnp.where(place == 0, moved_tail, jnp.zeros_like(moved_tail))
    tail_size = held_tail.shape[0]
    tail_flat = held_tail
    near_keys = []
    near_values = []
    nearby_positions = []
    near_valid = []
    own = pack_rows(incoming_keys, new_values)
    own_size = own.shape[0]
    for back in range(lookback_length, 0, -1):
        moved = from_behind(jnp.concatenate([own, held_tail]), "seq", back)
        got_keys, got_values = unpack_rows(moved, query_count, key_width, value_width)
        tail_flat = jnp.where(place == back, moved[own_size : own_size + tail_size], tail_flat)
        near_keys.append(got_keys)
        near_values.append(got_values)
        nearby_positions.append(
            (place - back) * query_count + jnp.arange(query_count, dtype=jnp.int32)
        )
        near_valid.append(jnp.broadcast_to(place >= back, (query_count,)))
    tail_keys, tail_values = unpack_rows(tail_flat, WINDOW, key_width, value_width)
    near_keys.append(tail_keys)
    near_values.append(tail_values)
    nearby_positions.append(jnp.arange(WINDOW, dtype=jnp.int32) - WINDOW)
    near_valid.append(jnp.ones((WINDOW,), dtype=bool))
    near_keys.append(incoming_keys)
    near_values.append(new_values)
    nearby_positions.append(stretch_pos)
    near_valid.append(jnp.ones((query_count,), dtype=bool))
    half_keys = CMP_STRIDE * key_width
    half_values = CMP_STRIDE * value_width
    lead_keys = jnp.concatenate([edge_keys, cache_keys[: cache_count - CMP_STRIDE]]).reshape(
        -1, half_keys
    )
    lead_values = jnp.concatenate([edge_values, cache_values[: cache_count - CMP_STRIDE]]).reshape(
        -1, half_values
    )
    comp_keys = (
        jnp.dot(lead_keys, weight_keys[:half_keys], preferred_element_type=jnp.float32)
        + jnp.dot(
            cache_keys.reshape(-1, half_keys),
            weight_keys[half_keys:],
            preferred_element_type=jnp.float32,
        )
    ).astype(jnp.bfloat16)
    comp_values = (
        jnp.dot(lead_values, weight_values[:half_values], preferred_element_type=jnp.float32)
        + jnp.dot(
            cache_values.reshape(-1, half_values),
            weight_values[half_values:],
            preferred_element_type=jnp.float32,
        )
    ).astype(jnp.bfloat16)
    start = jnp.int32(0)
    top = jnp.full((row_total,), MASKED, jnp.float32)
    total = jnp.zeros((row_total,), jnp.float32)
    summed = jnp.zeros((row_total, value_width), jnp.float32)
    keys = lax.all_gather(comp_keys, "seq", axis=0, tiled=True)
    values = lax.all_gather(comp_values, "seq", axis=0, tiled=True)
    length = keys.shape[0]
    block = length
    for size in (1024, 512, 256, 128):
        if length % size == 0:
            block = size
            break
    for index in range(length // block):
        key_block = keys[index * block : (index + 1) * block]
        value_block = values[index * block : (index + 1) * block]
        scores = (
            jnp.einsum("rd,kd->rk", rows, key_block, preferred_element_type=jnp.float32) * scale
        )
        key_at = start + index * block + jnp.arange(block, dtype=jnp.int32)
        scores = jnp.where(key_at[None, :] > 0, scores, MASKED)
        newtop = jnp.maximum(top, jnp.max(scores, axis=1))
        factor = jnp.exp(top - newtop)
        weights = jnp.exp(scores - newtop[:, None])
        total = total * factor + jnp.sum(weights, axis=1)
        summed = summed * factor[:, None] + jnp.dot(
            weights.astype(jnp.bfloat16), value_block, preferred_element_type=jnp.float32
        )
        top = newtop
    top, total, summed = (top, total, summed)
    compressed_out = summed / total[:, None]
    chosen = select_blocks.reshape(-1)
    shard_blocks = cache_count // SEL_BLOCK
    capacity = max(2, 2 * chosen.shape[0] // ranks)
    owner = chosen // shard_blocks
    local = chosen - owner * shard_blocks
    count = chosen.shape[0]
    order = jnp.arange(count, dtype=jnp.int32)
    same = owner[:, None] == owner[None, :]
    position = jnp.sum((same & (order[None, :] < order[:, None])).astype(jnp.int32), axis=1)
    where_at = owner * capacity + position
    slots = jnp.arange(ranks * capacity, dtype=jnp.int32)
    wanted = where_at[:, None] == slots[None, :]
    request = jnp.sum(jnp.where(wanted, local[:, None], 0), axis=0).reshape(ranks, capacity)
    asked = lax.all_to_all(request, "seq", split_axis=0, concat_axis=0, tiled=True)
    tile_count = select_blocks.shape[0]

    def picked(hot, table):
        return jnp.dot(
            hot.astype(jnp.bfloat16), table, preferred_element_type=jnp.float32
        ).astype(jnp.bfloat16)

    asked_hot = asked.reshape(-1, 1) == jnp.arange(shard_blocks, dtype=jnp.int32)[None, :]

    def fetched(table):
        sent = picked(asked_hot, table.reshape(shard_blocks, -1)).reshape(ranks, capacity, -1)
        got = lax.all_to_all(sent, "seq", split_axis=0, concat_axis=0, tiled=True)
        return picked(wanted, got.reshape(ranks * capacity, -1))

    gathered_keys = fetched(cache_keys)
    picked_values = fetched(cache_values)
    gathered_keys, picked_values = (
        gathered_keys.reshape(tile_count, -1, key_width),
        picked_values.reshape(tile_count, -1, value_width),
    )
    tile_count = gathered_keys.shape[0]
    tile_row_count = rows.reshape(tile_count, -1, key_width)
    tile_scores = (
        jnp.einsum(
            "izu,ixu->izx", tile_row_count, gathered_keys, preferred_element_type=jnp.float32
        )
        * scale
    )
    selected_out = finish_rows(tile_scores, picked_values).reshape(row_total, value_width)
    context_keys = jnp.concatenate(near_keys)
    context_values = jnp.concatenate(near_values)
    context_positions = jnp.concatenate(nearby_positions)
    context_valid = jnp.concatenate(near_valid)
    sliding_scores = (
        jnp.einsum("rd,kd->rk", rows, context_keys, preferred_element_type=jnp.float32) * scale
    )
    allowed = (
        context_valid[None, :]
        & (context_positions[None, :] <= stretch_pos[:, None])
        & (context_positions[None, :] > stretch_pos[:, None] - WINDOW)
    )
    sliding_scores = jnp.where(
        allowed[:, None, :], sliding_scores.reshape(query_count, heads, -1), MASKED
    )
    window_out = finish_rows(sliding_scores.reshape(row_total, -1), context_values)
    logits = jnp.einsum(
        "thd,hdb->thb",
        queries.reshape(query_count, heads, key_width),
        gate_weight,
        preferred_element_type=jnp.float32,
    )
    gates = jax.nn.sigmoid(logits)
    mixed = (
        gates[:, :, 0:1] * compressed_out.reshape(query_count, heads, value_width)
        + gates[:, :, 1:2] * selected_out.reshape(query_count, heads, value_width)
        + gates[:, :, 2:3] * window_out.reshape(query_count, heads, value_width)
    )
    return mixed.astype(jnp.bfloat16).reshape(query_count, heads * value_width)


CORES = 2
CHIPS, GROUPS = 4, 4
PIECES = 8
LOG2E = 1.4426950408889634
MESH = pl.DeviceIdType.MESH
FAR, NEAR, ACROSS = range(3)
OWN_INNER, NEAR_INNER, TAIL_OUTER, OWN_MATE, NEAR_MATE, ACROSS_MATE, FAR_MATE = range(7)


def fused_kernel(
    n_seq,
    n_kv,
    tiles,
    sel,
    sel_out,
    q,
    ckt,
    cv,
    ikt,
    iv,
    wkt,
    wv,
    gw,
    out,
    q_vm,
    q_far,
    sel_vm,
    sel_far,
    ckt_vm,
    ikt_vm,
    gw_vm,
    kv,
    new,
    edge_own,
    edge_in,
    lhs_k,
    lhs_v,
    wk_all,
    wv_all,
    comp_vm,
    comp_all,
    compk,
    compv,
    rows_vm,
    rows_far,
    gates_vm,
    acc,
    part_out,
    part_in,
    out_vm,
    win_k,
    win_v,
    sel_k,
    sel_v,
    local_sem,
    own_sem,
    sel_sem,
    out_sem,
    kv_send,
    kv_recv,
    kv_mate,
    new_send,
    new_recv,
    q_send,
    q_recv,
    far_send,
    far_recv,
    part_send,
    part_recv,
    w_send,
    w_recv,
    w_mate,
    comp_send,
    comp_recv,
):
    me = lax.axis_index("seq")
    group = lax.axis_index("kv")
    z = me // CORES
    core = lax.rem(me, CORES)
    chips = n_seq // CORES
    mate = z * CORES + 1 - core
    half_line = z // (chips // 2)
    step = CORES - 2 * CORES * half_line
    inner = me + step
    outer = lax.rem(me - step + n_seq, n_seq)
    middle = (z > 0) & (z < chips - 1)
    at_end = jnp.logical_not(middle)
    right = lax.rem(me + CORES, n_seq)
    width, cache = ckt.shape
    fresh = ikt.shape[1]
    vw = cv.shape[2]
    low = width - vw
    wide = rows_vm.shape[1]
    per = cache // SEL_BLOCK
    size = per // PIECES
    new_per = fresh // SEL_BLOCK
    half_block = SEL_BLOCK // 2
    heads = q.shape[1] // width
    tile = fresh // tiles
    picks = sel.shape[1]
    count = heads * tile
    lookback = WINDOW // fresh
    hops = -(-lookback // CORES)
    chunks = cache // CMP_STRIDE
    pad = chunks + CMP_STRIDE
    factor = width**-0.5 * LOG2E
    tail_pieces = range(PIECES - WINDOW // SEL_BLOCK // size, PIECES)[::-1]
    all_pieces = range(PIECES)[::-1]

    across = inner
    near = (n_seq - CORES) * half_line + core
    far = (n_seq - CORES) * (1 - half_line) + core
    last = n_seq - 1
    takes_tail = (z == 0) & (core == CORES - 1)
    gives_tail = (z == 1) & (core == CORES - 1)
    wants_tail = (z == 0) & (core == 0)

    flip = group + 1 - 2 * lax.rem(group, 2)
    turn = lax.rem(group + n_kv // 2, n_kv)
    beside = (flip + core * (turn - flip), turn + core * (flip - turn))
    opposite = n_kv - 1 - group

    barrier = pltpu.get_barrier_semaphore()
    for to, when in (
        (me + CORES, z < chips - 1),
        (me - CORES, z > 0),
        (me + 1, (core == CORES - 1) & (z < chips - 1)),
        (me - 1, (core == 0) & (z > 0)),
    ):

        @pl.when(when)
        def _():
            pl.semaphore_signal(barrier, inc=1, device_id={"seq": to}, device_id_type=MESH)

    pl.semaphore_signal(barrier, inc=1, device_id={"seq": mate}, device_id_type=MESH)
    for to in beside:
        pl.semaphore_signal(barrier, inc=1, device_id={"kv": to}, device_id_type=MESH)

    half_k = wkt.shape[1] // CORES
    half_v = wv.shape[0] // CORES
    value_rows = pl.ds(SEL_BLOCK, SEL_BLOCK)
    loads = []
    for half in range(CORES):
        loads.append((wkt.at[:, pl.ds(half * half_k, half_k)], wk_all.at[group, half]))
        loads.append((wv.at[pl.ds(half * half_v, half_v)], wv_all.at[group, half]))
    held_weights = len(loads)
    loads += [
        (ikt, ikt_vm),
        (iv, new.at[pl.ds(me * new_per, new_per), value_rows]),
        (ckt, ckt_vm),
        (q, q_vm),
        (gw, gw_vm),
    ]
    load_copies = [pltpu.make_async_copy(a, b, local_sem.at[n]) for n, (a, b) in enumerate(loads)]
    for copy in load_copies:
        copy.start()

    own_at = pl.multiple_of(me * per, per)
    own_values = pltpu.make_async_copy(
        cv, kv.at[pl.ds(own_at, per), value_rows], local_sem.at[len(loads)]
    )
    own_values.start()

    def remote(src, dst, send, recv, to, axis="seq"):
        return pltpu.make_async_remote_copy(
            src_ref=src,
            dst_ref=dst,
            send_sem=send,
            recv_sem=recv,
            device_id={axis: to},
            device_id_type=MESH,
        )

    def blocks(slot, piece, pieces=1):
        return kv.at[pl.ds(pl.multiple_of(slot * per + piece * size, size), pieces * size)]

    def kv_msg(slot, piece, send, recv, to, pieces=1):
        ref = blocks(slot, piece, pieces)
        return remote(ref, ref, kv_send.at[send], recv, to)

    def kv_taken(slot, recv, piece=0, pieces=PIECES):
        kv_msg(slot, piece, 0, recv, mate, pieces).wait_recv()

    def new_msg(slot, send, recv, to):
        ref = new.at[pl.ds(slot * new_per, new_per)]
        return remote(ref, ref, new_send.at[send], new_recv.at[recv], to)

    def new_taken(slot, recv):
        new_msg(slot, 0, recv, mate).wait_recv()

    def new_sent(send):
        new_msg(me, send, 0, mate).wait_send()

    def q_msg(t):
        ref = pl.ds(t * tile, tile)
        return remote(q.at[ref], q_far.at[ref], q_send, q_recv.at[t], inner)

    def sel_msg():
        return remote(sel_out, sel_vm, far_send.at[0], far_recv.at[0], inner)

    def edge_msg():
        return remote(
            edge_own, edge_in, far_send.at[1], far_recv.at[1], lax.rem(me + 1, n_seq)
        )

    def half_msg(n):
        ref = pl.ds(n * (count // 2), count // 2)
        recv = part_recv.at[n * tiles]
        return remote(part_out.at[0, ref], part_in.at[0, ref], part_send, recv, outer)

    def part_msg(t):
        return remote(part_out.at[t], part_in.at[t], part_send, part_recv.at[t], outer)

    w_all = (wk_all, wv_all)
    origins = (*beside, opposite)

    def w_msg(n, part):
        return remote(
            w_all[part].at[group, core],
            w_all[part].at[group, core],
            w_send.at[part],
            w_recv.at[n, part],
            beside[n],
            "kv",
        )

    def w_onward(part):
        ref = w_all[part].at[beside[0], core]
        return remote(ref, ref, w_send.at[part], w_recv.at[2, part], beside[1], "kv")

    def w_pass(n, part):
        ref = w_all[part].at[origins[n], core]
        return remote(ref, ref, w_send.at[2 + part], w_mate.at[part], mate)

    def w_taken(n, part):
        ref = w_all[part].at[origins[n], core]
        remote(ref, ref, w_send.at[part], w_recv.at[n, part], mate).wait_recv()

    def w_all_but_own(part, send):
        ref = w_all[part].at[pl.ds(0, n_kv - 1), 0]
        return remote(ref, ref, w_send.at[send], w_mate.at[part], mate)


    def pack(keys, blocks, held, at):
        held[pl.ds(at, blocks), 0:SEL_BLOCK] = keys[:, 0:vw].reshape(blocks, SEL_BLOCK, vw)
        part = keys[:, vw:width].reshape(blocks, 2, half_block, low)
        held[pl.ds(at, blocks), 2 * SEL_BLOCK :] = jnp.concatenate(
            [part[:, 0], part[:, 1]], axis=-1
        )

    for copy in load_copies[held_weights : held_weights + 3]:
        copy.wait()
    pack(ikt_vm[...].T, new_per, new, me * new_per)

    keys = ckt_vm[...].T
    pack(keys, per, kv, own_at)
    own_values.wait()

    none = jnp.zeros((CMP_STRIDE, wide - width), jnp.bfloat16)
    edge_own[:, 0:wide] = jnp.concatenate([keys[cache - CMP_STRIDE :], none], axis=-1)
    edge_own[:, wide:] = kv[own_at + per - 1, 2 * SEL_BLOCK - CMP_STRIDE : 2 * SEL_BLOCK]
    @pl.when(middle)
    def _():
        pl.semaphore_wait(barrier, 6)

    @pl.when(at_end)
    def _():
        pl.semaphore_wait(barrier, 4 + (1 - half_line) * core + half_line * (1 - core))

    @pl.when(at_end)
    def _():
        sel_msg().start()

    up = z < chips - 1

    @pl.when(up)
    def _():
        new_msg(me, 0, 0, right).start()

    has_next = me < n_seq - 1

    @pl.when(has_next)
    def _():
        edge_msg().start()

    @pl.when(at_end)
    def _():
        for piece in all_pieces:
            kv_msg(me, piece, OWN_INNER, kv_recv.at[NEAR, piece], inner).start()
        q_msg(0).start()

    @pl.when(middle)
    def _():
        for piece in all_pieces:
            kv_msg(me, piece, OWN_INNER, kv_recv.at[ACROSS, piece], inner).start()
        for piece in all_pieces:
            kv_msg(me, piece, OWN_MATE, kv_mate.at[0], mate).start()

    for copy in load_copies[:held_weights]:
        copy.wait()
    for part in range(2):
        for n in range(2):
            w_msg(n, part).start()

    new_msg(me, 2, 2, mate).start()
    for copy in load_copies[held_weights + 3 :]:
        copy.wait()

    lane = lax.broadcasted_iota(jnp.int32, (tile, wide - width), 1)
    one = jnp.where(lane == 0, 1.0, 0.0).astype(jnp.bfloat16)

    for held in (compv, win_v, sel_v.at[0], sel_v.at[1]):
        held[:, vw:] = jnp.ones((held.shape[0], vw), jnp.bfloat16)

    def split_heads(src, t, dst, at):
        part = src[pl.ds(pl.multiple_of(t * tile, tile), tile), :]
        for h in range(heads):
            dst[pl.ds(at + h * tile, tile), :] = jnp.concatenate(
                [part[:, h * width : (h + 1) * width], one], axis=-1
            )

    @pl.loop(0, tiles)
    def _(t):
        split_heads(q_vm, t, rows_vm, pl.multiple_of(t * count, count))

    logits = lax.dot_general(
        rows_vm[:, 0:width],
        gw_vm[...],
        (((1,), (1,)), ((), ())),
        preferred_element_type=jnp.float32,
    )
    gates_vm[...] = jax.nn.sigmoid(logits)

    def relay_new(d):
        slot = me - CORES * d

        @pl.when(z >= d)
        def _():
            new_taken(slot, d - 1)
            new_msg(slot, 2 + d, 2 + d, mate).start()

    def raise_new(at):
        @pl.when(at)
        def _():
            new_msg(me - CORES, 1, 1, right).start()

    def relay_across(pieces):
        @pl.when(middle)
        def _():
            for piece in pieces:
                kv_taken(across, kv_recv.at[ACROSS, piece], piece, 1)
                kv_msg(across, piece, ACROSS_MATE, kv_mate.at[1], mate).start()

    def relay_near(pieces):
        @pl.when(middle)
        def _():
            for piece in pieces:
                kv_taken(near, kv_recv.at[NEAR, piece], piece, 1)
                kv_msg(near, piece, NEAR_INNER, kv_recv.at[FAR, piece], inner).start()
                kv_msg(near, piece, NEAR_MATE, kv_mate.at[2], mate).start()

    def relay_far(pieces):
        @pl.when(middle)
        def _():
            for piece in pieces:
                kv_taken(far, kv_recv.at[FAR, piece], piece, 1)
                sem = kv_mate.at[3 if piece in tail_pieces else 4]
                kv_msg(far, piece, FAR_MATE, sem, mate).start()
                if piece in tail_pieces:

                    @pl.when(gives_tail)
                    def _():
                        kv_msg(
                            last, piece, TAIL_OUTER, kv_recv.at[FAR, piece], outer
                        ).start()

    def take_tail():
        @pl.when(takes_tail)
        def _():
            for piece in tail_pieces:
                kv_taken(last, kv_recv.at[FAR, piece], piece, 1)
                kv_msg(last, piece, FAR_MATE, kv_mate.at[3], mate).start()

        @pl.when(wants_tail)
        def _():
            kv_taken(last, kv_mate.at[3], tail_pieces[-1], len(tail_pieces))

    def comp_msg(slot, send, recv, to):
        ref = comp_all.at[slot]
        src = comp_vm if slot is me else ref
        return remote(src, ref, comp_send.at[send], comp_recv.at[recv], to)

    def comp_some(slots, send):
        ref = comp_all.at[pl.ds(0, slots)]
        return remote(ref, ref, comp_send.at[send], comp_recv.at[3], mate)

    def comp_relay(n, to=None, recv=0):
        @pl.when(middle)
        def _():
            slot = (outer, inner, far)[n]
            comp_msg(slot, 0, n, mate).wait_recv()
            if to is not None:
                comp_msg(slot, 1, recv, to).start()
            comp_msg(slot, 0, 3, mate).start()

    comp_keep = pltpu.make_async_copy(comp_vm, comp_all.at[me], own_sem)

    group_rows = CMP_STRIDE * CMP_STRIDE

    def spread_tokens():
        row = lax.broadcasted_iota(jnp.int32, (group_rows, group_rows), 0)
        token = lax.broadcasted_iota(jnp.int32, (group_rows, group_rows), 1)
        want = lax.rem(row, CMP_STRIDE) * CMP_STRIDE + row // CMP_STRIDE
        perm = jnp.where(token == want, 1.0, 0.0).astype(jnp.bfloat16)

        def lay(lhs, at, spread, each):
            spread = spread.astype(jnp.bfloat16)
            for p in range(CMP_STRIDE):
                lhs[at : at + CMP_STRIDE, p * each : (p + 1) * each] = spread[
                    p * CMP_STRIDE : (p + 1) * CMP_STRIDE
                ]

        for n in range(cache // group_rows):
            some = group_rows // SEL_BLOCK
            v = kv[pl.ds(own_at + n * some, some), SEL_BLOCK : 2 * SEL_BLOCK]
            v = v.reshape(group_rows, vw)
            lay(lhs_v, n * CMP_STRIDE, jnp.dot(perm, v, preferred_element_type=jnp.float32), vw)

        for n in range(cache // group_rows):
            spread = lax.dot_general(
                perm,
                ckt_vm[:, n * group_rows : (n + 1) * group_rows],
                (((1,), (1,)), ((), ())),
                preferred_element_type=jnp.float32,
            )
            lay(lhs_k, n * CMP_STRIDE, spread, width)

        @pl.when(me == 0)
        def _():
            edge_in[...] = jnp.zeros(edge_in.shape, jnp.bfloat16)

        @pl.when(me > 0)
        def _():
            edge_msg().wait_recv()

        row = lax.broadcasted_iota(jnp.int32, (group_rows, CMP_STRIDE), 0)
        token = lax.broadcasted_iota(jnp.int32, (group_rows, CMP_STRIDE), 1)
        want = (token == row // CMP_STRIDE) & (lax.rem(row, CMP_STRIDE) == CMP_STRIDE - 1)
        lead = jnp.where(want, 1.0, 0.0).astype(jnp.bfloat16)
        spread = jnp.dot(lead, edge_in[...], preferred_element_type=jnp.float32)
        lay(lhs_k, chunks, spread[:, 0:width], width)
        lay(lhs_v, chunks, spread[:, wide:], vw)

    def relay_weights():
        for part in range(2):
            w_taken(0, part)
            w_onward(part).start()
            w_pass(0, part).start()
        for part in range(2):
            w_taken(1, part)
            w_pass(1, part).start()

    def pass_weights():
        for part in range(2):
            w_taken(2, part)
            w_pass(2, part).start()

    def compress():
        for part in range(2):
            w_all_but_own(part, part).wait_recv()
        results = []
        for lhs, w, dims in (
            (lhs_k, wk_all, (((1,), (1,)), ((), ()))),
            (lhs_v, wv_all, (((1,), (0,)), ((), ()))),
        ):
            pieces = n_kv * CORES // 2
            depth = lhs.shape[1] // pieces
            sums = []
            for side in range(2):
                total = None
                for n in range(pieces):
                    at = side * pieces + n
                    term = lax.dot_general(
                        lhs[:, n * depth : (n + 1) * depth],
                        w[at // CORES, at % CORES],
                        dims,
                        preferred_element_type=jnp.float32,
                    )
                    total = term if total is None else total + term
                sums.append(total)
            lead = jnp.concatenate([sums[0][pad - 1 : pad], sums[0][0 : chunks - 1]], axis=0)
            results.append((lead + sums[1][0:chunks]).astype(jnp.bfloat16))
        made, made_v = results
        comp_vm[0:chunks, :] = made[:, 0:vw]
        comp_vm[chunks : 2 * chunks, :] = made_v
        comp_vm[2 * chunks :, :] = jnp.concatenate(
            [made[0 : chunks // 2, vw:width], made[chunks // 2 :, vw:width]], axis=-1
        )
        @pl.when(middle)
        def _():
            comp_msg(me, 1, 1, inner).start()
            comp_msg(me, 1, 0, outer).start()

        @pl.when(at_end)
        def _():
            comp_msg(me, 1, 0, inner).start()

        comp_msg(me, 0, 3, mate).start()
        comp_keep.start()

    def attend(rows, keys, values, mask):
        half = rows.shape[0] // 2
        done = []
        for n in range(2):
            s = lax.dot_general(
                rows[n * half : (n + 1) * half],
                keys,
                (((1,), (1,)), ((), ())),
                preferred_element_type=jnp.float32,
            )
            if mask is not None:
                s = mask(s)
            top = jnp.max(s, axis=-1, keepdims=True)
            w = jnp.exp2((s - top) * factor).astype(jnp.bfloat16)
            o = jnp.dot(w, values, preferred_element_type=jnp.float32)
            done.append(o[:, 0:vw] / o[:, vw:])
        return jnp.concatenate(done, axis=0)

    def gated(branch, t, o, emit):
        g = gates_vm[pl.ds(pl.multiple_of(t * count, count), count), :]
        for h in range(heads):
            a = slice(h * tile, (h + 1) * tile)
            at = branch * heads + h
            emit(h, pl.ds(pl.multiple_of(t * count + h * tile, tile), tile), g[a, at : at + 1] * o[a])

    def rows_of(t):
        return rows_vm[pl.ds(pl.multiple_of(t * count, count), count), :]

    def bias_lanes(rows, value):
        lane = lax.broadcasted_iota(jnp.int32, (rows, wide - width), 1)
        return jnp.where(lane == 0, value, 0.0).astype(jnp.bfloat16)

    def compressed():
        comp_keep.wait()

        @pl.when(at_end)
        def _():
            for n in range(chips - 1):
                slot = me + step * (n + 1)
                comp_msg(slot, 0, n, mate).wait_recv()
                comp_msg(slot, 0, 3, mate).start()

        comp_some(chips, 0).wait_recv()
        for slot in range(n_seq):
            at, mid = slot * chunks, slot * chunks + chunks // 2
            compk[at : at + chunks, 0:vw] = comp_all[slot, 0:chunks]
            compk[at:mid, vw:width] = comp_all[slot, 2 * chunks :, 0:low]
            compk[mid : at + chunks, vw:width] = comp_all[slot, 2 * chunks :, low : 2 * low]
            compv[at : at + chunks, 0:vw] = comp_all[slot, chunks : 2 * chunks]

        @pl.loop(0, tiles)
        def _(t):
            o = attend(rows_of(t), compk[...], compv[...], None)

            def emit(h, at, x):
                acc[at, :] += x

            gated(0, t, o, emit)

    def put(dk, dv, at, block, bias):
        rest = block[2 * SEL_BLOCK :]
        rest = jnp.concatenate([rest[:, 0:low], rest[:, low : 2 * low]], axis=0)
        dk[pl.ds(at, SEL_BLOCK), 0:vw] = block[0:SEL_BLOCK]
        dk[pl.ds(at, SEL_BLOCK), vw:wide] = jnp.concatenate([rest, bias], axis=-1)
        dv[pl.ds(at, SEL_BLOCK), 0:vw] = block[SEL_BLOCK : 2 * SEL_BLOCK]

    def window():
        relay_new(hops)
        for d in range(hops + 1):

            @pl.when(z >= d)
            def _():
                new_taken((z - d) * CORES + 1 - core, 2 + d)

        none = bias_lanes(SEL_BLOCK, 0.0)
        for i in range(lookback + 1):
            chunk = me + i
            for b in range(new_per):
                at = (i * new_per + b) * SEL_BLOCK

                @pl.when(chunk < lookback)
                def _():
                    block = n_seq * per - lookback * new_per + chunk * new_per + b
                    put(win_k, win_v, at, kv[block], none)

                @pl.when(chunk >= lookback)
                def _():
                    put(win_k, win_v, at, new[(chunk - lookback) * new_per + b], none)

        span = WINDOW + tile

        def edges(first, last):
            diff = lax.broadcasted_iota(jnp.int32, (count // 2, last - first), 1) + first
            diff = diff - lax.rem(lax.broadcasted_iota(jnp.int32, diff.shape, 0), tile)
            return (diff > 0) & (diff <= WINDOW)

        head_ok, tail_ok = edges(0, vw), edges(WINDOW, span)

        def mask(s):
            return jnp.concatenate(
                [
                    jnp.where(head_ok, s[:, 0:vw], MASKED),
                    s[:, vw:WINDOW],
                    jnp.where(tail_ok, s[:, WINDOW:span], MASKED),
                ],
                axis=-1,
            )

        @pl.loop(0, tiles)
        def _(t):
            off = pl.multiple_of(t * tile, tile)
            o = attend(rows_of(t), win_k[pl.ds(off, span), :], win_v[pl.ds(off, span), :], mask)

            def emit(h, at, x):
                acc[at, :] = x

            gated(2, t, o, emit)

    def pick(chosen, t, sel_k, sel_v):
        none = bias_lanes(SEL_BLOCK, 0.0)
        for n in range(picks):
            put(sel_k, sel_v, n * SEL_BLOCK, kv[chosen[t, n]], none)

    early = tiles // 2

    def far_row(t):
        q_msg(t).wait_recv()
        split_heads(q_far, t, rows_far, pl.multiple_of(t * count, count))

    def far_rows(first, last):
        @pl.when(middle)
        def _():
            pl.loop(first, last)(far_row)

    def exported():
        pick(sel_far, 0, sel_k.at[0], sel_v.at[0])
        for n in range(2):
            at = n * (count // 2)
            o = attend(rows_far[at : at + count // 2, :], sel_k[0], sel_v[0], None)
            part_out[0, at : at + count // 2] = o.astype(jnp.bfloat16)
            half_msg(n).start()

        @pl.loop(1, tiles)
        def _(t):
            pl.when(t >= early)(lambda: far_row(t))
            pick(sel_far, t, sel_k.at[0], sel_v.at[0])
            far_at = pl.ds(pl.multiple_of(t * count, count), count)
            o = attend(rows_far[far_at, :], sel_k[0], sel_v[0], None)
            part_out[t] = o.astype(jnp.bfloat16)
            part_msg(t).start()

            @pl.when(t == 1)
            def _():
                comp_relay(1, outer, 1)
                comp_relay(2, outer, 2)

    def finish(t, o):
        to = pl.ds(pl.multiple_of(t * tile, tile), tile)

        def emit(h, at, x):
            out_vm[to, h * vw : (h + 1) * vw] = (acc[at, :] + x).astype(out.dtype)

        gated(1, t, o, emit)
        pltpu.make_async_copy(out_vm.at[to], out.at[to], out_sem).start()

    first = lax.broadcasted_iota(jnp.int32, (n_seq * chunks, wide - width), 0) == 0
    compk[:, width:wide] = bias_lanes(n_seq * chunks, jnp.where(first, MASKED, 0.0))
    relay_new(1)
    raise_new(middle)
    spread_tokens()
    for piece in all_pieces[:4]:
        relay_across((piece,))
        relay_near((piece,))
    relay_weights()
    for piece in all_pieces[4:]:
        relay_across((piece,))
        relay_near((piece,))
    pass_weights()
    compress()

    @pl.when(at_end)
    def _():
        for t in range(1, tiles):
            q_msg(t).start()

    comp_relay(0, inner, 2)
    relay_far(tail_pieces)
    take_tail()
    rest = tail_pieces[-1]

    @pl.when(middle)
    def _():
        kv_taken(far + 1 - 2 * core, kv_mate.at[3], rest, PIECES - rest)

    window()
    relay_far(range(rest)[::-1])
    far_rows(0, early)

    @pl.when(middle)
    def _():
        sel_msg().wait_recv()
        copy = pltpu.make_async_copy(sel_vm, sel_far, sel_sem)
        copy.start()
        copy.wait()
        kv_taken(mate, kv_mate.at[0])
        kv_taken(across + 1 - 2 * core, kv_mate.at[1])
        kv_taken(near + 1 - 2 * core, kv_mate.at[2])
        kv_taken(far + 1 - 2 * core, kv_mate.at[4], 0, rest)
        exported()

    compressed()

    @pl.when(middle)
    def _():
        @pl.loop(0, tiles, step=2)
        def _(t):
            for n in range(2):
                pick(sel, t + n, sel_k.at[n], sel_v.at[n])
            both = [attend(rows_of(t + n), sel_k[n], sel_v[n], None) for n in range(2)]
            for n in range(2):
                finish(t + n, both[n])

        remote(part_out, part_in, part_send, part_recv.at[0], outer).wait_send()
        for send in (OWN_INNER, NEAR_INNER, OWN_MATE, NEAR_MATE, ACROSS_MATE, FAR_MATE):
            kv_msg(me, 0, send, kv_mate.at[0], mate, PIECES).wait_send()

    @pl.when(gives_tail)
    def _():
        kv_msg(me, 0, TAIL_OUTER, kv_mate.at[0], mate, len(tail_pieces)).wait_send()

    @pl.when(at_end)
    def _():
        @pl.loop(0, tiles)
        def _(t):
            @pl.when(t == 0)
            def _():
                half_msg(0).wait_recv()
                half_msg(1).wait_recv()

            @pl.when(t > 0)
            def _():
                part_msg(t).wait_recv()

            finish(t, part_in[t].astype(jnp.float32))

        kv_msg(me, 0, OWN_INNER, kv_mate.at[0], mate, PIECES).wait_send()
        sel_msg().wait_send()
        remote(q_vm, q_far, q_send, q_recv.at[0], inner).wait_send()

    @pl.when(takes_tail)
    def _():
        kv_msg(me, 0, FAR_MATE, kv_mate.at[0], mate, len(tail_pieces)).wait_send()

    @pl.when(has_next)
    def _():
        edge_msg().wait_send()

    @pl.when(up)
    def _():
        new_sent(0)

    @pl.when(up & (z > 0))
    def _():
        new_sent(1)

    new_sent(2)
    for d in range(1, hops + 1):

        @pl.when(z >= d)
        def _():
            new_sent(2 + d)

    for part in range(2):
        w_all_but_own(part, part).wait_send()
        w_all_but_own(part, 2 + part).wait_send()
    comp_some(chips, 0).wait_send()

    @pl.when(middle)
    def _():
        comp_some(chips + 1, 1).wait_send()

    @pl.when(at_end)
    def _():
        comp_some(1, 1).wait_send()

    pltpu.make_async_copy(out_vm, out, out_sem).wait()


def shards_gathered(q, ck, cv, ik, iv, wk, wv, sel, gw):
    n_seq, n_kv = lax.axis_size("seq"), lax.axis_size("kv")
    heads, width, branches = gw.shape
    vw = cv.shape[1]
    cache, fresh = ck.shape[0], ik.shape[0]
    tiles, picks = sel.shape[0], sel.shape[-1]
    chunks = cache // CMP_STRIDE
    pad = chunks + CMP_STRIDE
    per, new_per = cache // SEL_BLOCK, fresh // SEL_BLOCK
    tile_rows = heads * fresh
    count = tile_rows // tiles
    wide = -(-width // 128) * 128
    block_rows = 2 * SEL_BLOCK + SEL_BLOCK // 2
    bf = jnp.bfloat16
    any_spec = pl.BlockSpec(memory_space=pl.ANY)
    half_k, half_v = wk.shape[0] // CORES, wv.shape[0] // CORES

    def held(*shape):
        return pltpu.VMEM(shape, bf)

    dma = pltpu.SemaphoreType.DMA
    picked = sel.reshape(tiles, picks)
    return pl.pallas_call(
        functools.partial(fused_kernel, n_seq, n_kv, tiles),
        out_shape=jax.ShapeDtypeStruct((fresh, heads * vw), bf),
        in_specs=[
            pl.BlockSpec(memory_space=pltpu.SMEM),
            pl.BlockSpec(memory_space=pltpu.VMEM),
        ]
        + [any_spec] * 8,
        out_specs=any_spec,
        scratch_shapes=[
            held(*q.shape),
            held(*q.shape),
            pltpu.VMEM((tiles, picks), jnp.int32),
            pltpu.SMEM((tiles, picks), jnp.int32),
            held(width, cache),
            held(width, fresh),
            held(heads * branches, width),
            held(n_seq * per, block_rows, vw),
            held(n_seq * new_per, block_rows, vw),
            held(CMP_STRIDE, wide + vw),
            held(CMP_STRIDE, wide + vw),
            held(pad, CMP_STRIDE * width),
            held(pad, CMP_STRIDE * vw),
            held(n_kv, CORES, width, half_k),
            held(n_kv, CORES, half_v, vw),
            held(2 * chunks + chunks // 2, vw),
            held(n_seq, 2 * chunks + chunks // 2, vw),
            held(n_seq * chunks, wide),
            held(n_seq * chunks, 2 * vw),
            held(tile_rows, wide),
            held(tile_rows, wide),
            pltpu.VMEM((tile_rows, heads * branches), jnp.float32),
            pltpu.VMEM((tile_rows, vw), jnp.float32),
            held(tiles, count, vw),
            held(tiles, count, vw),
            held(fresh, heads * vw),
            held(fresh + WINDOW, wide),
            held(fresh + WINDOW, 2 * vw),
            held(2, picks * SEL_BLOCK, wide),
            held(2, picks * SEL_BLOCK, 2 * vw),
            dma((6 + 2 * CORES,)),
            dma,
            dma,
            dma,
            dma((7,)),
            dma((3, PIECES)),
            dma((5,)),
            dma((3 + -(-WINDOW // (fresh * CORES)),)),
            dma((3 + -(-WINDOW // (fresh * CORES)),)),
            dma,
            dma((tiles,)),
            dma((2,)),
            dma((2,)),
            dma,
            dma((tiles + 1,)),
            dma((4,)),
            dma((3, 2)),
            dma((2,)),
            dma((2,)),
            dma((4,)),
        ],
        compiler_params=pltpu.CompilerParams(
            collective_id=0, has_side_effects=True, vmem_limit_bytes=60 << 20
        ),
    )(
        picked,
        picked,
        q,
        ck.T,
        cv.reshape(per, SEL_BLOCK, vw),
        ik.T,
        iv.reshape(new_per, SEL_BLOCK, vw),
        wk.T,
        wv,
        jnp.transpose(gw, (2, 0, 1)).reshape(heads * branches, width),
    )


GATHER_BYTES = 1 << 24


def shards(queries, cache_keys, cache_values, *rest):
    ranks = lax.axis_size("seq")
    size = ranks * 2 * (cache_keys.size + cache_values.size)
    fits = size <= GATHER_BYTES and ranks == CORES * CHIPS and lax.axis_size("kv") == GROUPS
    form = shards_gathered if fits else shards_by_request
    return form(queries, cache_keys, cache_values, *rest)


def solution(mesh):
    placed = (
        P("seq", "kv"),
        P("seq", "kv"),
        P("seq", "kv"),
        P("seq", "kv"),
        P("seq", "kv"),
        P("kv", None),
        P("kv", None),
        P("seq", "kv", None),
        P("kv", None, None),
    )
    return jax.shard_map(
        shards, mesh=mesh, in_specs=placed, out_specs=P("seq", "kv"), check_vma=False
    )
```
